128 devices in a mesh: blk: 16 (over y, x_lo, core), lag: 8 (over z, x_hi).
Axes of the slice: x: 4 (x_hi: 2, x_lo: 2; x = x_hi * 2 + x_lo), y: 4, z: 4, core: 2. Of those that a mesh axis runs over, the one named last changes fastest.
Arguments:
- raw: float32 [8192, 4096], P(('blk', 'lag')), may hold values from -60 to 60
- mask: int32 [16, 16], replicated, may hold values from 0 to 1, as said below
Outputs:
- stack: float32 [8, 8192], P(None, ('blk', 'lag'))
The draws below stay inside these ranges and needn't reach their ends.
Inputs may be any that keep to these rules, and one draw needn't show every extreme that they name: mask is 0 or 1 and symmetric; it is 0 wherever |I - J| exceeds a limit between 8 and 14.
All inputs are finite; a program needn't handle non-finite values.
Results may differ from the reference program's by a relative error of at most 0.008.
Values may be sent and summed in bfloat16 or wider, within the bound.
No kernel may reach another device: no remote copies, remote signals or barrier semaphores. Data moves between devices by JAX's collectives and lax.ppermute only.
A program may use at most 192 MiB of HBM per device.

```python
import math
import jax
import jax.numpy as jnp
from jax import lax

NT = 8192
C = 4096
NB = 2048
K0 = 16
SW = 32
TAPER = 128
LAGS = 8
LAG_STEP = 32
BLOCKS = 16
BLOCK_CH = 256
OFFSETS = 8192


def draw_raw(key, part):
    noise_key, scale_key = jax.random.split(jax.random.fold_in(key, 11), 2)
    scales = jnp.exp(jax.random.uniform(scale_key, (1, C), minval=0.0, maxval=math.log(10.0)))
    noise = jax.random.truncated_normal(noise_key, -6.0, 6.0, (NT, C))
    return (scales * noise).astype(jnp.float32)


def draw_mask(key, part):
    alive_key, limit_key, keep_key = jax.random.split(jax.random.fold_in(key, 7), 3)
    labels = jnp.arange(BLOCKS, dtype=jnp.int32)
    keeper = jax.random.randint(keep_key, (), 0, BLOCKS)
    alive = (jax.random.randint(alive_key, (BLOCKS,), 0, 8) > 0) | (labels == keeper)
    limit = jax.random.randint(limit_key, (), BLOCKS // 2, BLOCKS - 1)
    near = jnp.abs(labels[:, None] - labels[None, :]) <= limit
    return (alive[:, None] & alive[None, :] & near).astype(jnp.int32)


def setup_inputs(seed: int = 0) -> dict:
    key_list = jax.random.split(jax.random.key(seed), 3)
    return {
        "raw": draw_raw(jax.random.fold_in(key_list[2], 71), 0),
        "mask": draw_mask(jax.random.fold_in(key_list[2], 71), 0),
    }


EPS = 1e-06

def taper_weights(first_bin, count):
    position = (first_bin + lax.iota(jnp.int32, count)).astype(jnp.float32)
    edge = jnp.minimum(position, NB - 1 - position)
    curve = 0.5 - 0.5 * jnp.cos(math.pi * (edge + 0.5) / TAPER)
    return jnp.where(edge < TAPER, curve, jnp.ones_like(curve))

def lag_phases(bins):
    number = lax.iota(jnp.int32, LAGS)
    shifts = LAG_STEP * (2 * number + 1 - LAGS) // 2
    return jnp.mod(shifts[:, None] * bins[None, :], NT).astype(jnp.float32) * (2 * math.pi / NT)

def moving_mean(padded):
    window = lax.reduce_window(padded, jnp.zeros((), padded.dtype), lax.add, (1, 2 * SW + 1), (1, 1), 'VALID')
    return window / (2 * SW + 1)

def rotate(own_real, own_imag, cosines, sines):
    real_part = own_real.astype(jnp.float32)[None]
    imag_part = own_imag.astype(jnp.float32)[None]
    rot_real = real_part * cosines[:, None, :] - imag_part * sines[:, None, :]
    rot_imag = real_part * sines[:, None, :] + imag_part * cosines[:, None, :]
    joined = jnp.concatenate([rot_real, rot_imag], axis=2).astype(jnp.bfloat16)
    return joined.reshape(joined.shape[0] * joined.shape[1], joined.shape[2])

def diagonal_sums(product, rows):
    count = product.shape[2]
    padded = jnp.pad(product, ((0, 0), (0, 0), (0, rows)))
    width = count + rows - 1
    flat = padded.reshape(product.shape[0], rows * (count + rows))[:, :rows * width]
    return lax.optimization_barrier(jnp.sum(flat.reshape(product.shape[0], rows, width), axis=1))

def place(total, values, first_col):
    anchor = jnp.zeros((), jnp.int32)
    current = lax.dynamic_slice(total, (anchor, first_col), values.shape)
    return lax.dynamic_update_slice(total, current + values, (anchor, first_col))

def pair_counts(mask, columns):
    blocks = mask.shape[0]
    width = C // blocks
    labels = lax.iota(jnp.int32, blocks)
    apart = labels[None, :] - labels[:, None]
    deltas = lax.iota(jnp.int32, 2 * blocks - 1) - (blocks - 1)
    per_delta = lax.optimization_barrier(jnp.sum(mask[None] * (apart[None] == deltas[:, None, None]).astype(jnp.int32), axis=(1, 2)))
    offsets = columns - C
    intersection = jnp.maximum(0, width - jnp.abs(offsets[:, None] - width * deltas[None, :]))
    return lax.optimization_barrier(jnp.sum(intersection * per_delta[None, :], axis=1))

def stack_scale(counts):
    return 1.0 / jnp.sqrt(NB * jnp.maximum(counts, 1).astype(jnp.float32))

def reference(raw, mask):
    spectrum = jnp.fft.rfft(raw, axis=0)[K0:K0 + NB]
    real_spec = jnp.real(spectrum).astype(jnp.float32).T
    imag_spec = jnp.imag(spectrum).astype(jnp.float32).T
    amplitude = jnp.sqrt(real_spec * real_spec + imag_spec * imag_spec)
    smooth = moving_mean(jnp.pad(amplitude, ((0, 0), (SW, SW))))
    weights = taper_weights(0, NB)
    real_white = (real_spec * weights[None, :] / (smooth + EPS)).astype(jnp.bfloat16)
    imag_white = (imag_spec * weights[None, :] / (smooth + EPS)).astype(jnp.bfloat16)
    phases = lag_phases(K0 + lax.iota(jnp.int32, NB))
    cosines = jnp.cos(phases)
    sines = jnp.sin(phases)
    spectra = jnp.concatenate([real_white, imag_white], axis=1)

    def one_block(total, index):
        row_mask = lax.dynamic_index_in_dim(mask, index, 0, keepdims=False)
        live = jnp.repeat(row_mask, BLOCK_CH).astype(jnp.bfloat16)
        masked = spectra * live[:, None]
        own_real = lax.dynamic_slice_in_dim(real_white, index * BLOCK_CH, BLOCK_CH, 0)[::-1]
        own_imag = lax.dynamic_slice_in_dim(imag_white, index * BLOCK_CH, BLOCK_CH, 0)[::-1]
        rotated = rotate(own_real, own_imag, cosines, sines)
        product = jnp.dot(rotated.astype(jnp.float32), masked.astype(jnp.float32).T, precision=lax.Precision.HIGHEST)
        diagonal = diagonal_sums(product.reshape(LAGS, BLOCK_CH, C), BLOCK_CH)
        first_col = C - BLOCK_CH + 1 - index * BLOCK_CH
        return (place(total, diagonal, first_col), None)
    total, _ = lax.scan(one_block, jnp.zeros((LAGS, OFFSETS), jnp.float32), lax.iota(jnp.int32, BLOCKS))
    counts = pair_counts(mask, lax.iota(jnp.int32, OFFSETS))
    return total * stack_scale(counts)[None, :]
```

```python
import math

import jax
import jax.numpy as jnp
import numpy as np
from jax import lax
from jax.experimental import pallas as pl
from jax.experimental.pallas import tpu as pltpu
from jax.sharding import PartitionSpec as P

NT = 8192
C = 4096
NB = 2048
K0 = 16
SW = 32
TAPER = 128
LAGS = 8
LAG_STEP = 32
EPS = 1e-06

DEV = 128
ROWS = NT // DEV
BLK = 16
J2 = NB // DEV
Q = 512
FAR = 15

BF = jnp.bfloat16
F32 = jnp.float32


def split(x):
    hi = x.astype(BF)
    return hi, (x - hi.astype(F32)).astype(BF)


def np_split(x):
    hi = np.asarray(x, np.float32).astype(jnp.bfloat16)
    lo = (np.asarray(x, np.float64) - hi.astype(np.float64)).astype(jnp.bfloat16)
    return hi, lo


def cs(numer, period):
    angle = 2 * np.pi * np.mod(numer, period) / period
    return np.cos(angle), np.sin(angle)


def time_tables():
    j1, p = np.arange(DEV), np.arange(DEV)
    c, s = cs((K0 + j1)[:, None] * p[None], DEV)
    stage1 = np.concatenate([c, -s], axis=0).astype(jnp.bfloat16)
    r = np.tile(np.arange(ROWS), 2)
    c, s = cs((K0 + j1)[:, None] * r[None], NT)
    twiddle = np.stack([c, s]).astype(np.float32)
    r, j2 = np.arange(ROWS), np.arange(J2)
    c, s = cs(r[:, None] * j2[None], ROWS)
    eye = np.eye(8)
    place = lambda t: np.einsum("ab,rj->arbj", eye, t).reshape(8 * ROWS, 8 * J2)
    stage2 = np.block([[place(c), place(-s)], [place(s), place(c)]])
    return stage1, twiddle, stage2.astype(jnp.bfloat16)


def window_table():
    i, j = np.arange(DEV)[:, None], np.arange(DEV)[None]
    near = lambda d: (np.abs(d) <= SW).astype(np.float32)
    return np.concatenate([near(i - j), near(i - j - DEV), near(i - j + DEV)], axis=1).astype(
        jnp.bfloat16
    )


def taper_table():
    position = np.arange(DEV)[:, None] + DEV * np.arange(J2)[None]
    edge = np.minimum(position, NB - 1 - position)
    curve = 0.5 - 0.5 * np.cos(math.pi * (edge + 0.5) / TAPER)
    return np.tile(np.where(edge < TAPER, curve, 1.0), (1, DEV // J2)).astype(np.float32)


def channel_table():
    c, s = cs(np.arange(256)[:, None] * np.arange(Q)[None], Q)
    return np_split(np.block([[c, -s], [s, c]]))


def offset_table():
    m = np.concatenate([np.arange(256), 256 - np.arange(256)])
    c, s = cs(np.arange(Q)[:, None] * m[None], Q)
    return np_split(np.concatenate([c, s], axis=0) / Q)


def sign_table():
    table = np.zeros((32, 256), np.float32)
    for delta in range(BLK):
        for j2 in range(J2):
            table[(j2 % 2) * 16 + delta, delta * J2 + j2] = 1.0 if j2 % 4 < 2 else -1.0
    return table.astype(jnp.bfloat16)


def pack_kernel(raw_ref, out_ref, buf_ref):
    for i in range(BLK):
        x = raw_ref[:, i * 256 : (i + 1) * 256]
        rows = jnp.concatenate([x[:, :DEV], x[:, DEV:]], axis=0)
        buf_ref[pl.ds(i, DEV, stride=BLK), :] = rows.T
    out_ref[...] = buf_ref[...].astype(BF)


def dot(a, b):
    return jnp.dot(a, b, preferred_element_type=F32)


def spectra_kernel(in_ref, s1_ref, tw_ref, s2_ref, win_ref, taper_ref, out_ref, buf_ref, wide_ref):
    buf_ref[...] = in_ref[...].astype(F32)
    stage1, stage2 = s1_ref[...], s2_ref[...]
    cos, sin = tw_ref[0], tw_ref[1]
    lane = lax.broadcasted_iota(jnp.int32, (DEV, DEV), 1) % J2
    for g in range(4):
        samples = jnp.concatenate(
            [buf_ref[pl.ds(4 * g + s, DEV, stride=BLK), :] for s in range(4)], axis=1
        ).astype(BF)
        y = dot(stage1, samples)
        reals, imags = [], []
        for s in range(4):
            y_re, y_im = y[:DEV, s * DEV : (s + 1) * DEV], y[DEV:, s * DEV : (s + 1) * DEV]
            reals.append((y_re * cos + y_im * sin).astype(BF))
            imags.append((y_im * cos - y_re * sin).astype(BF))
        spec = dot(jnp.concatenate(reals + imags, axis=1), stage2)
        re, im = spec[:, :DEV], spec[:, DEV:]
        wide_ref[g] = re
        wide_ref[4 + g] = im
    for g in range(4):
        re, im = wide_ref[g], wide_ref[4 + g]
        amp = jnp.sqrt(re * re + im * im)
        after = jnp.where(lane == J2 - 1, 0.0, pltpu.roll(amp, DEV - 1, 1))
        before = jnp.where(lane == 0, 0.0, pltpu.roll(amp, 1, 1))
        total = dot(win_ref[...], jnp.concatenate([amp, after, before], axis=0).astype(BF))
        gain = taper_ref[...] / (total * (1.0 / (2 * SW + 1)) + EPS)
        buf_ref[pl.ds(g, DEV, stride=8), :] = re * gain
        buf_ref[pl.ds(4 + g, DEV, stride=8), :] = im * gain
    out_ref[...] = buf_ref[: 8 * DEV, :].astype(BF)


def stack_kernel(
    in_ref, mask_ref, rot_ref, eh_ref, el_ref, sign_ref, dh_ref, dl_ref, out_ref,
    buf_ref, f_ref, acc_ref, v_ref,
):
    buf_ref[...] = in_ref[...].astype(F32)
    pieces = [buf_ref[pl.ds(t, DEV, stride=8), :].T.astype(BF) for t in range(8)]
    rows = []
    for i in range(BLK):
        g, s = i // 4, i % 4
        tiles = [
            pieces[4 * part + g][(2 * s + h) * J2 : (2 * s + h + 1) * J2]
            for part in range(2)
            for h in range(2)
        ]
        rows.append(jnp.concatenate(tiles, axis=1))
    white = jnp.concatenate(rows, axis=0)
    f_ref[...] = dot(white, eh_ref[...]) + dot(white, el_ref[...])
    acc_ref[FAR * J2 :, :] = jnp.zeros((J2, 2 * Q), F32)

    def unit(u, carry):
        half = pl.multiple_of((u // 4) * 8, 8)
        col = pl.multiple_of((u % 4) * DEV, DEV)
        at = lambda i: pl.ds(i * J2 + half, 8)
        res, ims = pl.ds(col, DEV), pl.ds(col + Q, DEV)
        f_re = [f_ref[at(i), res] for i in range(BLK)]
        f_im = [f_ref[at(i), ims] for i in range(BLK)]
        for delta in range(FAR):
            sum_re = sum_im = jnp.zeros((8, DEV), F32)
            for i in range(BLK - delta):
                j, live = i + delta, mask_ref[i, i + delta]
                a_re, a_im = f_re[i] * live, f_im[i] * live
                sum_re = sum_re + (a_re * f_re[j] + a_im * f_im[j])
                sum_im = sum_im + (a_im * f_re[j] - a_re * f_im[j])
            acc_ref[at(delta), res] = sum_re
            acc_ref[at(delta), ims] = sum_im
        return carry

    lax.fori_loop(0, 8, unit, 0)
    hi, lo = split(acc_ref[...])
    sums = dot(sign_ref[...], hi) + dot(sign_ref[...], lo)
    far = lax.broadcasted_iota(jnp.int32, sums.shape, 0) % BLK == BLK - 1
    odd = lax.broadcasted_iota(jnp.int32, sums.shape, 1) % 2 == 1
    nearer = jnp.where(far, 0.0, pltpu.roll(sums, 2 * BLK - 1, 0))
    sums = sums + jnp.where(odd, -nearer, nearer)
    a_re, a_im, b_re, b_im = sums[:16, :Q], sums[:16, Q:], sums[16:, :Q], sums[16:, Q:]
    quarter = ((a_re - b_im, a_im + b_re), (a_re + b_im, a_im - b_re))
    for j in range(LAGS):
        g_re, g_im = quarter[0 if (2 * j - 7) % 4 == 1 else 1]
        c, s = rot_ref[0, j], rot_ref[1, j]
        v_re, v_im = c * g_re - s * g_im, c * g_im + s * g_re
        for t in range(4):
            v_ref[pl.ds(t * DEV + j, BLK, stride=LAGS), :] = v_re[:, t * DEV : (t + 1) * DEV]
            v_ref[pl.ds((4 + t) * DEV + j, BLK, stride=LAGS), :] = v_im[:, t * DEV : (t + 1) * DEV]
    v_hi, v_lo = split(jnp.concatenate([v_ref[t * DEV : (t + 1) * DEV] for t in range(8)], axis=1))
    stacked = dot(v_hi, dh_ref[...]) + dot(v_hi, dl_ref[...]) + dot(v_lo, dh_ref[...])
    for delta in range(BLK):
        for w in range(4):
            ahead = stacked[8 * delta : 8 * delta + 8, (w // 2) * DEV : (w // 2 + 1) * DEV]
            behind = stacked[8 * delta : 8 * delta + 8, 256 + (w // 2) * DEV : 256 + (w // 2 + 1) * DEV]
            to = 64 + 4 * delta + w
            out_ref[8 * to : 8 * to + 8, :] = ahead.astype(out_ref.dtype)
            to = 4 * (BLK - 1 - delta) + w
            out_ref[8 * to : 8 * to + 8, :] = behind.astype(out_ref.dtype)


def total_kernel(in_ref, place_ref, scale_ref, out_ref):
    total = jnp.sum(in_ref[...].astype(F32), axis=0)
    rolled = jnp.where(place_ref[1] == 1, pltpu.roll(total, 64, 1), total)
    flipped = jnp.concatenate([rolled[7 - j : 8 - j] for j in range(LAGS)], axis=0)
    out = jnp.where(place_ref[0] == 1, flipped, rolled)
    out_ref[...] = out[:, :64] * scale_ref[...]


def pair_counts(mask, columns):
    blocks = mask.shape[0]
    width = C // blocks
    labels = lax.iota(jnp.int32, blocks)
    apart = labels[None, :] - labels[:, None]
    deltas = lax.iota(jnp.int32, 2 * blocks - 1) - (blocks - 1)
    per_delta = jnp.sum(
        mask[None] * (apart[None] == deltas[:, None, None]).astype(jnp.int32), axis=(1, 2)
    )
    offsets = columns - C
    intersection = jnp.maximum(0, width - jnp.abs(offsets[:, None] - width * deltas[None, :]))
    return jnp.sum(intersection * per_delta[None, :], axis=1)


def stack_scale(counts):
    return 1.0 / jnp.sqrt(NB * jnp.maximum(counts, 1).astype(jnp.float32))


VM = pl.BlockSpec(memory_space=pltpu.VMEM)
SM = pl.BlockSpec(memory_space=pltpu.SMEM)


def exchange(x, rows):
    x = x.reshape(DEV, rows, DEV)
    return lax.all_to_all(x, ("blk", "lag"), split_axis=0, concat_axis=0, tiled=True)


def on_device(raw, mask):
    device = lax.axis_index("blk") * lax.axis_size("lag") + lax.axis_index("lag")
    packed = pl.pallas_call(
        pack_kernel,
        out_shape=jax.ShapeDtypeStruct((BLK * DEV, DEV), BF),
        in_specs=[VM],
        out_specs=VM,
        scratch_shapes=[pltpu.VMEM((BLK * DEV, DEV), F32)],
    )(raw)
    series = exchange(packed, BLK).reshape(BLK * DEV, DEV)
    stage1, twiddle, stage2 = time_tables()
    white = pl.pallas_call(
        spectra_kernel,
        out_shape=jax.ShapeDtypeStruct((8 * DEV, DEV), BF),
        in_specs=[VM] * 6,
        out_specs=VM,
        scratch_shapes=[pltpu.VMEM((BLK * DEV, DEV), F32), pltpu.VMEM((8, DEV, DEV), F32)],
    )(series, stage1, twiddle, stage2, window_table(), taper_table())
    banded = exchange(white, 8).reshape(8 * DEV, DEV)
    odd = 2 * lax.iota(jnp.int32, LAGS) - (LAGS - 1)
    angle = jnp.mod(odd * (K0 + device), Q).astype(F32) * (2 * math.pi / Q)
    rotation = jnp.stack([jnp.cos(angle), jnp.sin(angle)])
    parts = pl.pallas_call(
        stack_kernel,
        out_shape=jax.ShapeDtypeStruct((8 * DEV, DEV), BF),
        in_specs=[VM, SM, SM] + [VM] * 5,
        out_specs=VM,
        scratch_shapes=[
            pltpu.VMEM((8 * DEV, DEV), F32),
            pltpu.VMEM((BLK * J2, 2 * Q), F32),
            pltpu.VMEM((BLK * J2, 2 * Q), F32),
            pltpu.VMEM((8 * DEV, DEV), F32),
        ],
    )(banded, mask.astype(F32), rotation, *channel_table(), sign_table(), *offset_table())
    shares = exchange(parts, 8)
    columns = device * 64 + lax.iota(jnp.int32, 64)
    scale = stack_scale(pair_counts(mask, columns))[None, :]
    place = jnp.stack([(device < 64).astype(jnp.int32), device % 2])
    return pl.pallas_call(
        total_kernel,
        out_shape=jax.ShapeDtypeStruct((LAGS, 64), F32),
        in_specs=[VM, SM, VM],
        out_specs=VM,
    )(shares, place, scale)


def solution(mesh):
    return jax.shard_map(
        on_device,
        mesh=mesh,
        in_specs=(P(("blk", "lag"), None), P()),
        out_specs=P(None, ("blk", "lag")),
        check_vma=False,
    )
```

```python
import math

import jax
import jax.numpy as jnp
import numpy as np
from jax import lax
from jax.experimental import pallas as pl
from jax.experimental.pallas import tpu as pltpu
from jax.sharding import PartitionSpec as P

NT = 8192
C = 4096
NB = 2048
K0 = 16
SW = 32
TAPER = 128
LAGS = 8
LAG_STEP = 32
EPS = 1e-06

DEV = 128
ROWS = NT // DEV
BLK = 16
J2 = NB // DEV
Q = 512
FAR = 15

BF = jnp.bfloat16
F32 = jnp.float32


def split(x):
    hi = x.astype(BF)
    return hi, (x - hi.astype(F32)).astype(BF)


def np_split(x):
    hi = np.asarray(x, np.float32).astype(jnp.bfloat16)
    lo = (np.asarray(x, np.float64) - hi.astype(np.float64)).astype(jnp.bfloat16)
    return hi, lo


def cs(numer, period):
    angle = 2 * np.pi * np.mod(numer, period) / period
    return np.cos(angle), np.sin(angle)


def time_tables():
    j1, p = np.arange(DEV), np.arange(DEV)
    c, s = cs((K0 + j1)[:, None] * p[None], DEV)
    stage1 = np.concatenate([c, -s], axis=0).astype(jnp.bfloat16)
    r = np.tile(np.arange(ROWS), 2)
    c, s = cs((K0 + j1)[:, None] * r[None], NT)
    twiddle = np.stack([c, s]).astype(np.float32)
    r, j2 = np.arange(ROWS), np.arange(J2)
    c, s = cs(r[:, None] * j2[None], ROWS)
    eye = np.eye(8)
    place = lambda t: np.einsum("ab,rj->arbj", eye, t).reshape(8 * ROWS, 8 * J2)
    stage2 = np.block([[place(c), place(-s)], [place(s), place(c)]])
    return stage1, twiddle, stage2.astype(jnp.bfloat16)


def window_table():
    i, j = np.arange(DEV)[:, None], np.arange(DEV)[None]
    near = lambda d: (np.abs(d) <= SW).astype(np.float32)
    return np.concatenate([near(i - j), near(i - j - DEV), near(i - j + DEV)], axis=1).astype(
        jnp.bfloat16
    )


def taper_table():
    position = np.arange(DEV)[:, None] + DEV * np.arange(J2)[None]
    edge = np.minimum(position, NB - 1 - position)
    curve = 0.5 - 0.5 * np.cos(math.pi * (edge + 0.5) / TAPER)
    return np.tile(np.where(edge < TAPER, curve, 1.0), (1, DEV // J2)).astype(np.float32)


def channel_table():
    c, s = cs(np.arange(256)[:, None] * np.arange(Q)[None], Q)
    return np_split(np.block([[c, -s], [s, c]]))


def offset_table():
    m = np.concatenate([np.arange(256), 256 - np.arange(256)])
    c, s = cs(np.arange(Q)[:, None] * m[None], Q)
    return np_split(np.concatenate([c, s], axis=0) / Q)


def sign_table():
    table = np.zeros((32, 256), np.float32)
    for delta in range(BLK):
        for j2 in range(J2):
            table[(j2 % 2) * 16 + delta, delta * J2 + j2] = 1.0 if j2 % 4 < 2 else -1.0
    return table.astype(jnp.bfloat16)


def pack_kernel(raw_ref, out_ref, raw_buf, buf_ref, sems):
    wide = C // 4
    copies = [
        pltpu.make_async_copy(
            raw_ref.at[:, pl.ds(k * wide, wide)], raw_buf.at[:, pl.ds(k * wide, wide)], sems.at[k]
        )
        for k in range(4)
    ]
    for copy in copies:
        copy.start()
    for i in range(BLK):
        if i % 4 == 0:
            copies[i // 4].wait()
        x = raw_buf[:, i * 256 : (i + 1) * 256]
        rows = jnp.concatenate([x[:, :DEV], x[:, DEV:]], axis=0)
        buf_ref[pl.ds(i, DEV, stride=BLK), :] = rows.T
    out_ref[...] = buf_ref[...].astype(BF)


def dot(a, b):
    return jnp.dot(a, b, preferred_element_type=F32)


def spectra_kernel(in_ref, s1_ref, tw_ref, s2_ref, win_ref, taper_ref, out_ref, buf_ref, wide_ref):
    buf_ref[...] = in_ref[...].astype(F32)
    stage1, stage2 = s1_ref[...], s2_ref[...]
    cos, sin = tw_ref[0], tw_ref[1]
    lane = lax.broadcasted_iota(jnp.int32, (DEV, DEV), 1) % J2
    for g in range(4):
        samples = jnp.concatenate(
            [buf_ref[pl.ds(4 * g + s, DEV, stride=BLK), :] for s in range(4)], axis=1
        ).astype(BF)
        y = dot(stage1, samples)
        reals, imags = [], []
        for s in range(4):
            y_re, y_im = y[:DEV, s * DEV : (s + 1) * DEV], y[DEV:, s * DEV : (s + 1) * DEV]
            reals.append((y_re * cos + y_im * sin).astype(BF))
            imags.append((y_im * cos - y_re * sin).astype(BF))
        spec = dot(jnp.concatenate(reals + imags, axis=1), stage2)
        re, im = spec[:, :DEV], spec[:, DEV:]
        wide_ref[g] = re
        wide_ref[4 + g] = im
    for g in range(4):
        re, im = wide_ref[g], wide_ref[4 + g]
        amp = jnp.sqrt(re * re + im * im)
        after = jnp.where(lane == J2 - 1, 0.0, pltpu.roll(amp, DEV - 1, 1))
        before = jnp.where(lane == 0, 0.0, pltpu.roll(amp, 1, 1))
        total = dot(win_ref[...], jnp.concatenate([amp, after, before], axis=0).astype(BF))
        gain = taper_ref[...] / (total * (1.0 / (2 * SW + 1)) + EPS)
        buf_ref[pl.ds(g, DEV, stride=8), :] = re * gain
        buf_ref[pl.ds(4 + g, DEV, stride=8), :] = im * gain
    out_ref[...] = buf_ref[: 8 * DEV, :].astype(BF)


def stack_kernel(
    in_ref, mask_ref, rot_ref, eh_ref, el_ref, sign_ref, dh_far, dl_far, out_ref,
    buf_ref, f_ref, acc_ref, v_ref, dh_ref, dl_ref, sems,
):
    tables = (
        pltpu.make_async_copy(dh_far, dh_ref, sems.at[0]),
        pltpu.make_async_copy(dl_far, dl_ref, sems.at[1]),
    )
    for table in tables:
        table.start()
    buf_ref[...] = in_ref[...].astype(F32)
    pieces = [buf_ref[pl.ds(t, DEV, stride=8), :].T.astype(BF) for t in range(8)]
    rows = []
    for i in range(BLK):
        g, s = i // 4, i % 4
        tiles = [
            pieces[4 * part + g][(2 * s + h) * J2 : (2 * s + h + 1) * J2]
            for part in range(2)
            for h in range(2)
        ]
        rows.append(jnp.concatenate(tiles, axis=1))
    white = jnp.concatenate(rows, axis=0)
    f_ref[...] = dot(white, eh_ref[...]) + dot(white, el_ref[...])
    acc_ref[FAR * J2 :, :] = jnp.zeros((J2, 2 * Q), F32)

    def unit(u, carry):
        half = pl.multiple_of((u // 4) * 8, 8)
        col = pl.multiple_of((u % 4) * DEV, DEV)
        at = lambda i: pl.ds(i * J2 + half, 8)
        res, ims = pl.ds(col, DEV), pl.ds(col + Q, DEV)
        f_re = [f_ref[at(i), res] for i in range(BLK)]
        f_im = [f_ref[at(i), ims] for i in range(BLK)]
        for delta in range(FAR):
            sum_re = sum_im = jnp.zeros((8, DEV), F32)
            for i in range(BLK - delta):
                j, live = i + delta, mask_ref[i, i + delta]
                a_re, a_im = f_re[i] * live, f_im[i] * live
                sum_re = sum_re + (a_re * f_re[j] + a_im * f_im[j])
                sum_im = sum_im + (a_im * f_re[j] - a_re * f_im[j])
            acc_ref[at(delta), res] = sum_re
            acc_ref[at(delta), ims] = sum_im
        return carry

    lax.fori_loop(0, 8, unit, 0)
    hi, lo = split(acc_ref[...])
    sums = dot(sign_ref[...], hi) + dot(sign_ref[...], lo)
    far = lax.broadcasted_iota(jnp.int32, sums.shape, 0) % BLK == BLK - 1
    odd = lax.broadcasted_iota(jnp.int32, sums.shape, 1) % 2 == 1
    nearer = jnp.where(far, 0.0, pltpu.roll(sums, 2 * BLK - 1, 0))
    sums = sums + jnp.where(odd, -nearer, nearer)
    a_re, a_im, b_re, b_im = sums[:16, :Q], sums[:16, Q:], sums[16:, :Q], sums[16:, Q:]
    quarter = ((a_re - b_im, a_im + b_re), (a_re + b_im, a_im - b_re))
    for j in range(LAGS):
        g_re, g_im = quarter[0 if (2 * j - 7) % 4 == 1 else 1]
        c, s = rot_ref[0, j], rot_ref[1, j]
        v_re, v_im = c * g_re - s * g_im, c * g_im + s * g_re
        for t in range(4):
            v_ref[pl.ds(t * DEV + j, BLK, stride=LAGS), :] = v_re[:, t * DEV : (t + 1) * DEV]
            v_ref[pl.ds((4 + t) * DEV + j, BLK, stride=LAGS), :] = v_im[:, t * DEV : (t + 1) * DEV]
    v_hi, v_lo = split(jnp.concatenate([v_ref[t * DEV : (t + 1) * DEV] for t in range(8)], axis=1))
    for table in tables:
        table.wait()
    stacked = dot(v_hi, dh_ref[...]) + dot(v_hi, dl_ref[...]) + dot(v_lo, dh_ref[...])
    row = lax.broadcasted_iota(jnp.int32, (8, DEV), 0) < 4
    low = lax.broadcasted_iota(jnp.int32, (8, DEV), 1) < 64
    for delta in range(BLK):
        for t in range(4):
            tile = stacked[8 * delta : 8 * delta + 8, t * DEV : (t + 1) * DEV]
            pair = jnp.where(row == low, tile, pltpu.roll(pltpu.roll(tile, 4, 0), 64, 1))
            to = 64 + 4 * delta if t < 2 else 4 * (BLK - 1 - delta)
            at = 4 * (to + 2 * (t % 2))
            out_ref[at : at + 8, :] = pair.astype(BF)


def total_kernel(in_ref, place_ref, scale_ref, out_ref):
    total = jnp.sum(in_ref[...].astype(F32).reshape(DEV // 2, 8, DEV), axis=0)
    total = total + pltpu.roll(total, 4, 0)
    low = lax.broadcasted_iota(jnp.int32, (8, DEV), 0) < 4
    lags = jnp.where(low, total, pltpu.roll(total, 64, 1))[:, :64]
    flipped = jnp.concatenate([lags[7 - j : 8 - j] for j in range(LAGS)], axis=0)
    out_ref[...] = jnp.where(place_ref[0] == 1, flipped, lags) * scale_ref[...]


def pair_counts(mask, columns):
    blocks = mask.shape[0]
    width = C // blocks
    labels = lax.iota(jnp.int32, blocks)
    apart = labels[None, :] - labels[:, None]
    deltas = lax.iota(jnp.int32, 2 * blocks - 1) - (blocks - 1)
    per_delta = jnp.sum(
        mask[None] * (apart[None] == deltas[:, None, None]).astype(jnp.int32), axis=(1, 2)
    )
    offsets = columns - C
    intersection = jnp.maximum(0, width - jnp.abs(offsets[:, None] - width * deltas[None, :]))
    return jnp.sum(intersection * per_delta[None, :], axis=1)


def stack_scale(counts):
    return 1.0 / jnp.sqrt(NB * jnp.maximum(counts, 1).astype(jnp.float32))


VM = pl.BlockSpec(memory_space=pltpu.VMEM)
SM = pl.BlockSpec(memory_space=pltpu.SMEM)
LIMIT = pltpu.CompilerParams(vmem_limit_bytes=24 * 1024 * 1024)


def exchange(x, rows):
    x = x.reshape(DEV, rows, DEV)
    return lax.all_to_all(x, ("blk", "lag"), split_axis=0, concat_axis=0, tiled=True)


def on_device(raw, mask):
    device = lax.axis_index("blk") * lax.axis_size("lag") + lax.axis_index("lag")
    packed = pl.pallas_call(
        pack_kernel,
        out_shape=jax.ShapeDtypeStruct((BLK * DEV, DEV), BF),
        in_specs=[pl.BlockSpec(memory_space=pltpu.HBM)],
        out_specs=VM,
        compiler_params=LIMIT,
        scratch_shapes=[
            pltpu.VMEM((ROWS, C), F32),
            pltpu.VMEM((BLK * DEV, DEV), F32),
            pltpu.SemaphoreType.DMA((4,)),
        ],
    )(raw)
    series = exchange(packed, BLK).reshape(BLK * DEV, DEV)
    stage1, twiddle, stage2 = time_tables()
    white = pl.pallas_call(
        spectra_kernel,
        out_shape=jax.ShapeDtypeStruct((8 * DEV, DEV), BF),
        in_specs=[VM] * 6,
        out_specs=VM,
        compiler_params=LIMIT,
        scratch_shapes=[pltpu.VMEM((BLK * DEV, DEV), F32), pltpu.VMEM((8, DEV, DEV), F32)],
    )(series, stage1, twiddle, stage2, window_table(), taper_table())
    banded = exchange(white, 8).reshape(8 * DEV, DEV)
    odd = 2 * lax.iota(jnp.int32, LAGS) - (LAGS - 1)
    angle = jnp.mod(odd * (K0 + device), Q).astype(F32) * (2 * math.pi / Q)
    rotation = jnp.stack([jnp.cos(angle), jnp.sin(angle)])
    parts = pl.pallas_call(
        stack_kernel,
        out_shape=jax.ShapeDtypeStruct((4 * DEV, DEV), BF),
        in_specs=[VM, SM, SM] + [VM] * 3 + [pl.BlockSpec(memory_space=pltpu.HBM)] * 2,
        out_specs=VM,
        compiler_params=LIMIT,
        scratch_shapes=[
            pltpu.VMEM((8 * DEV, DEV), F32),
            pltpu.VMEM((BLK * J2, 2 * Q), F32),
            pltpu.VMEM((BLK * J2, 2 * Q), F32),
            pltpu.VMEM((8 * DEV, DEV), F32),
            pltpu.VMEM((2 * Q, Q), BF),
            pltpu.VMEM((2 * Q, Q), BF),
            pltpu.SemaphoreType.DMA((2,)),
        ],
    )(banded, mask.astype(F32), rotation, *channel_table(), sign_table(), *offset_table())
    shares = exchange(parts, 4).reshape(4 * DEV, DEV)
    columns = device * 64 + lax.iota(jnp.int32, 64)
    scale = stack_scale(pair_counts(mask, columns))[None, :]
    place = (device < 64).astype(jnp.int32)[None]
    return pl.pallas_call(
        total_kernel,
        out_shape=jax.ShapeDtypeStruct((LAGS, 64), F32),
        in_specs=[VM, SM, VM],
        out_specs=VM,
        compiler_params=LIMIT,
    )(shares, place, scale)


def solution(mesh):
    return jax.shard_map(
        on_device,
        mesh=mesh,
        in_specs=(P(("blk", "lag"), None), P()),
        out_specs=P(None, ("blk", "lag")),
        check_vma=False,
    )
```

```python
import math

import jax
import jax.numpy as jnp
import numpy as np
from jax import lax
from jax.experimental import pallas as pl
from jax.experimental.pallas import tpu as pltpu
from jax.sharding import PartitionSpec as P

NT = 8192
C = 4096
NB = 2048
K0 = 16
SW = 32
TAPER = 128
LAGS = 8
LAG_STEP = 32
EPS = 1e-06

DEV = 128
ROWS = NT // DEV
BLK = 16
J2 = NB // DEV
Q = 512
FAR = 15

BF = jnp.bfloat16
F32 = jnp.float32


def split(x):
    hi = x.astype(BF)
    return hi, (x - hi.astype(F32)).astype(BF)


def np_split(x):
    hi = np.asarray(x, np.float32).astype(jnp.bfloat16)
    lo = (np.asarray(x, np.float64) - hi.astype(np.float64)).astype(jnp.bfloat16)
    return hi, lo


def cs(numer, period):
    angle = 2 * np.pi * np.mod(numer, period) / period
    return np.cos(angle), np.sin(angle)


def time_tables():
    j1, p = np.arange(DEV), np.arange(DEV)
    c, s = cs((K0 + j1)[:, None] * p[None], DEV)
    stage1 = np.concatenate([c, -s], axis=0).astype(jnp.bfloat16)
    r = np.tile(np.arange(ROWS), 2)
    c, s = cs((K0 + j1)[:, None] * r[None], NT)
    twiddle = np.stack([c, s]).astype(np.float32)
    r, j2 = np.arange(ROWS), np.arange(J2)
    c, s = cs(r[:, None] * j2[None], ROWS)
    eye = np.eye(8)
    place = lambda t: np.einsum("ab,rj->arbj", eye, t).reshape(8 * ROWS, 8 * J2)
    stage2 = np.block([[place(c), place(-s)], [place(s), place(c)]])
    return stage1, twiddle, stage2.astype(jnp.bfloat16)


def window_table():
    i, j = np.arange(DEV)[:, None], np.arange(DEV)[None]
    near = lambda d: (np.abs(d) <= SW).astype(np.float32)
    return np.concatenate([near(i - j), near(i - j - DEV), near(i - j + DEV)], axis=1).astype(
        jnp.bfloat16
    )


def taper_table():
    position = np.arange(DEV)[:, None] + DEV * np.arange(J2)[None]
    edge = np.minimum(position, NB - 1 - position)
    curve = 0.5 - 0.5 * np.cos(math.pi * (edge + 0.5) / TAPER)
    return np.tile(np.where(edge < TAPER, curve, 1.0), (1, DEV // J2)).astype(np.float32)


def channel_table():
    c, s = cs(np.arange(256)[:, None] * np.arange(Q)[None], Q)
    return np_split(np.concatenate([c, s], axis=1))


def offset_table():
    c, s = cs(np.arange(Q)[:, None] * np.arange(256)[None], Q)
    return np_split(np.concatenate([c, s], axis=0) / Q)


def pack_kernel(raw_ref, out_ref, raw_buf, buf_ref, sems):
    wide = C // 4
    copies = [
        pltpu.make_async_copy(
            raw_ref.at[:, pl.ds(k * wide, wide)], raw_buf.at[:, pl.ds(k * wide, wide)], sems.at[k]
        )
        for k in range(4)
    ]
    for copy in copies:
        copy.start()
    for i in range(BLK):
        if i % 4 == 0:
            copies[i // 4].wait()
        x = raw_buf[:, i * 256 : (i + 1) * 256]
        rows = jnp.concatenate([x[:, :DEV], x[:, DEV:]], axis=0)
        buf_ref[pl.ds(i, DEV, stride=BLK), :] = rows.T
    out_ref[...] = buf_ref[...].astype(BF)


def dot(a, b):
    return jnp.dot(a, b, preferred_element_type=F32)


def spectra_kernel(in_ref, s1_ref, tw_ref, s2_ref, win_ref, taper_ref, out_ref, buf_ref, wide_ref):
    buf_ref[...] = in_ref[...].astype(F32)
    stage1, stage2 = s1_ref[...], s2_ref[...]
    cos, sin = tw_ref[0], tw_ref[1]
    lane = lax.broadcasted_iota(jnp.int32, (DEV, DEV), 1) % J2
    for g in range(4):
        samples = jnp.concatenate(
            [buf_ref[pl.ds(4 * g + s, DEV, stride=BLK), :] for s in range(4)], axis=1
        ).astype(BF)
        y = dot(stage1, samples)
        reals, imags = [], []
        for s in range(4):
            y_re, y_im = y[:DEV, s * DEV : (s + 1) * DEV], y[DEV:, s * DEV : (s + 1) * DEV]
            reals.append((y_re * cos + y_im * sin).astype(BF))
            imags.append((y_im * cos - y_re * sin).astype(BF))
        spec = dot(jnp.concatenate(reals + imags, axis=1), stage2)
        re, im = spec[:, :DEV], spec[:, DEV:]
        wide_ref[g] = re
        wide_ref[4 + g] = im
    for g in range(4):
        re, im = wide_ref[g], wide_ref[4 + g]
        amp = jnp.sqrt(re * re + im * im)
        after = jnp.where(lane == J2 - 1, 0.0, pltpu.roll(amp, DEV - 1, 1))
        before = jnp.where(lane == 0, 0.0, pltpu.roll(amp, 1, 1))
        total = dot(win_ref[...], jnp.concatenate([amp, after, before], axis=0).astype(BF))
        gain = taper_ref[...] / (total * (1.0 / (2 * SW + 1)) + EPS)
        buf_ref[pl.ds(g, DEV, stride=8), :] = re * gain
        buf_ref[pl.ds(4 + g, DEV, stride=8), :] = im * gain
    out_ref[...] = buf_ref[: 8 * DEV, :].astype(BF)


def stack_kernel(
    in_ref, mask_ref, rot_ref, eh_ref, el_ref, dh_ref, dl_ref, out_ref,
    buf_ref, f_ref, acc_ref, v_ref,
):
    buf_ref[...] = in_ref[...].astype(F32)
    pieces = [buf_ref[pl.ds(t, DEV, stride=8), :].T.astype(BF) for t in range(8)]
    rows = []
    for part in range(2):
        for i in range(BLK):
            g, s = i // 4, i % 4
            tiles = [
                pieces[4 * part + g][(2 * s + h) * J2 : (2 * s + h + 1) * J2] for h in range(2)
            ]
            rows.append(jnp.concatenate(tiles, axis=1))
    white = jnp.concatenate(rows, axis=0)
    product = dot(white, eh_ref[...]) + dot(white, el_ref[...])
    half = BLK * J2
    f_re = product[:half, :Q] + product[half:, Q:]
    f_im = product[half:, :Q] - product[:half, Q:]
    for part, value in enumerate((f_re, f_im)):
        for k in range(2 * BLK):
            for t in range(4):
                f_ref[pl.ds(part * 1024 + 32 * k + t, 8, stride=4), :] = value[
                    8 * k : 8 * k + 8, t * DEV : (t + 1) * DEV
                ]
    acc_ref[...] = jnp.zeros_like(acc_ref)

    def unit(u, carry):
        at = lambda i, part: pl.ds(pl.multiple_of(part * 1024 + i * 64 + u * 8, 8), 8)
        re = [f_ref[at(i, 0), :] for i in range(BLK)]
        im = [f_ref[at(i, 1), :] for i in range(BLK)]
        for delta in range(FAR):
            sum_re = sum_im = None
            for i in range(BLK - delta):
                j = i + delta
                live = mask_ref[pl.ds(i * BLK + j, 8, stride=0), :]
                a_re, a_im = re[i] * live, im[i] * live
                term = a_re * re[j] + a_im * im[j]
                sum_re = term if sum_re is None else sum_re + term
                if delta:
                    term = a_im * re[j] - a_re * im[j]
                    sum_im = term if sum_im is None else sum_im + term
            acc_ref[2 * delta] = sum_re - acc_ref[2 * delta]
            if delta:
                acc_ref[2 * delta + 1] = sum_im - acc_ref[2 * delta + 1]
        return carry

    lax.fori_loop(0, J2 // 2, unit, 0)
    first = lax.broadcasted_iota(jnp.int32, (8, DEV), 0) < 4
    lane = lax.broadcasted_iota(jnp.int32, (8, DEV), 1)
    parity = jnp.where(lane % 2 == 1, -1.0, 1.0)
    turn = jnp.where(first, -1.0, 1.0)
    for delta in range(BLK):
        if delta < FAR:
            x_re, x_im = acc_ref[2 * delta], acc_ref[2 * delta + 1]
            if delta + 1 < FAR:
                x_re = x_re + parity * acc_ref[2 * delta + 2]
                x_im = x_im + parity * acc_ref[2 * delta + 3]
            s_re, s_im = pltpu.roll(x_re, 4, 0), pltpu.roll(x_im, 4, 0)
            g_re = jnp.where(first, x_re, s_re) + turn * jnp.where(first, s_im, x_im)
            g_im = jnp.where(first, x_im, s_im) - turn * jnp.where(first, s_re, x_re)
        for u in range(4):
            at = pl.ds((delta * 4 + u) * 8, 8)
            to = pl.ds(512 + (delta * 4 + u) * 8, 8)
            if delta < FAR:
                c, s = rot_ref[0, u], rot_ref[1, u]
                v_ref[at, :] = s * g_im - c * g_re
                v_ref[to, :] = -(c * g_im) - s * g_re
            else:
                v_ref[at, :] = jnp.zeros((8, DEV), F32)
                v_ref[to, :] = jnp.zeros((8, DEV), F32)
    shifted = [v_ref[pl.ds(512 * c + t, DEV, stride=4), :] for c in range(2) for t in range(4)]
    v_hi, v_lo = split(jnp.concatenate(shifted, axis=1))
    stacked = dot(v_hi, dh_ref[...]) + dot(v_hi, dl_ref[...]) + dot(v_lo, dh_ref[...])
    left, right = stacked[:, :DEV], stacked[:, DEV:]
    last = lax.broadcasted_iota(jnp.int32, (DEV, DEV), 1) == DEV - 1
    left1, right1 = pltpu.roll(left, DEV - 1, 1), pltpu.roll(right, DEV - 1, 1)
    beyond = jnp.concatenate([left1[8:], jnp.zeros((8, DEV), F32)], axis=0)
    behind = (jnp.where(last, right1, left1), jnp.where(last, beyond, right1))
    same = first == (lane < 64)
    for delta in range(BLK):
        for t in range(2):
            tile = (left, right)[t][8 * delta : 8 * delta + 8]
            pair = jnp.where(same, tile, pltpu.roll(pltpu.roll(tile, 4, 0), 64, 1))
            at = 4 * (64 + 4 * delta + 2 * t)
            out_ref[at : at + 8, :] = pair.astype(BF)
            tile = behind[t][8 * delta : 8 * delta + 8]
            pair = jnp.where(same, pltpu.roll(tile, 64, 1), pltpu.roll(tile, 4, 0))
            at = 4 * (4 * (BLK - 1 - delta) + 2 - 2 * t)
            out_ref[at : at + 8, :] = pair.astype(BF)


def total_kernel(in_ref, place_ref, scale_ref, out_ref):
    total = jnp.sum(in_ref[...].astype(F32).reshape(DEV // 2, 8, DEV), axis=0)
    total = total + pltpu.roll(total, 4, 0)
    low = lax.broadcasted_iota(jnp.int32, (8, DEV), 0) < 4
    lags = jnp.where(low, total, pltpu.roll(total, 64, 1))
    lane = lax.broadcasted_iota(jnp.int32, (8, DEV), 1)
    flipped = jnp.concatenate([lags[7 - j : 8 - j] for j in range(LAGS)], axis=0)
    flipped = jnp.take_along_axis(flipped, (63 - lane) & 127, axis=1)
    out = jnp.where(place_ref[0] == 1, flipped, lags)
    out_ref[...] = out[:, :64] * scale_ref[...]


def pair_counts(mask, columns):
    blocks = mask.shape[0]
    width = C // blocks
    labels = lax.iota(jnp.int32, blocks)
    apart = labels[None, :] - labels[:, None]
    deltas = lax.iota(jnp.int32, 2 * blocks - 1) - (blocks - 1)
    per_delta = jnp.sum(
        mask[None] * (apart[None] == deltas[:, None, None]).astype(jnp.int32), axis=(1, 2)
    )
    offsets = columns - C
    intersection = jnp.maximum(0, width - jnp.abs(offsets[:, None] - width * deltas[None, :]))
    return jnp.sum(intersection * per_delta[None, :], axis=1)


def stack_scale(counts):
    return 1.0 / jnp.sqrt(NB * jnp.maximum(counts, 1).astype(jnp.float32))


VM = pl.BlockSpec(memory_space=pltpu.VMEM)
SM = pl.BlockSpec(memory_space=pltpu.SMEM)
LIMIT = pltpu.CompilerParams(vmem_limit_bytes=24 * 1024 * 1024)


def exchange(x, rows):
    x = x.reshape(DEV, rows, DEV)
    return lax.all_to_all(x, ("blk", "lag"), split_axis=0, concat_axis=0, tiled=True)


def on_device(raw, mask):
    device = lax.axis_index("blk") * lax.axis_size("lag") + lax.axis_index("lag")
    packed = pl.pallas_call(
        pack_kernel,
        out_shape=jax.ShapeDtypeStruct((BLK * DEV, DEV), BF),
        in_specs=[pl.BlockSpec(memory_space=pltpu.HBM)],
        out_specs=VM,
        scratch_shapes=[
            pltpu.VMEM((ROWS, C), F32),
            pltpu.VMEM((BLK * DEV, DEV), F32),
            pltpu.SemaphoreType.DMA((4,)),
        ],
    )(raw)
    series = exchange(packed, BLK).reshape(BLK * DEV, DEV)
    stage1, twiddle, stage2 = time_tables()
    white = pl.pallas_call(
        spectra_kernel,
        out_shape=jax.ShapeDtypeStruct((8 * DEV, DEV), BF),
        in_specs=[VM] * 6,
        out_specs=VM,
        compiler_params=LIMIT,
        scratch_shapes=[pltpu.VMEM((BLK * DEV, DEV), F32), pltpu.VMEM((8, DEV, DEV), F32)],
    )(series, stage1, twiddle, stage2, window_table(), taper_table())
    banded = exchange(white, 8).reshape(8 * DEV, DEV)
    odd = 2 * lax.iota(jnp.int32, LAGS) - (LAGS - 1)
    angle = jnp.mod(odd * (K0 + device), Q).astype(F32) * (2 * math.pi / Q)
    spread = lambda x: jnp.broadcast_to(x.reshape(4, 2, 1, 1), (4, 2, 4, DEV)).reshape(4, 8, DEV)
    rotation = jnp.stack([spread(jnp.cos(angle)), spread(jnp.sin(angle))])
    live = jnp.broadcast_to(mask.astype(F32).reshape(BLK * BLK, 1), (BLK * BLK, DEV))
    parts = pl.pallas_call(
        stack_kernel,
        out_shape=jax.ShapeDtypeStruct((4 * DEV, DEV), BF),
        in_specs=[VM] * 7,
        out_specs=VM,
        compiler_params=LIMIT,
        scratch_shapes=[
            pltpu.VMEM((8 * DEV, DEV), F32),
            pltpu.VMEM((2048, DEV), F32),
            pltpu.VMEM((2 * FAR, 8, DEV), F32),
            pltpu.VMEM((8 * DEV, DEV), F32),
        ],
    )(banded, live, rotation, *channel_table(), *offset_table())
    shares = exchange(parts, 4).reshape(4 * DEV, DEV)
    columns = device * 64 + lax.iota(jnp.int32, 64)
    scale = stack_scale(pair_counts(mask, columns))[None, :]
    place = (device < 64).astype(jnp.int32)[None]
    return pl.pallas_call(
        total_kernel,
        out_shape=jax.ShapeDtypeStruct((LAGS, 64), F32),
        in_specs=[VM, SM, VM],
        out_specs=VM,
        compiler_params=LIMIT,
    )(shares, place, scale)


def solution(mesh):
    return jax.shard_map(
        on_device,
        mesh=mesh,
        in_specs=(P(("blk", "lag"), None), P()),
        out_specs=P(None, ("blk", "lag")),
        check_vma=False,
    )
```

```python
import math

import jax
import jax.numpy as jnp
import numpy as np
from jax import lax
from jax.experimental import pallas as pl
from jax.experimental.pallas import tpu as pltpu
from jax.sharding import PartitionSpec as P

NT = 8192
C = 4096
NB = 2048
K0 = 16
SW = 32
TAPER = 128
LAGS = 8
LAG_STEP = 32
EPS = 1e-06

DEV = 128
ROWS = NT // DEV
BLK = 16
J2 = NB // DEV
Q = 512
FAR = 15

BF = jnp.bfloat16
F32 = jnp.float32


def split(x):
    hi = x.astype(BF)
    return hi, (x - hi.astype(F32)).astype(BF)


def np_split(x):
    hi = np.asarray(x, np.float32).astype(jnp.bfloat16)
    lo = (np.asarray(x, np.float64) - hi.astype(np.float64)).astype(jnp.bfloat16)
    return hi, lo


def cs(numer, period):
    angle = 2 * np.pi * np.mod(numer, period) / period
    return np.cos(angle), np.sin(angle)


def time_tables():
    j1, p = np.arange(DEV), np.arange(DEV)
    c, s = cs((K0 + j1)[:, None] * p[None], DEV)
    stage1 = np.concatenate([c, -s], axis=0).astype(jnp.bfloat16)
    r = np.tile(np.arange(ROWS), 2)
    c, s = cs((K0 + j1)[:, None] * r[None], NT)
    twiddle = np.stack([c, s]).astype(np.float32)
    r, j2 = np.arange(ROWS), np.arange(J2)
    c, s = cs(r[:, None] * j2[None], ROWS)
    eye = np.eye(8)
    place = lambda t: np.einsum("ab,rj->arbj", eye, t).reshape(8 * ROWS, 8 * J2)
    stage2 = np.block([[place(c), place(-s)], [place(s), place(c)]])
    return stage1, twiddle, stage2.astype(jnp.bfloat16)


def window_table():
    i, j = np.arange(DEV)[:, None], np.arange(DEV)[None]
    near = lambda d: (np.abs(d) <= SW).astype(np.float32)
    return np.concatenate([near(i - j), near(i - j - DEV), near(i - j + DEV)], axis=1).astype(
        jnp.bfloat16
    )


def taper_table():
    position = np.arange(DEV)[:, None] + DEV * np.arange(J2)[None]
    edge = np.minimum(position, NB - 1 - position)
    curve = 0.5 - 0.5 * np.cos(math.pi * (edge + 0.5) / TAPER)
    return np.tile(np.where(edge < TAPER, curve, 1.0), (1, DEV // J2)).astype(np.float32)


def channel_table():
    c, s = cs(np.arange(256)[:, None] * (2 * np.arange(256) + 1)[None], 2 * Q)
    return np_split(np.concatenate([c, s], axis=1))


def offset_table():
    c, s = cs((2 * np.arange(256) + 1)[:, None] * np.arange(256)[None], 2 * Q)
    return np_split(np.concatenate([c, s], axis=0) / Q)


def pack_kernel(raw_ref, out_ref, raw_buf, buf_ref, out_buf, in_sems, out_sems):
    wide = C // 8
    takes = [
        pltpu.make_async_copy(
            raw_ref.at[:, pl.ds(k * wide, wide)], raw_buf.at[:, pl.ds(k * wide, wide)], in_sems.at[k]
        )
        for k in range(8)
    ]
    for take in takes:
        take.start()
    gives = []
    for k in range(2):
        for i in range(8):
            if i % 2 == 0:
                takes[4 * k + i // 2].wait()
            at = (8 * k + i) * 256
            rows = jnp.concatenate([raw_buf[:, at : at + DEV], raw_buf[:, at + DEV : at + 256]], axis=0)
            buf_ref[pl.ds(1024 * k + i, DEV, stride=8), :] = rows.T
        out_buf[k] = buf_ref[1024 * k : 1024 * (k + 1), :].reshape(DEV, 8, DEV).astype(BF)
        give = pltpu.make_async_copy(
            out_buf.at[k], out_ref.at[:, pl.ds(8 * k, 8), :], out_sems.at[k]
        )
        give.start()
        gives.append(give)
    for give in gives:
        give.wait()


def dot(a, b):
    return jnp.dot(a, b, preferred_element_type=F32)


def spectra_kernel(
    in_ref, s1_ref, tw_ref, s2_ref, win_ref, taper_ref, out_ref, buf_ref, z_ref, spec_ref
):
    series = in_ref[...].astype(F32).reshape(DEV, 2, 8, DEV)
    for k in range(2):
        buf_ref[1024 * k : 1024 * (k + 1), :] = series[:, k].reshape(1024, DEV)
    stage1 = s1_ref[...]
    for g in range(4):
        samples = jnp.concatenate(
            [
                buf_ref[pl.ds(1024 * (g // 2) + (4 * g + s) % 8, DEV, stride=8), :]
                for s in range(4)
            ],
            axis=1,
        ).astype(BF)
        y = dot(stage1, samples)
        for s in range(4):
            y_re, y_im = y[:DEV, s * DEV : (s + 1) * DEV], y[DEV:, s * DEV : (s + 1) * DEV]
            z_ref[g * DEV : (g + 1) * DEV, s * DEV : (s + 1) * DEV] = (
                y_re * tw_ref[0] + y_im * tw_ref[1]
            ).astype(BF)
            z_ref[g * DEV : (g + 1) * DEV, (4 + s) * DEV : (5 + s) * DEV] = (
                y_im * tw_ref[0] - y_re * tw_ref[1]
            ).astype(BF)
    spec_ref[...] = dot(z_ref[...], s2_ref[...])
    lane = lax.broadcasted_iota(jnp.int32, (DEV, DEV), 1) % J2
    for g in range(4):
        re, im = spec_ref[g * DEV : (g + 1) * DEV, :DEV], spec_ref[g * DEV : (g + 1) * DEV, DEV:]
        amp = jnp.sqrt(re * re + im * im)
        after = jnp.where(lane == J2 - 1, 0.0, pltpu.roll(amp, DEV - 1, 1))
        before = jnp.where(lane == 0, 0.0, pltpu.roll(amp, 1, 1))
        total = dot(win_ref[...], jnp.concatenate([amp, after, before], axis=0).astype(BF))
        gain = taper_ref[...] / (total * (1.0 / (2 * SW + 1)) + EPS)
        buf_ref[pl.ds(g, DEV, stride=8), :] = re * gain
        buf_ref[pl.ds(4 + g, DEV, stride=8), :] = im * gain
    out_ref[...] = buf_ref[: 8 * DEV, :].astype(BF)


def stack_kernel(
    in_ref, mask_ref, rot_ref, eh_ref, el_ref, dh_ref, dl_ref, out_ref,
    buf_ref, f_ref, acc_ref, v_ref,
):
    buf_ref[...] = in_ref[...].astype(F32)
    pieces = [buf_ref[pl.ds(t, DEV, stride=8), :].T.astype(BF) for t in range(8)]
    rows = []
    for part in range(2):
        for i in range(BLK):
            g, s = i // 4, i % 4
            tiles = [
                pieces[4 * part + g][(2 * s + h) * J2 : (2 * s + h + 1) * J2] for h in range(2)
            ]
            rows.append(jnp.concatenate(tiles, axis=1))
    white = jnp.concatenate(rows, axis=0)
    product = dot(white, eh_ref[...]) + dot(white, el_ref[...])
    half = BLK * J2
    for t in range(2):
        at = slice(t * DEV, (t + 1) * DEV)
        to = slice(256 + t * DEV, 256 + (t + 1) * DEV)
        rc, rs, ic, ims = product[:half, at], product[:half, to], product[half:, at], product[half:, to]
        for part, sign, value in (
            (0, 0, rc + ims), (0, 1, rc - ims), (1, 0, ic - rs), (1, 1, ic + rs)
        ):
            for k in range(2 * BLK):
                f_ref[pl.ds(part * 1024 + 32 * k + 2 * sign + t, 8, stride=4), :] = value[
                    8 * k : 8 * k + 8
                ]
    acc_ref[...] = jnp.zeros_like(acc_ref)

    def unit(u, carry):
        at = lambda i, part: pl.ds(pl.multiple_of(part * 1024 + i * 64 + u * 8, 8), 8)
        re = [f_ref[at(i, 0), :] for i in range(BLK)]
        im = [f_ref[at(i, 1), :] for i in range(BLK)]
        both = [re[i] + im[i] for i in range(BLK)]
        less = [re[i] - im[i] for i in range(BLK)]
        for delta in range(FAR):
            sums = [None, None, None]
            for i in range(BLK - delta):
                j = i + delta
                live = mask_ref[pl.ds(i * BLK + j, 8, stride=0), :]
                a_re, a_im = re[i] * live, im[i] * live
                if delta == 0:
                    terms = [a_re * re[j] + a_im * im[j]]
                else:
                    terms = [(a_re + a_im) * re[j], a_im * less[j], a_re * both[j]]
                sums = [t if s is None else s + t for s, t in zip(sums, terms)]
            if delta == 0:
                acc_ref[0] = sums[0] - acc_ref[0]
            else:
                acc_ref[2 * delta] = sums[0] - sums[1] - acc_ref[2 * delta]
                acc_ref[2 * delta + 1] = sums[0] - sums[2] - acc_ref[2 * delta + 1]
        return carry

    lax.fori_loop(0, J2 // 2, unit, 0)
    first = lax.broadcasted_iota(jnp.int32, (8, DEV), 0) < 4
    lane = lax.broadcasted_iota(jnp.int32, (8, DEV), 1)
    row = lax.broadcasted_iota(jnp.int32, (8, DEV), 0)
    beside = jnp.where((lane % 2 == 1) == (row % 4 < 2), -1.0, 1.0)
    turn = jnp.where(first, -1.0, 1.0)
    for delta in range(BLK):
        if delta < FAR:
            x_re, x_im = acc_ref[2 * delta], acc_ref[2 * delta + 1]
            if delta + 1 < FAR:
                x_re = x_re - beside * acc_ref[2 * delta + 3]
                x_im = x_im + beside * acc_ref[2 * delta + 2]
            s_re, s_im = pltpu.roll(x_re, 4, 0), pltpu.roll(x_im, 4, 0)
            g_re = jnp.where(first, x_re, s_re) + turn * jnp.where(first, s_im, x_im)
            g_im = jnp.where(first, x_im, s_im) - turn * jnp.where(first, s_re, x_re)
        for u in range(4):
            at = pl.ds((delta * 4 + u) * 8, 8)
            to = pl.ds(512 + (delta * 4 + u) * 8, 8)
            if delta < FAR:
                c, s = rot_ref[0, u], rot_ref[1, u]
                v_ref[at, :] = s * g_im - c * g_re
                v_ref[to, :] = -(c * g_im) - s * g_re
            else:
                v_ref[at, :] = jnp.zeros((8, DEV), F32)
                v_ref[to, :] = jnp.zeros((8, DEV), F32)
    load = lambda c, t: v_ref[pl.ds(512 * c + t, DEV, stride=4), :]
    folded = [load(0, 0) + load(0, 2), load(0, 1) + load(0, 3)]
    folded += [load(1, 0) - load(1, 2), load(1, 1) - load(1, 3)]
    v_hi, v_lo = split(jnp.concatenate(folded, axis=1))
    fine = dot(jnp.concatenate([v_hi, v_lo], axis=0), dh_ref[...])
    stacked = fine[:DEV] + fine[DEV:] + dot(v_hi, dl_ref[...])
    left, right = stacked[:, :DEV], stacked[:, DEV:]
    last = lax.broadcasted_iota(jnp.int32, (DEV, DEV), 1) == DEV - 1
    left1, right1 = pltpu.roll(left, DEV - 1, 1), pltpu.roll(right, DEV - 1, 1)
    beyond = jnp.concatenate([left1[8:], jnp.zeros((8, DEV), F32)], axis=0)
    behind = (jnp.where(last, right1, left1), jnp.where(last, beyond, right1))
    same = first == (lane < 64)
    for delta in range(BLK):
        for t in range(2):
            tile = (left, right)[t][8 * delta : 8 * delta + 8]
            pair = jnp.where(same, tile, pltpu.roll(pltpu.roll(tile, 4, 0), 64, 1))
            at = 4 * (64 + 4 * delta + 2 * t)
            out_ref[at : at + 8, :] = pair.astype(BF)
            tile = behind[t][8 * delta : 8 * delta + 8]
            pair = jnp.where(same, pltpu.roll(tile, 64, 1), pltpu.roll(tile, 4, 0))
            at = 4 * (4 * (BLK - 1 - delta) + 2 - 2 * t)
            out_ref[at : at + 8, :] = pair.astype(BF)


def total_kernel(in_ref, place_ref, scale_ref, out_ref):
    total = jnp.sum(in_ref[...].astype(F32).reshape(DEV // 2, 8, DEV), axis=0)
    total = total + pltpu.roll(total, 4, 0)
    low = lax.broadcasted_iota(jnp.int32, (8, DEV), 0) < 4
    lags = jnp.where(low, total, pltpu.roll(total, 64, 1))
    lane = lax.broadcasted_iota(jnp.int32, (8, DEV), 1)
    flipped = jnp.concatenate([lags[7 - j : 8 - j] for j in range(LAGS)], axis=0)
    flipped = jnp.take_along_axis(flipped, (63 - lane) & 127, axis=1)
    out = jnp.where(place_ref[0] == 1, flipped, lags)
    out_ref[...] = out[:, :64] * scale_ref[...]


def pair_counts(mask, columns):
    blocks = mask.shape[0]
    width = C // blocks
    labels = lax.iota(jnp.int32, blocks)
    apart = labels[None, :] - labels[:, None]
    deltas = lax.iota(jnp.int32, 2 * blocks - 1) - (blocks - 1)
    per_delta = jnp.sum(
        mask[None] * (apart[None] == deltas[:, None, None]).astype(jnp.int32), axis=(1, 2)
    )
    offsets = columns - C
    intersection = jnp.maximum(0, width - jnp.abs(offsets[:, None] - width * deltas[None, :]))
    return jnp.sum(intersection * per_delta[None, :], axis=1)


def stack_scale(counts):
    return 1.0 / jnp.sqrt(NB * jnp.maximum(counts, 1).astype(jnp.float32))


VM = pl.BlockSpec(memory_space=pltpu.VMEM)
SM = pl.BlockSpec(memory_space=pltpu.SMEM)
LIMIT = pltpu.CompilerParams(vmem_limit_bytes=24 * 1024 * 1024)


def exchange(x, rows):
    x = x.reshape(DEV, rows, DEV)
    return lax.all_to_all(x, ("blk", "lag"), split_axis=0, concat_axis=0, tiled=True)


def on_device(raw, mask):
    device = lax.axis_index("blk") * lax.axis_size("lag") + lax.axis_index("lag")
    packed = pl.pallas_call(
        pack_kernel,
        out_shape=jax.ShapeDtypeStruct((DEV, BLK, DEV), BF),
        in_specs=[pl.BlockSpec(memory_space=pltpu.HBM)],
        out_specs=pl.BlockSpec(memory_space=pltpu.HBM),
        scratch_shapes=[
            pltpu.VMEM((ROWS, C), F32),
            pltpu.VMEM((BLK * DEV, DEV), F32),
            pltpu.VMEM((2, DEV, 8, DEV), BF),
            pltpu.SemaphoreType.DMA((8,)),
            pltpu.SemaphoreType.DMA((2,)),
        ],
    )(raw)
    series = exchange(packed, BLK).reshape(BLK * DEV, DEV)
    stage1, twiddle, stage2 = time_tables()
    white = pl.pallas_call(
        spectra_kernel,
        out_shape=jax.ShapeDtypeStruct((8 * DEV, DEV), BF),
        in_specs=[VM] * 6,
        out_specs=VM,
        compiler_params=LIMIT,
        scratch_shapes=[
            pltpu.VMEM((BLK * DEV, DEV), F32),
            pltpu.VMEM((4 * DEV, 8 * DEV), BF),
            pltpu.VMEM((4 * DEV, 2 * DEV), F32),
        ],
    )(series, stage1, twiddle, stage2, window_table(), taper_table())
    banded = exchange(white, 8).reshape(8 * DEV, DEV)
    odd = 2 * lax.iota(jnp.int32, LAGS) - (LAGS - 1)
    angle = jnp.mod(odd * (K0 + device), Q).astype(F32) * (2 * math.pi / Q)
    spread = lambda x: jnp.broadcast_to(x.reshape(4, 2, 1, 1), (4, 2, 4, DEV)).reshape(4, 8, DEV)
    rotation = jnp.stack([spread(jnp.cos(angle)), spread(jnp.sin(angle))])
    live = jnp.broadcast_to(mask.astype(F32).reshape(BLK * BLK, 1), (BLK * BLK, DEV))
    parts = pl.pallas_call(
        stack_kernel,
        out_shape=jax.ShapeDtypeStruct((4 * DEV, DEV), BF),
        in_specs=[VM] * 7,
        out_specs=VM,
        compiler_params=LIMIT,
        scratch_shapes=[
            pltpu.VMEM((8 * DEV, DEV), F32),
            pltpu.VMEM((2048, DEV), F32),
            pltpu.VMEM((2 * FAR, 8, DEV), F32),
            pltpu.VMEM((8 * DEV, DEV), F32),
        ],
    )(banded, live, rotation, *channel_table(), *offset_table())
    shares = exchange(parts, 4).reshape(4 * DEV, DEV)
    columns = device * 64 + lax.iota(jnp.int32, 64)
    scale = stack_scale(pair_counts(mask, columns))[None, :]
    place = (device < 64).astype(jnp.int32)[None]
    return pl.pallas_call(
        total_kernel,
        out_shape=jax.ShapeDtypeStruct((LAGS, 64), F32),
        in_specs=[VM, SM, VM],
        out_specs=VM,
        compiler_params=LIMIT,
    )(shares, place, scale)


def solution(mesh):
    return jax.shard_map(
        on_device,
        mesh=mesh,
        in_specs=(P(("blk", "lag"), None), P()),
        out_specs=P(None, ("blk", "lag")),
        check_vma=False,
    )
```

```python
import math

import jax
import jax.numpy as jnp
import numpy as np
from jax import lax
from jax.experimental import pallas as pl
from jax.experimental.pallas import tpu as pltpu
from jax.sharding import PartitionSpec as P

NT = 8192
C = 4096
NB = 2048
K0 = 16
SW = 32
TAPER = 128
LAGS = 8
LAG_STEP = 32
EPS = 1e-06

DEV = 128
ROWS = NT // DEV
BLK = 16
J2 = NB // DEV
Q = 512
FAR = 15

BF = jnp.bfloat16
F32 = jnp.float32


def split(x):
    hi = x.astype(BF)
    return hi, (x - hi.astype(F32)).astype(BF)


def np_split(x):
    hi = np.asarray(x, np.float32).astype(jnp.bfloat16)
    lo = (np.asarray(x, np.float64) - hi.astype(np.float64)).astype(jnp.bfloat16)
    return hi, lo


def cs(numer, period):
    angle = 2 * np.pi * np.mod(numer, period) / period
    return np.cos(angle), np.sin(angle)


def first_bins():
    n = np.arange(64)
    residue = np.concatenate([n, (DEV - n) % DEV])
    residue[64] = 64
    return np.where(residue < K0, residue + DEV, residue)


def first_bin(row):
    residue = jnp.where(row <= 64, row, 192 - row)
    return jnp.where(residue < K0, residue + DEV, residue)


def time_tables():
    n, p = np.arange(64), np.arange(DEV)
    c, s = cs(n[:, None] * p[None], DEV)
    stage1 = np.concatenate([c, -s], axis=0)
    stage1[64] = np.cos(np.pi * p)
    r = np.tile(np.arange(ROWS), 2)
    c, s = cs(first_bins()[:, None] * r[None], NT)
    mirror = np.where(np.arange(DEV) < 64, 1.0, -1.0)[:, None]
    twiddle = np.stack([c, mirror * s, mirror * c, s]).astype(np.float32)
    r, j2 = np.arange(ROWS), np.arange(J2)
    c, s = cs(r[:, None] * j2[None], ROWS)
    eye = np.eye(8)
    place = lambda t: np.einsum("ab,rj->arbj", eye, t).reshape(8 * ROWS, 8 * J2)
    stage2 = np.block([[place(c), place(-s)], [place(s), place(c)]])
    return stage1.astype(jnp.bfloat16), twiddle, stage2.astype(jnp.bfloat16)


AFTER, BEFORE = slice(16, 48), (slice(0, 16), slice(64, 96))


def window_table():
    bins = first_bins()
    gap = bins[:, None] - bins[None]
    near = lambda d: (np.abs(d) <= SW).astype(np.float32)
    after, before = near(gap - DEV), near(gap + DEV)
    return np.concatenate(
        [near(gap), after[:, AFTER]] + [before[:, rows] for rows in BEFORE], axis=1
    ).astype(jnp.bfloat16)


def taper_table():
    position = (first_bins() - K0)[:, None] + DEV * np.arange(J2)[None]
    edge = np.minimum(position, NB - 1 - position)
    curve = 0.5 - 0.5 * np.cos(math.pi * (edge + 0.5) / TAPER)
    return np.tile(np.where(edge < TAPER, curve, 1.0), (1, 2 * DEV // J2)).astype(np.float32)


def channel_table():
    c, s = cs(np.arange(256)[:, None] * (2 * np.arange(256) + 1)[None], 2 * Q)
    return np_split(np.concatenate([c, s], axis=1))


def offset_table():
    c, s = cs((2 * np.arange(256) + 1)[:, None] * np.arange(256)[None], 2 * Q)
    return np_split(np.concatenate([c, s], axis=0) / Q)


def pack_kernel(raw_ref, out_ref, raw_buf, buf_ref, out_buf, in_sems, out_sems):
    wide = C // 2
    takes = [
        pltpu.make_async_copy(
            raw_ref.at[:, pl.ds(k * wide, wide)], raw_buf.at[:, pl.ds(k * wide, wide)], in_sems.at[k]
        )
        for k in range(2)
    ]
    for take in takes:
        take.start()
    gives = []
    for k in range(2):
        takes[k].wait()
        for i in range(8):
            at = (8 * k + i) * 256
            rows = jnp.concatenate([raw_buf[:, at : at + DEV], raw_buf[:, at + DEV : at + 256]], axis=0)
            buf_ref[pl.ds(1024 * k + i, DEV, stride=8), :] = rows.T
        out_buf[k] = buf_ref[1024 * k : 1024 * (k + 1), :].reshape(DEV, 8, DEV).astype(BF)
        give = pltpu.make_async_copy(
            out_buf.at[k], out_ref.at[:, pl.ds(8 * k, 8), :], out_sems.at[k]
        )
        give.start()
        gives.append(give)
    for give in gives:
        give.wait()


def dot(a, b):
    return jnp.dot(a, b, preferred_element_type=F32)


def spectra_kernel(
    in_ref, s1_ref, tw_ref, s2_ref, win_ref, taper_ref, out_ref, buf_ref, z_ref, white_ref
):
    series = in_ref[...].astype(F32).reshape(DEV, 2, 8, DEV)
    for k in range(2):
        buf_ref[1024 * k : 1024 * (k + 1), :] = series[:, k].reshape(1024, DEV)
    top_row = lax.broadcasted_iota(jnp.int32, (8, DEV), 0) == 0
    lane = lax.broadcasted_iota(jnp.int32, (1, DEV), 1) % J2

    def turn(g, w):
        rows = [
            buf_ref[pl.ds(1024 * (g // 2) + (4 * g + 2 * w + s) % 8, DEV, stride=8), :]
            for s in range(2)
        ]
        y = dot(s1_ref[...], jnp.concatenate(rows, axis=1).astype(BF))
        for s in range(2):
            re, im = y[:64, s * DEV : (s + 1) * DEV], y[64:, s * DEV : (s + 1) * DEV]
            no_im = jnp.concatenate([jnp.where(top_row, 0.0, im[:8]), im[8:]], axis=0)
            re_64 = jnp.concatenate([jnp.where(top_row, im[:8], re[:8]), re[8:]], axis=0)
            for half, real in enumerate((re, re_64)):
                at = slice(half * 64, half * 64 + 64)
                to = slice(g * DEV + half * 64, g * DEV + half * 64 + 64)
                col = 2 * w + s
                z_ref[to, col * DEV : (col + 1) * DEV] = (
                    real * tw_ref[0, at] + no_im * tw_ref[1, at]
                ).astype(BF)
                z_ref[to, (4 + col) * DEV : (5 + col) * DEV] = (
                    no_im * tw_ref[2, at] - real * tw_ref[3, at]
                ).astype(BF)

    def shifted(x, by, edge):
        tiles = [pltpu.roll(x[:, s * DEV : (s + 1) * DEV], by, 1) for s in range(2)]
        return jnp.concatenate([jnp.where(lane == edge, 0.0, t) for t in tiles], axis=1)

    def whiten(h, spec):
        re, im = (
            jnp.concatenate([spec[:DEV, at : at + DEV], spec[DEV:, at : at + DEV]], axis=1)
            for at in (0, DEV)
        )
        power = re * re + im * im
        amp = power * lax.rsqrt(jnp.maximum(power, 1e-30))
        near = [amp, shifted(amp[AFTER], DEV - 1, J2 - 1)]
        near += [shifted(amp[rows], 1, 0) for rows in BEFORE]
        total = dot(win_ref[...], jnp.concatenate(near, axis=0).astype(BF))
        gain = taper_ref[...] / (total * (1.0 / (2 * SW + 1)) + EPS)
        for part, value in enumerate((re * gain, im * gain)):
            for s in range(2):
                white_ref[pl.ds(4 * part + 2 * h + s, DEV, stride=8), :] = value[
                    :, s * DEV : (s + 1) * DEV
                ]

    for h in range(2):
        for g in (2 * h, 2 * h + 1):
            for w in range(2):
                turn(g, w)
        whiten(h, dot(z_ref[2 * h * DEV : 2 * (h + 1) * DEV, :], s2_ref[...]))
    out_ref[...] = white_ref[...].astype(BF)


def stack_kernel(
    in_ref, mask_ref, rot_ref, eh_ref, el_ref, dh_ref, dl_ref, out_ref,
    buf_ref, f_ref, acc_ref, v_ref,
):
    buf_ref[...] = in_ref[...].astype(F32)
    pieces = [buf_ref[pl.ds(t, DEV, stride=8), :].T.astype(BF) for t in range(8)]
    rows = []
    for part in range(2):
        for i in range(BLK):
            g, s = i // 4, i % 4
            tiles = [
                pieces[4 * part + g][(2 * s + h) * J2 : (2 * s + h + 1) * J2] for h in range(2)
            ]
            rows.append(jnp.concatenate(tiles, axis=1))
    white = jnp.concatenate(rows, axis=0)
    product = dot(white, eh_ref[...]) + dot(white, el_ref[...])
    half = BLK * J2
    for t in range(2):
        at = slice(t * DEV, (t + 1) * DEV)
        to = slice(256 + t * DEV, 256 + (t + 1) * DEV)
        rc, rs, ic, ims = product[:half, at], product[:half, to], product[half:, at], product[half:, to]
        for part, sign, value in (
            (0, 0, rc + ims), (0, 1, rc - ims), (1, 0, ic - rs), (1, 1, ic + rs)
        ):
            for k in range(2 * BLK):
                f_ref[pl.ds(part * 1024 + 32 * k + 2 * sign + t, 8, stride=4), :] = value[
                    8 * k : 8 * k + 8
                ]
    acc_ref[...] = jnp.zeros_like(acc_ref)

    def unit(u, carry):
        at = lambda i, part: pl.ds(pl.multiple_of(part * 1024 + i * 64 + u * 8, 8), 8)
        re = [f_ref[at(i, 0), :] for i in range(BLK)]
        im = [f_ref[at(i, 1), :] for i in range(BLK)]
        both = [re[i] + im[i] for i in range(BLK)]
        less = [re[i] - im[i] for i in range(BLK)]
        for delta in range(FAR):
            sums = [None, None, None]
            for i in range(BLK - delta):
                j = i + delta
                live = mask_ref[pl.ds(i * BLK + j, 8, stride=0), :]
                a_re, a_im = re[i] * live, im[i] * live
                if delta == 0:
                    terms = [a_re * re[j] + a_im * im[j]]
                else:
                    terms = [(a_re + a_im) * re[j], a_im * less[j], a_re * both[j]]
                sums = [t if s is None else s + t for s, t in zip(sums, terms)]
            if delta == 0:
                acc_ref[0] = sums[0] - acc_ref[0]
            else:
                acc_ref[2 * delta] = sums[0] - sums[1] - acc_ref[2 * delta]
                acc_ref[2 * delta + 1] = sums[0] - sums[2] - acc_ref[2 * delta + 1]
        return carry

    lax.fori_loop(0, J2 // 2, unit, 0)
    first = lax.broadcasted_iota(jnp.int32, (8, DEV), 0) < 4
    lane = lax.broadcasted_iota(jnp.int32, (8, DEV), 1)
    row = lax.broadcasted_iota(jnp.int32, (8, DEV), 0)
    beside = jnp.where((lane % 2 == 1) == (row % 4 < 2), -1.0, 1.0)
    turn = jnp.where(first, -1.0, 1.0)
    for delta in range(BLK):
        if delta < FAR:
            x_re, x_im = acc_ref[2 * delta], acc_ref[2 * delta + 1]
            if delta + 1 < FAR:
                x_re = x_re - beside * acc_ref[2 * delta + 3]
                x_im = x_im + beside * acc_ref[2 * delta + 2]
            s_re, s_im = pltpu.roll(x_re, 4, 0), pltpu.roll(x_im, 4, 0)
            g_re = jnp.where(first, x_re, s_re) + turn * jnp.where(first, s_im, x_im)
            g_im = jnp.where(first, x_im, s_im) - turn * jnp.where(first, s_re, x_re)
        for u in range(4):
            at = pl.ds((delta * 4 + u) * 8, 8)
            to = pl.ds(512 + (delta * 4 + u) * 8, 8)
            if delta < FAR:
                c, s = rot_ref[0, u], rot_ref[1, u]
                v_ref[at, :] = s * g_im - c * g_re
                v_ref[to, :] = -(c * g_im) - s * g_re
            else:
                v_ref[at, :] = jnp.zeros((8, DEV), F32)
                v_ref[to, :] = jnp.zeros((8, DEV), F32)
    load = lambda c, t: v_ref[pl.ds(512 * c + t, DEV, stride=4), :]
    folded = [load(0, 0) + load(0, 2), load(0, 1) + load(0, 3)]
    folded += [load(1, 0) - load(1, 2), load(1, 1) - load(1, 3)]
    v_hi, v_lo = split(jnp.concatenate(folded, axis=1))
    fine = dot(jnp.concatenate([v_hi, v_lo], axis=0), dh_ref[...])
    stacked = fine[:DEV] + fine[DEV:] + dot(v_hi, dl_ref[...])
    left, right = stacked[:, :DEV], stacked[:, DEV:]
    last = lax.broadcasted_iota(jnp.int32, (DEV, DEV), 1) == DEV - 1
    left1, right1 = pltpu.roll(left, DEV - 1, 1), pltpu.roll(right, DEV - 1, 1)
    beyond = jnp.concatenate([left1[8:], jnp.zeros((8, DEV), F32)], axis=0)
    behind = (jnp.where(last, right1, left1), jnp.where(last, beyond, right1))
    same = first == (lane < 64)
    for delta in range(BLK):
        for t in range(2):
            tile = (left, right)[t][8 * delta : 8 * delta + 8]
            pair = jnp.where(same, tile, pltpu.roll(pltpu.roll(tile, 4, 0), 64, 1))
            at = 4 * (64 + 4 * delta + 2 * t)
            out_ref[at : at + 8, :] = pair.astype(BF)
            tile = behind[t][8 * delta : 8 * delta + 8]
            pair = jnp.where(same, pltpu.roll(tile, 64, 1), pltpu.roll(tile, 4, 0))
            at = 4 * (4 * (BLK - 1 - delta) + 2 - 2 * t)
            out_ref[at : at + 8, :] = pair.astype(BF)


def total_kernel(in_ref, place_ref, scale_ref, out_ref):
    total = jnp.sum(in_ref[...].astype(F32).reshape(DEV // 2, 8, DEV), axis=0)
    total = total + pltpu.roll(total, 4, 0)
    low = lax.broadcasted_iota(jnp.int32, (8, DEV), 0) < 4
    lags = jnp.where(low, total, pltpu.roll(total, 64, 1))
    lane = lax.broadcasted_iota(jnp.int32, (8, DEV), 1)
    flipped = jnp.concatenate([lags[7 - j : 8 - j] for j in range(LAGS)], axis=0)
    flipped = jnp.take_along_axis(flipped, (63 - lane) & 127, axis=1)
    out = jnp.where(place_ref[0] == 1, flipped, lags)
    out_ref[...] = out[:, :64] * scale_ref[...]


def pair_counts(mask, columns):
    blocks = mask.shape[0]
    width = C // blocks
    labels = lax.iota(jnp.int32, blocks)
    apart = labels[None, :] - labels[:, None]
    deltas = lax.iota(jnp.int32, 2 * blocks - 1) - (blocks - 1)
    per_delta = jnp.sum(
        mask[None] * (apart[None] == deltas[:, None, None]).astype(jnp.int32), axis=(1, 2)
    )
    offsets = columns - C
    intersection = jnp.maximum(0, width - jnp.abs(offsets[:, None] - width * deltas[None, :]))
    return jnp.sum(intersection * per_delta[None, :], axis=1)


def stack_scale(counts):
    return 1.0 / jnp.sqrt(NB * jnp.maximum(counts, 1).astype(jnp.float32))


VM = pl.BlockSpec(memory_space=pltpu.VMEM)
SM = pl.BlockSpec(memory_space=pltpu.SMEM)
LIMIT = pltpu.CompilerParams(vmem_limit_bytes=24 * 1024 * 1024)


def exchange(x, rows):
    x = x.reshape(DEV, rows, DEV)
    return lax.all_to_all(x, ("blk", "lag"), split_axis=0, concat_axis=0, tiled=True)


def on_device(raw, mask):
    device = lax.axis_index("blk") * lax.axis_size("lag") + lax.axis_index("lag")
    packed = pl.pallas_call(
        pack_kernel,
        out_shape=jax.ShapeDtypeStruct((DEV, BLK, DEV), BF),
        in_specs=[pl.BlockSpec(memory_space=pltpu.HBM)],
        out_specs=pl.BlockSpec(memory_space=pltpu.HBM),
        scratch_shapes=[
            pltpu.VMEM((ROWS, C), F32),
            pltpu.VMEM((BLK * DEV, DEV), F32),
            pltpu.VMEM((2, DEV, 8, DEV), BF),
            pltpu.SemaphoreType.DMA((2,)),
            pltpu.SemaphoreType.DMA((2,)),
        ],
    )(raw)
    series = exchange(packed, BLK).reshape(BLK * DEV, DEV)
    stage1, twiddle, stage2 = time_tables()
    white = pl.pallas_call(
        spectra_kernel,
        out_shape=jax.ShapeDtypeStruct((8 * DEV, DEV), BF),
        in_specs=[VM] * 6,
        out_specs=VM,
        compiler_params=LIMIT,
        scratch_shapes=[
            pltpu.VMEM((BLK * DEV, DEV), F32),
            pltpu.VMEM((4 * DEV, 8 * DEV), BF),
            pltpu.VMEM((8 * DEV, DEV), F32),
        ],
    )(series, stage1, twiddle, stage2, window_table(), taper_table())
    banded = exchange(white, 8).reshape(8 * DEV, DEV)
    odd = 2 * lax.iota(jnp.int32, LAGS) - (LAGS - 1)
    angle = jnp.mod(odd * first_bin(device), Q).astype(F32) * (2 * math.pi / Q)
    spread = lambda x: jnp.broadcast_to(x.reshape(4, 2, 1, 1), (4, 2, 4, DEV)).reshape(4, 8, DEV)
    rotation = jnp.stack([spread(jnp.cos(angle)), spread(jnp.sin(angle))])
    live = jnp.broadcast_to(mask.astype(F32).reshape(BLK * BLK, 1), (BLK * BLK, DEV))
    parts = pl.pallas_call(
        stack_kernel,
        out_shape=jax.ShapeDtypeStruct((4 * DEV, DEV), BF),
        in_specs=[VM] * 7,
        out_specs=VM,
        compiler_params=LIMIT,
        scratch_shapes=[
            pltpu.VMEM((8 * DEV, DEV), F32),
            pltpu.VMEM((2048, DEV), F32),
            pltpu.VMEM((2 * FAR, 8, DEV), F32),
            pltpu.VMEM((8 * DEV, DEV), F32),
        ],
    )(banded, live, rotation, *channel_table(), *offset_table())
    shares = exchange(parts, 4).reshape(4 * DEV, DEV)
    columns = device * 64 + lax.iota(jnp.int32, 64)
    scale = stack_scale(pair_counts(mask, columns))[None, :]
    place = (device < 64).astype(jnp.int32)[None]
    return pl.pallas_call(
        total_kernel,
        out_shape=jax.ShapeDtypeStruct((LAGS, 64), F32),
        in_specs=[VM, SM, VM],
        out_specs=VM,
        compiler_params=LIMIT,
    )(shares, place, scale)


def solution(mesh):
    return jax.shard_map(
        on_device,
        mesh=mesh,
        in_specs=(P(("blk", "lag"), None), P()),
        out_specs=P(None, ("blk", "lag")),
        check_vma=False,
    )
```

```python
import math

import jax
import jax.numpy as jnp
import numpy as np
from jax import lax
from jax.experimental import pallas as pl
from jax.experimental.pallas import tpu as pltpu
from jax.sharding import PartitionSpec as P

NT = 8192
C = 4096
NB = 2048
K0 = 16
SW = 32
TAPER = 128
LAGS = 8
LAG_STEP = 32
EPS = 1e-06

DEV = 128
ROWS = NT // DEV
BLK = 16
J2 = NB // DEV
Q = 512
FAR = 15

BF = jnp.bfloat16
F32 = jnp.float32


def split(x):
    hi = x.astype(BF)
    return hi, (x - hi.astype(F32)).astype(BF)


def np_split(x):
    hi = np.asarray(x, np.float32).astype(jnp.bfloat16)
    lo = (np.asarray(x, np.float64) - hi.astype(np.float64)).astype(jnp.bfloat16)
    return hi, lo


def cs(numer, period):
    angle = 2 * np.pi * np.mod(numer, period) / period
    return np.cos(angle), np.sin(angle)


def first_bins():
    n = np.arange(64)
    residue = np.concatenate([n, (DEV - n) % DEV])
    residue[64] = 64
    return np.where(residue < K0, residue + DEV, residue)


def first_bin(row):
    residue = jnp.where(row <= 64, row, 192 - row)
    return jnp.where(residue < K0, residue + DEV, residue)


def time_tables():
    n, p = np.arange(64), np.arange(DEV)
    c, s = cs(n[:, None] * p[None], DEV)
    stage1 = np.concatenate([c, -s], axis=0)
    stage1[64] = np.cos(np.pi * p)
    r = np.tile(np.arange(ROWS), 2)
    c, s = cs(first_bins()[:, None] * r[None], NT)
    mirror = np.where(np.arange(DEV) < 64, 1.0, -1.0)[:, None]
    twiddle = np.stack([c, mirror * s, mirror * c, s]).astype(np.float32)
    r, j2 = np.arange(ROWS), np.arange(J2)
    c, s = cs(r[:, None] * j2[None], ROWS)
    eye = np.eye(8)
    place = lambda t: np.einsum("ab,rj->arbj", eye, t).reshape(8 * ROWS, 8 * J2)
    stage2 = np.block([[place(c), place(-s)], [place(s), place(c)]])
    return stage1.astype(jnp.bfloat16), twiddle, stage2.astype(jnp.bfloat16)


AFTER, BEFORE = slice(16, 48), (slice(0, 16), slice(64, 96))


def window_table():
    bins = first_bins()
    gap = bins[:, None] - bins[None]
    near = lambda d: (np.abs(d) <= SW).astype(np.float32)
    after, before = near(gap - DEV), near(gap + DEV)
    return np.concatenate(
        [near(gap), after[:, AFTER]] + [before[:, rows] for rows in BEFORE], axis=1
    ).astype(jnp.bfloat16)


def taper_table():
    position = (first_bins() - K0)[:, None] + DEV * np.arange(J2)[None]
    edge = np.minimum(position, NB - 1 - position)
    curve = 0.5 - 0.5 * np.cos(math.pi * (edge + 0.5) / TAPER)
    return np.tile(np.where(edge < TAPER, curve, 1.0), (1, 2 * DEV // J2)).astype(np.float32)


def channel_table():
    c, s = cs(np.arange(256)[:, None] * (2 * np.arange(256) + 1)[None], 2 * Q)
    return np_split(np.concatenate([c, s], axis=1))


def offset_table():
    c, s = cs((2 * np.arange(256) + 1)[:, None] * np.arange(256)[None], 2 * Q)
    return np_split(np.concatenate([c, s], axis=0) / Q)


def pack_kernel(raw_ref, out_ref, raw_buf, buf_ref, out_buf, in_sems, out_sems):
    wide = C // 2
    takes = [
        pltpu.make_async_copy(
            raw_ref.at[:, pl.ds(k * wide, wide)], raw_buf.at[:, pl.ds(k * wide, wide)], in_sems.at[k]
        )
        for k in range(2)
    ]
    for take in takes:
        take.start()
    gives = []
    for k in range(2):
        takes[k].wait()
        for i in range(8):
            at = (8 * k + i) * 256
            rows = jnp.concatenate([raw_buf[:, at : at + DEV], raw_buf[:, at + DEV : at + 256]], axis=0)
            buf_ref[pl.ds(1024 * k + i, DEV, stride=8), :] = rows.T
        out_buf[k] = buf_ref[1024 * k : 1024 * (k + 1), :].reshape(DEV, 8, DEV).astype(BF)
        give = pltpu.make_async_copy(
            out_buf.at[k], out_ref.at[:, pl.ds(8 * k, 8), :], out_sems.at[k]
        )
        give.start()
        gives.append(give)
    for give in gives:
        give.wait()


def dot(a, b):
    return jnp.dot(a, b, preferred_element_type=F32)


def spectra_kernel(
    in_ref, s1_ref, tw_ref, s2_ref, win_ref, taper_ref, out_ref, buf_ref, z_ref, white_ref
):
    series = in_ref[...].astype(F32).reshape(DEV, 2, 8, DEV)
    for k in range(2):
        buf_ref[1024 * k : 1024 * (k + 1), :] = series[:, k].reshape(1024, DEV)
    top_row = lax.broadcasted_iota(jnp.int32, (8, DEV), 0) == 0
    lane = lax.broadcasted_iota(jnp.int32, (1, DEV), 1) % J2

    def turn(g, w=0):
        rows = [
            buf_ref[pl.ds(1024 * (g // 2) + (4 * g + s) % 8, DEV, stride=8), :]
            for s in range(4)
        ]
        y = dot(s1_ref[...], jnp.concatenate(rows, axis=1).astype(BF))
        for s in range(4):
            re, im = y[:64, s * DEV : (s + 1) * DEV], y[64:, s * DEV : (s + 1) * DEV]
            no_im = jnp.concatenate([jnp.where(top_row, 0.0, im[:8]), im[8:]], axis=0)
            re_64 = jnp.concatenate([jnp.where(top_row, im[:8], re[:8]), re[8:]], axis=0)
            for half, real in enumerate((re, re_64)):
                at = slice(half * 64, half * 64 + 64)
                to = slice(g * DEV + half * 64, g * DEV + half * 64 + 64)
                col = s
                z_ref[to, col * DEV : (col + 1) * DEV] = (
                    real * tw_ref[0, at] + no_im * tw_ref[1, at]
                ).astype(BF)
                z_ref[to, (4 + col) * DEV : (5 + col) * DEV] = (
                    no_im * tw_ref[2, at] - real * tw_ref[3, at]
                ).astype(BF)

    def shifted(x, by, edge):
        tiles = [pltpu.roll(x[:, s * DEV : (s + 1) * DEV], by, 1) for s in range(2)]
        return jnp.concatenate([jnp.where(lane == edge, 0.0, t) for t in tiles], axis=1)

    def whiten(h, spec):
        re, im = (
            jnp.concatenate([spec[:DEV, at : at + DEV], spec[DEV:, at : at + DEV]], axis=1)
            for at in (0, DEV)
        )
        power = re * re + im * im
        amp = power * lax.rsqrt(jnp.maximum(power, 1e-30))
        near = [amp, shifted(amp[AFTER], DEV - 1, J2 - 1)]
        near += [shifted(amp[rows], 1, 0) for rows in BEFORE]
        total = dot(win_ref[...], jnp.concatenate(near, axis=0).astype(BF))
        gain = taper_ref[...] / (total * (1.0 / (2 * SW + 1)) + EPS)
        for part, value in enumerate((re * gain, im * gain)):
            for s in range(2):
                white_ref[pl.ds(4 * part + 2 * h + s, DEV, stride=8), :] = value[
                    :, s * DEV : (s + 1) * DEV
                ]

    for g in range(4):
        turn(g)
    spec = dot(z_ref[...], s2_ref[...])
    for h in range(2):
        whiten(h, spec[2 * h * DEV : 2 * (h + 1) * DEV])
    out_ref[...] = white_ref[...].astype(BF)


def stack_kernel(
    in_ref, mask_ref, rot_ref, eh_ref, el_ref, dh_ref, dl_ref, out_ref,
    buf_ref, f_ref, acc_ref, v_ref,
):
    buf_ref[...] = in_ref[...].astype(F32)
    pieces = [buf_ref[pl.ds(t, DEV, stride=8), :].T.astype(BF) for t in range(8)]
    rows = []
    for part in range(2):
        for i in range(BLK):
            g, s = i // 4, i % 4
            tiles = [
                pieces[4 * part + g][(2 * s + h) * J2 : (2 * s + h + 1) * J2] for h in range(2)
            ]
            rows.append(jnp.concatenate(tiles, axis=1))
    white = jnp.concatenate(rows, axis=0)
    product = dot(white, eh_ref[...]) + dot(white, el_ref[...])
    half = BLK * J2
    for t in range(2):
        at = slice(t * DEV, (t + 1) * DEV)
        to = slice(256 + t * DEV, 256 + (t + 1) * DEV)
        rc, rs, ic, ims = product[:half, at], product[:half, to], product[half:, at], product[half:, to]
        for part, sign, value in (
            (0, 0, rc + ims), (0, 1, rc - ims), (1, 0, ic - rs), (1, 1, ic + rs)
        ):
            for k in range(2 * BLK):
                f_ref[pl.ds(part * 1024 + 32 * k + 2 * sign + t, 8, stride=4), :] = value[
                    8 * k : 8 * k + 8
                ]
    acc_ref[...] = jnp.zeros_like(acc_ref)

    def unit(u, carry):
        at = lambda i, part: pl.ds(pl.multiple_of(part * 1024 + i * 64 + u * 8, 8), 8)
        re = [f_ref[at(i, 0), :] for i in range(BLK)]
        im = [f_ref[at(i, 1), :] for i in range(BLK)]
        both = [re[i] + im[i] for i in range(BLK)]
        less = [re[i] - im[i] for i in range(BLK)]
        for delta in range(FAR):
            sums = [None, None, None]
            for i in range(BLK - delta):
                j = i + delta
                live = mask_ref[pl.ds(i * BLK + j, 8, stride=0), :]
                a_re, a_im = re[i] * live, im[i] * live
                if delta == 0:
                    terms = [a_re * re[j] + a_im * im[j]]
                else:
                    terms = [(a_re + a_im) * re[j], a_im * less[j], a_re * both[j]]
                sums = [t if s is None else s + t for s, t in zip(sums, terms)]
            if delta == 0:
                acc_ref[0] = sums[0] - acc_ref[0]
            else:
                acc_ref[2 * delta] = sums[0] - sums[1] - acc_ref[2 * delta]
                acc_ref[2 * delta + 1] = sums[0] - sums[2] - acc_ref[2 * delta + 1]
        return carry

    lax.fori_loop(0, J2 // 2, unit, 0)
    first = lax.broadcasted_iota(jnp.int32, (8, DEV), 0) < 4
    lane = lax.broadcasted_iota(jnp.int32, (8, DEV), 1)
    row = lax.broadcasted_iota(jnp.int32, (8, DEV), 0)
    beside = jnp.where((lane % 2 == 1) == (row % 4 < 2), -1.0, 1.0)
    turn = jnp.where(first, -1.0, 1.0)
    for delta in range(BLK):
        if delta < FAR:
            x_re, x_im = acc_ref[2 * delta], acc_ref[2 * delta + 1]
            if delta + 1 < FAR:
                x_re = x_re - beside * acc_ref[2 * delta + 3]
                x_im = x_im + beside * acc_ref[2 * delta + 2]
            s_re, s_im = pltpu.roll(x_re, 4, 0), pltpu.roll(x_im, 4, 0)
            g_re = jnp.where(first, x_re, s_re) + turn * jnp.where(first, s_im, x_im)
            g_im = jnp.where(first, x_im, s_im) - turn * jnp.where(first, s_re, x_re)
        for u in range(4):
            at = pl.ds((delta * 4 + u) * 8, 8)
            to = pl.ds(512 + (delta * 4 + u) * 8, 8)
            if delta < FAR:
                c, s = rot_ref[0, u], rot_ref[1, u]
                v_ref[at, :] = s * g_im - c * g_re
                v_ref[to, :] = -(c * g_im) - s * g_re
            else:
                v_ref[at, :] = jnp.zeros((8, DEV), F32)
                v_ref[to, :] = jnp.zeros((8, DEV), F32)
    load = lambda c, t: v_ref[pl.ds(512 * c + t, DEV, stride=4), :]
    folded = [load(0, 0) + load(0, 2), load(0, 1) + load(0, 3)]
    folded += [load(1, 0) - load(1, 2), load(1, 1) - load(1, 3)]
    v_hi, v_lo = split(jnp.concatenate(folded, axis=1))
    fine = dot(jnp.concatenate([v_hi, v_lo], axis=0), dh_ref[...])
    stacked = fine[:DEV] + fine[DEV:] + dot(v_hi, dl_ref[...])
    left, right = stacked[:, :DEV], stacked[:, DEV:]
    last = lax.broadcasted_iota(jnp.int32, (DEV, DEV), 1) == DEV - 1
    left1, right1 = pltpu.roll(left, DEV - 1, 1), pltpu.roll(right, DEV - 1, 1)
    beyond = jnp.concatenate([left1[8:], jnp.zeros((8, DEV), F32)], axis=0)
    behind = (jnp.where(last, right1, left1), jnp.where(last, beyond, right1))
    same = first == (lane < 64)
    for delta in range(BLK):
        for t in range(2):
            tile = (left, right)[t][8 * delta : 8 * delta + 8]
            pair = jnp.where(same, tile, pltpu.roll(pltpu.roll(tile, 4, 0), 64, 1))
            at = 4 * (64 + 4 * delta + 2 * t)
            out_ref[at : at + 8, :] = pair.astype(BF)
            tile = behind[t][8 * delta : 8 * delta + 8]
            pair = jnp.where(same, pltpu.roll(tile, 64, 1), pltpu.roll(tile, 4, 0))
            at = 4 * (4 * (BLK - 1 - delta) + 2 - 2 * t)
            out_ref[at : at + 8, :] = pair.astype(BF)


def total_kernel(in_ref, place_ref, scale_ref, out_ref):
    total = jnp.sum(in_ref[...].astype(F32).reshape(DEV // 2, 8, DEV), axis=0)
    total = total + pltpu.roll(total, 4, 0)
    low = lax.broadcasted_iota(jnp.int32, (8, DEV), 0) < 4
    lags = jnp.where(low, total, pltpu.roll(total, 64, 1))
    lane = lax.broadcasted_iota(jnp.int32, (8, DEV), 1)
    flipped = jnp.concatenate([lags[7 - j : 8 - j] for j in range(LAGS)], axis=0)
    flipped = jnp.take_along_axis(flipped, (63 - lane) & 127, axis=1)
    out = jnp.where(place_ref[0] == 1, flipped, lags)
    out_ref[...] = out[:, :64] * scale_ref[...]


def pair_counts(mask, columns):
    blocks = mask.shape[0]
    width = C // blocks
    labels = lax.iota(jnp.int32, blocks)
    apart = labels[None, :] - labels[:, None]
    deltas = lax.iota(jnp.int32, 2 * blocks - 1) - (blocks - 1)
    per_delta = jnp.sum(
        mask[None] * (apart[None] == deltas[:, None, None]).astype(jnp.int32), axis=(1, 2)
    )
    offsets = columns - C
    intersection = jnp.maximum(0, width - jnp.abs(offsets[:, None] - width * deltas[None, :]))
    return jnp.sum(intersection * per_delta[None, :], axis=1)


def stack_scale(counts):
    return 1.0 / jnp.sqrt(NB * jnp.maximum(counts, 1).astype(jnp.float32))


VM = pl.BlockSpec(memory_space=pltpu.VMEM)
SM = pl.BlockSpec(memory_space=pltpu.SMEM)
LIMIT = pltpu.CompilerParams(vmem_limit_bytes=24 * 1024 * 1024)


def exchange(x, rows):
    x = x.reshape(DEV, rows, DEV)
    return lax.all_to_all(x, ("blk", "lag"), split_axis=0, concat_axis=0, tiled=True)


def on_device(raw, mask):
    device = lax.axis_index("blk") * lax.axis_size("lag") + lax.axis_index("lag")
    packed = pl.pallas_call(
        pack_kernel,
        out_shape=jax.ShapeDtypeStruct((DEV, BLK, DEV), BF),
        in_specs=[pl.BlockSpec(memory_space=pltpu.HBM)],
        out_specs=pl.BlockSpec(memory_space=pltpu.HBM),
        scratch_shapes=[
            pltpu.VMEM((ROWS, C), F32),
            pltpu.VMEM((BLK * DEV, DEV), F32),
            pltpu.VMEM((2, DEV, 8, DEV), BF),
            pltpu.SemaphoreType.DMA((2,)),
            pltpu.SemaphoreType.DMA((2,)),
        ],
    )(raw)
    series = exchange(packed, BLK).reshape(BLK * DEV, DEV)
    stage1, twiddle, stage2 = time_tables()
    white = pl.pallas_call(
        spectra_kernel,
        out_shape=jax.ShapeDtypeStruct((8 * DEV, DEV), BF),
        in_specs=[VM] * 6,
        out_specs=VM,
        compiler_params=LIMIT,
        scratch_shapes=[
            pltpu.VMEM((BLK * DEV, DEV), F32),
            pltpu.VMEM((4 * DEV, 8 * DEV), BF),
            pltpu.VMEM((8 * DEV, DEV), F32),
        ],
    )(series, stage1, twiddle, stage2, window_table(), taper_table())
    banded = exchange(white, 8).reshape(8 * DEV, DEV)
    odd = 2 * lax.iota(jnp.int32, LAGS) - (LAGS - 1)
    angle = jnp.mod(odd * first_bin(device), Q).astype(F32) * (2 * math.pi / Q)
    spread = lambda x: jnp.broadcast_to(x.reshape(4, 2, 1, 1), (4, 2, 4, DEV)).reshape(4, 8, DEV)
    rotation = jnp.stack([spread(jnp.cos(angle)), spread(jnp.sin(angle))])
    live = jnp.broadcast_to(mask.astype(F32).reshape(BLK * BLK, 1), (BLK * BLK, DEV))
    parts = pl.pallas_call(
        stack_kernel,
        out_shape=jax.ShapeDtypeStruct((4 * DEV, DEV), BF),
        in_specs=[VM] * 7,
        out_specs=VM,
        compiler_params=LIMIT,
        scratch_shapes=[
            pltpu.VMEM((8 * DEV, DEV), F32),
            pltpu.VMEM((2048, DEV), F32),
            pltpu.VMEM((2 * FAR, 8, DEV), F32),
            pltpu.VMEM((8 * DEV, DEV), F32),
        ],
    )(banded, live, rotation, *channel_table(), *offset_table())
    shares = exchange(parts, 4).reshape(4 * DEV, DEV)
    columns = device * 64 + lax.iota(jnp.int32, 64)
    scale = stack_scale(pair_counts(mask, columns))[None, :]
    place = (device < 64).astype(jnp.int32)[None]
    return pl.pallas_call(
        total_kernel,
        out_shape=jax.ShapeDtypeStruct((LAGS, 64), F32),
        in_specs=[VM, SM, VM],
        out_specs=VM,
        compiler_params=LIMIT,
    )(shares, place, scale)


def solution(mesh):
    return jax.shard_map(
        on_device,
        mesh=mesh,
        in_specs=(P(("blk", "lag"), None), P()),
        out_specs=P(None, ("blk", "lag")),
        check_vma=False,
    )
```

```python
import math

import jax
import jax.numpy as jnp
import numpy as np
from jax import lax
from jax.experimental import pallas as pl
from jax.experimental.pallas import tpu as pltpu
from jax.sharding import PartitionSpec as P

NT = 8192
C = 4096
NB = 2048
K0 = 16
SW = 32
TAPER = 128
LAGS = 8
LAG_STEP = 32
EPS = 1e-06

DEV = 128
ROWS = NT // DEV
BLK = 16
J2 = NB // DEV
Q = 512
FAR = 15

BF = jnp.bfloat16
F32 = jnp.float32


def split(x):
    hi = x.astype(BF)
    return hi, (x - hi.astype(F32)).astype(BF)


def np_split(x):
    hi = np.asarray(x, np.float32).astype(jnp.bfloat16)
    lo = (np.asarray(x, np.float64) - hi.astype(np.float64)).astype(jnp.bfloat16)
    return hi, lo


def cs(numer, period):
    angle = 2 * np.pi * np.mod(numer, period) / period
    return np.cos(angle), np.sin(angle)


def first_bins():
    n = np.arange(64)
    residue = np.concatenate([n, (DEV - n) % DEV])
    residue[64] = 64
    return np.where(residue < K0, residue + DEV, residue)


def first_bin(row):
    residue = jnp.where(row <= 64, row, 192 - row)
    return jnp.where(residue < K0, residue + DEV, residue)


def time_tables():
    n, p = np.arange(64), np.arange(DEV)
    c, s = cs(n[:, None] * p[None], DEV)
    stage1 = np.concatenate([c, -s], axis=0)
    stage1[64] = np.cos(np.pi * p)
    r = np.tile(np.arange(ROWS), 2)
    c, s = cs(first_bins()[:, None] * r[None], NT)
    mirror = np.where(np.arange(DEV) < 64, 1.0, -1.0)[:, None]
    twiddle = np.stack([c, mirror * s, mirror * c, s]).astype(np.float32)
    r, j2 = np.arange(ROWS), np.arange(J2)
    c, s = cs(r[:, None] * j2[None], ROWS)
    eye = np.eye(8)
    place = lambda t: np.einsum("ab,rj->arbj", eye, t).reshape(8 * ROWS, 8 * J2)
    stage2 = np.block([[place(c), place(-s)], [place(s), place(c)]])
    return stage1.astype(jnp.bfloat16), twiddle, stage2.astype(jnp.bfloat16)


AFTER, BEFORE = slice(16, 48), (slice(0, 16), slice(64, 96))


def window_table():
    bins = first_bins()
    gap = bins[:, None] - bins[None]
    near = lambda d: (np.abs(d) <= SW).astype(np.float32)
    after, before = near(gap - DEV), near(gap + DEV)
    return np.concatenate(
        [near(gap), after[:, AFTER]] + [before[:, rows] for rows in BEFORE], axis=1
    ).astype(jnp.bfloat16)


def taper_table():
    position = (first_bins() - K0)[:, None] + DEV * np.arange(J2)[None]
    edge = np.minimum(position, NB - 1 - position)
    curve = 0.5 - 0.5 * np.cos(math.pi * (edge + 0.5) / TAPER)
    return np.tile(np.where(edge < TAPER, curve, 1.0), (1, 2 * DEV // J2)).astype(np.float32)


def channel_table():
    c, s = cs(np.arange(256)[:, None] * (2 * np.arange(256) + 1)[None], 2 * Q)
    return np_split(np.concatenate([c, s], axis=1))


def offset_table():
    c, s = cs((2 * np.arange(256) + 1)[:, None] * np.arange(256)[None], 2 * Q)
    return np_split(np.concatenate([c, s], axis=0) / Q)


def pack_kernel(raw_ref, out_ref, raw_buf, buf_ref, out_buf, in_sems, out_sems):
    wide = C // 2
    takes = [
        pltpu.make_async_copy(
            raw_ref.at[:, pl.ds(k * wide, wide)], raw_buf.at[:, pl.ds(k * wide, wide)], in_sems.at[k]
        )
        for k in range(2)
    ]
    for take in takes:
        take.start()
    gives = []
    for k in range(2):
        takes[k].wait()
        for i in range(8):
            at = (8 * k + i) * 256
            rows = jnp.concatenate([raw_buf[:, at : at + DEV], raw_buf[:, at + DEV : at + 256]], axis=0)
            buf_ref[pl.ds(1024 * k + i, DEV, stride=8), :] = rows.T
        out_buf[k] = buf_ref[1024 * k : 1024 * (k + 1), :].reshape(DEV, 8, DEV).astype(BF)
        give = pltpu.make_async_copy(
            out_buf.at[k], out_ref.at[:, pl.ds(8 * k, 8), :], out_sems.at[k]
        )
        give.start()
        gives.append(give)
    for give in gives:
        give.wait()


def dot(a, b):
    return jnp.dot(a, b, preferred_element_type=F32)


def spectra_kernel(
    in_ref, s1_ref, tw_ref, s2_ref, win_ref, taper_ref, mask_ref, out_ref, live_ref,
    buf_ref, z_ref, white_ref,
):
    mask = mask_ref[...].astype(F32)
    for i in range(BLK):
        live_ref[i * BLK : (i + 1) * BLK, :] = jnp.broadcast_to(mask[:, i : i + 1], (BLK, DEV))
    series = in_ref[...].astype(F32).reshape(DEV, 2, 8, DEV)
    for k in range(2):
        buf_ref[1024 * k : 1024 * (k + 1), :] = series[:, k].reshape(1024, DEV)
    top_row = lax.broadcasted_iota(jnp.int32, (8, DEV), 0) == 0
    lane = lax.broadcasted_iota(jnp.int32, (1, DEV), 1) % J2

    def turn(g, w=0):
        rows = [
            buf_ref[pl.ds(1024 * (g // 2) + (4 * g + s) % 8, DEV, stride=8), :]
            for s in range(4)
        ]
        y = dot(s1_ref[...], jnp.concatenate(rows, axis=1).astype(BF))
        for s in range(4):
            re, im = y[:64, s * DEV : (s + 1) * DEV], y[64:, s * DEV : (s + 1) * DEV]
            no_im = jnp.concatenate([jnp.where(top_row, 0.0, im[:8]), im[8:]], axis=0)
            re_64 = jnp.concatenate([jnp.where(top_row, im[:8], re[:8]), re[8:]], axis=0)
            for half, real in enumerate((re, re_64)):
                at = slice(half * 64, half * 64 + 64)
                to = slice(g * DEV + half * 64, g * DEV + half * 64 + 64)
                col = s
                z_ref[to, col * DEV : (col + 1) * DEV] = (
                    real * tw_ref[0, at] + no_im * tw_ref[1, at]
                ).astype(BF)
                z_ref[to, (4 + col) * DEV : (5 + col) * DEV] = (
                    no_im * tw_ref[2, at] - real * tw_ref[3, at]
                ).astype(BF)

    def shifted(x, by, edge):
        tiles = [pltpu.roll(x[:, s * DEV : (s + 1) * DEV], by, 1) for s in range(2)]
        return jnp.concatenate([jnp.where(lane == edge, 0.0, t) for t in tiles], axis=1)

    def whiten(h, spec):
        re, im = (
            jnp.concatenate([spec[:DEV, at : at + DEV], spec[DEV:, at : at + DEV]], axis=1)
            for at in (0, DEV)
        )
        power = re * re + im * im
        amp = power * lax.rsqrt(jnp.maximum(power, 1e-30))
        near = [amp, shifted(amp[AFTER], DEV - 1, J2 - 1)]
        near += [shifted(amp[rows], 1, 0) for rows in BEFORE]
        total = dot(win_ref[...], jnp.concatenate(near, axis=0).astype(BF))
        gain = taper_ref[...] / (total * (1.0 / (2 * SW + 1)) + EPS)
        for part, value in enumerate((re * gain, im * gain)):
            for s in range(2):
                white_ref[pl.ds(4 * part + 2 * h + s, DEV, stride=8), :] = value[
                    :, s * DEV : (s + 1) * DEV
                ]

    for g in range(4):
        turn(g)
    spec = dot(z_ref[...], s2_ref[...])
    for h in range(2):
        whiten(h, spec[2 * h * DEV : 2 * (h + 1) * DEV])
    out_ref[...] = white_ref[...].astype(BF)


def stack_kernel(
    in_ref, mask_ref, rot_ref, eh_ref, el_ref, dh_ref, dl_ref, out_ref,
    buf_ref, f_ref, acc_ref, v_ref,
):
    buf_ref[...] = in_ref[...].astype(F32)
    pieces = [buf_ref[pl.ds(t, DEV, stride=8), :].T.astype(BF) for t in range(8)]
    rows = []
    for part in range(2):
        for i in range(BLK):
            g, s = i // 4, i % 4
            tiles = [
                pieces[4 * part + g][(2 * s + h) * J2 : (2 * s + h + 1) * J2] for h in range(2)
            ]
            rows.append(jnp.concatenate(tiles, axis=1))
    white = jnp.concatenate(rows, axis=0)
    product = dot(white, eh_ref[...]) + dot(white, el_ref[...])
    half = BLK * J2
    for t in range(2):
        at = slice(t * DEV, (t + 1) * DEV)
        to = slice(256 + t * DEV, 256 + (t + 1) * DEV)
        rc, rs, ic, ims = product[:half, at], product[:half, to], product[half:, at], product[half:, to]
        for part, sign, value in (
            (0, 0, rc + ims), (0, 1, rc - ims), (1, 0, ic - rs), (1, 1, ic + rs)
        ):
            for k in range(2 * BLK):
                f_ref[pl.ds(part * 1024 + 32 * k + 2 * sign + t, 8, stride=4), :] = value[
                    8 * k : 8 * k + 8
                ]
    acc_ref[...] = jnp.zeros_like(acc_ref)

    def unit(u, carry):
        at = lambda i, part: pl.ds(pl.multiple_of(part * 1024 + i * 64 + u * 8, 8), 8)
        re = [f_ref[at(i, 0), :] for i in range(BLK)]
        im = [f_ref[at(i, 1), :] for i in range(BLK)]
        both = [re[i] + im[i] for i in range(BLK)]
        less = [re[i] - im[i] for i in range(BLK)]
        for delta in range(FAR):
            sums = [None, None, None]
            for i in range(BLK - delta):
                j = i + delta
                live = mask_ref[pl.ds(i * BLK + j, 8, stride=0), :]
                a_re, a_im = re[i] * live, im[i] * live
                if delta == 0:
                    terms = [a_re * re[j] + a_im * im[j]]
                else:
                    terms = [(a_re + a_im) * re[j], a_im * less[j], a_re * both[j]]
                sums = [t if s is None else s + t for s, t in zip(sums, terms)]
            if delta == 0:
                acc_ref[0] = sums[0] - acc_ref[0]
            else:
                acc_ref[2 * delta] = sums[0] - sums[1] - acc_ref[2 * delta]
                acc_ref[2 * delta + 1] = sums[0] - sums[2] - acc_ref[2 * delta + 1]
        return carry

    lax.fori_loop(0, J2 // 2, unit, 0, unroll=2)
    first = lax.broadcasted_iota(jnp.int32, (8, DEV), 0) < 4
    lane = lax.broadcasted_iota(jnp.int32, (8, DEV), 1)
    row = lax.broadcasted_iota(jnp.int32, (8, DEV), 0)
    beside = jnp.where((lane % 2 == 1) == (row % 4 < 2), -1.0, 1.0)
    turn = jnp.where(first, -1.0, 1.0)
    for delta in range(BLK):
        if delta < FAR:
            x_re, x_im = acc_ref[2 * delta], acc_ref[2 * delta + 1]
            if delta + 1 < FAR:
                x_re = x_re - beside * acc_ref[2 * delta + 3]
                x_im = x_im + beside * acc_ref[2 * delta + 2]
            s_re, s_im = pltpu.roll(x_re, 4, 0), pltpu.roll(x_im, 4, 0)
            g_re = jnp.where(first, x_re, s_re) + turn * jnp.where(first, s_im, x_im)
            g_im = jnp.where(first, x_im, s_im) - turn * jnp.where(first, s_re, x_re)
        for u in range(4):
            at = pl.ds((delta * 4 + u) * 8, 8)
            to = pl.ds(512 + (delta * 4 + u) * 8, 8)
            if delta < FAR:
                c, s = rot_ref[0, u], rot_ref[1, u]
                v_ref[at, :] = s * g_im - c * g_re
                v_ref[to, :] = -(c * g_im) - s * g_re
            else:
                v_ref[at, :] = jnp.zeros((8, DEV), F32)
                v_ref[to, :] = jnp.zeros((8, DEV), F32)
    load = lambda c, t: v_ref[pl.ds(512 * c + t, DEV, stride=4), :]
    folded = [load(0, 0) + load(0, 2), load(0, 1) + load(0, 3)]
    folded += [load(1, 0) - load(1, 2), load(1, 1) - load(1, 3)]
    v_hi, v_lo = split(jnp.concatenate(folded, axis=1))
    fine = dot(jnp.concatenate([v_hi, v_lo], axis=0), dh_ref[...])
    stacked = fine[:DEV] + fine[DEV:] + dot(v_hi, dl_ref[...])
    left, right = stacked[:, :DEV], stacked[:, DEV:]
    last = lax.broadcasted_iota(jnp.int32, (DEV, DEV), 1) == DEV - 1
    left1, right1 = pltpu.roll(left, DEV - 1, 1), pltpu.roll(right, DEV - 1, 1)
    beyond = jnp.concatenate([left1[8:], jnp.zeros((8, DEV), F32)], axis=0)
    behind = (jnp.where(last, right1, left1), jnp.where(last, beyond, right1))
    same = first == (lane < 64)
    for delta in range(BLK):
        for t in range(2):
            tile = (left, right)[t][8 * delta : 8 * delta + 8]
            pair = jnp.where(same, tile, pltpu.roll(pltpu.roll(tile, 4, 0), 64, 1))
            at = 4 * (64 + 4 * delta + 2 * t)
            out_ref[at : at + 8, :] = pair.astype(BF)
            tile = behind[t][8 * delta : 8 * delta + 8]
            pair = jnp.where(same, pltpu.roll(tile, 64, 1), pltpu.roll(tile, 4, 0))
            at = 4 * (4 * (BLK - 1 - delta) + 2 - 2 * t)
            out_ref[at : at + 8, :] = pair.astype(BF)


def total_kernel(in_ref, place_ref, scale_ref, out_ref):
    total = jnp.sum(in_ref[...].astype(F32).reshape(DEV // 2, 8, DEV), axis=0)
    total = total + pltpu.roll(total, 4, 0)
    low = lax.broadcasted_iota(jnp.int32, (8, DEV), 0) < 4
    lags = jnp.where(low, total, pltpu.roll(total, 64, 1))
    lane = lax.broadcasted_iota(jnp.int32, (8, DEV), 1)
    flipped = jnp.concatenate([lags[7 - j : 8 - j] for j in range(LAGS)], axis=0)
    flipped = jnp.take_along_axis(flipped, (63 - lane) & 127, axis=1)
    out = jnp.where(place_ref[0] == 1, flipped, lags)
    out_ref[...] = out[:, :64] * scale_ref[...]


def pair_counts(mask, columns):
    blocks = mask.shape[0]
    width = C // blocks
    labels = lax.iota(jnp.int32, blocks)
    apart = labels[None, :] - labels[:, None]
    deltas = lax.iota(jnp.int32, 2 * blocks - 1) - (blocks - 1)
    per_delta = jnp.sum(
        mask[None] * (apart[None] == deltas[:, None, None]).astype(jnp.int32), axis=(1, 2)
    )
    offsets = columns - C
    intersection = jnp.maximum(0, width - jnp.abs(offsets[:, None] - width * deltas[None, :]))
    return jnp.sum(intersection * per_delta[None, :], axis=1)


def stack_scale(counts):
    return 1.0 / jnp.sqrt(NB * jnp.maximum(counts, 1).astype(jnp.float32))


VM = pl.BlockSpec(memory_space=pltpu.VMEM)
SM = pl.BlockSpec(memory_space=pltpu.SMEM)
LIMIT = pltpu.CompilerParams(vmem_limit_bytes=24 * 1024 * 1024)


def exchange(x, rows):
    x = x.reshape(DEV, rows, DEV)
    return lax.all_to_all(x, ("blk", "lag"), split_axis=0, concat_axis=0, tiled=True)


def on_device(raw, mask):
    device = lax.axis_index("blk") * lax.axis_size("lag") + lax.axis_index("lag")
    packed = pl.pallas_call(
        pack_kernel,
        out_shape=jax.ShapeDtypeStruct((DEV, BLK, DEV), BF),
        in_specs=[pl.BlockSpec(memory_space=pltpu.HBM)],
        out_specs=pl.BlockSpec(memory_space=pltpu.HBM),
        scratch_shapes=[
            pltpu.VMEM((ROWS, C), F32),
            pltpu.VMEM((BLK * DEV, DEV), F32),
            pltpu.VMEM((2, DEV, 8, DEV), BF),
            pltpu.SemaphoreType.DMA((2,)),
            pltpu.SemaphoreType.DMA((2,)),
        ],
    )(raw)
    series = exchange(packed, BLK).reshape(BLK * DEV, DEV)
    stage1, twiddle, stage2 = time_tables()
    white, live = pl.pallas_call(
        spectra_kernel,
        out_shape=(
            jax.ShapeDtypeStruct((8 * DEV, DEV), BF),
            jax.ShapeDtypeStruct((BLK * BLK, DEV), F32),
        ),
        in_specs=[VM] * 7,
        out_specs=(VM, VM),
        compiler_params=LIMIT,
        scratch_shapes=[
            pltpu.VMEM((BLK * DEV, DEV), F32),
            pltpu.VMEM((4 * DEV, 8 * DEV), BF),
            pltpu.VMEM((8 * DEV, DEV), F32),
        ],
    )(series, stage1, twiddle, stage2, window_table(), taper_table(), mask)
    banded = exchange(white, 8).reshape(8 * DEV, DEV)
    odd = 2 * lax.iota(jnp.int32, LAGS) - (LAGS - 1)
    angle = jnp.mod(odd * first_bin(device), Q).astype(F32) * (2 * math.pi / Q)
    spread = lambda x: jnp.broadcast_to(x.reshape(4, 2, 1, 1), (4, 2, 4, DEV)).reshape(4, 8, DEV)
    rotation = jnp.stack([spread(jnp.cos(angle)), spread(jnp.sin(angle))])
    parts = pl.pallas_call(
        stack_kernel,
        out_shape=jax.ShapeDtypeStruct((4 * DEV, DEV), BF),
        in_specs=[VM] * 7,
        out_specs=VM,
        compiler_params=LIMIT,
        scratch_shapes=[
            pltpu.VMEM((8 * DEV, DEV), F32),
            pltpu.VMEM((2048, DEV), F32),
            pltpu.VMEM((2 * FAR, 8, DEV), F32),
            pltpu.VMEM((8 * DEV, DEV), F32),
        ],
    )(banded, live, rotation, *channel_table(), *offset_table())
    shares = exchange(parts, 4).reshape(4 * DEV, DEV)
    columns = device * 64 + lax.iota(jnp.int32, 64)
    scale = stack_scale(pair_counts(mask, columns))[None, :]
    place = (device < 64).astype(jnp.int32)[None]
    return pl.pallas_call(
        total_kernel,
        out_shape=jax.ShapeDtypeStruct((LAGS, 64), F32),
        in_specs=[VM, SM, VM],
        out_specs=VM,
        compiler_params=LIMIT,
    )(shares, place, scale)


def solution(mesh):
    return jax.shard_map(
        on_device,
        mesh=mesh,
        in_specs=(P(("blk", "lag"), None), P()),
        out_specs=P(None, ("blk", "lag")),
        check_vma=False,
    )
```

```python
import math

import jax
import jax.numpy as jnp
import numpy as np
from jax import lax
from jax.experimental import pallas as pl
from jax.experimental.pallas import tpu as pltpu
from jax.sharding import PartitionSpec as P

NT = 8192
C = 4096
NB = 2048
K0 = 16
SW = 32
TAPER = 128
LAGS = 8
LAG_STEP = 32
EPS = 1e-06

DEV = 128
ROWS = NT // DEV
BLK = 16
J2 = NB // DEV
Q = 512
FAR = 15

BF = jnp.bfloat16
F32 = jnp.float32


def split(x):
    hi = x.astype(BF)
    return hi, (x - hi.astype(F32)).astype(BF)


def np_split(x):
    hi = np.asarray(x, np.float32).astype(jnp.bfloat16)
    lo = (np.asarray(x, np.float64) - hi.astype(np.float64)).astype(jnp.bfloat16)
    return hi, lo


def cs(numer, period):
    angle = 2 * np.pi * np.mod(numer, period) / period
    return np.cos(angle), np.sin(angle)


def first_bins():
    n = np.arange(64)
    residue = np.concatenate([n, (DEV - n) % DEV])
    residue[64] = 64
    return np.where(residue < K0, residue + DEV, residue)


def first_bin(row):
    residue = jnp.where(row <= 64, row, 192 - row)
    return jnp.where(residue < K0, residue + DEV, residue)


def time_tables():
    n, p = np.arange(64), np.arange(DEV)
    c, s = cs(n[:, None] * p[None], DEV)
    stage1 = np.concatenate([c, -s], axis=0)
    stage1[64] = np.cos(np.pi * p)
    r = np.tile(np.arange(ROWS), 2)
    c, s = cs(first_bins()[:, None] * r[None], NT)
    mirror = np.where(np.arange(DEV) < 64, 1.0, -1.0)[:, None]
    twiddle = np.stack([c, mirror * s, mirror * c, s]).astype(np.float32)
    r, j2 = np.arange(ROWS), np.arange(J2)
    c, s = cs(r[:, None] * j2[None], ROWS)
    eye = np.eye(8)
    place = lambda t: np.einsum("ab,rj->arbj", eye, t).reshape(8 * ROWS, 8 * J2)
    stage2 = np.block([[place(c), place(-s)], [place(s), place(c)]])
    return stage1.astype(jnp.bfloat16), twiddle, stage2.astype(jnp.bfloat16)


AFTER, BEFORE = slice(16, 48), (slice(0, 16), slice(64, 96))


def window_table():
    bins = first_bins()
    gap = bins[:, None] - bins[None]
    near = lambda d: (np.abs(d) <= SW).astype(np.float32)
    after, before = near(gap - DEV), near(gap + DEV)
    return np.concatenate(
        [near(gap), after[:, AFTER]] + [before[:, rows] for rows in BEFORE], axis=1
    ).astype(jnp.bfloat16)


def taper_table():
    position = (first_bins() - K0)[:, None] + DEV * np.arange(J2)[None]
    edge = np.minimum(position, NB - 1 - position)
    curve = 0.5 - 0.5 * np.cos(math.pi * (edge + 0.5) / TAPER)
    return np.tile(np.where(edge < TAPER, curve, 1.0), (1, 2 * DEV // J2)).astype(np.float32)


def channel_table():
    c, s = cs(np.arange(256)[:, None] * (2 * np.arange(256) + 1)[None], 2 * Q)
    return np_split(np.concatenate([c, s], axis=1))


def offset_table():
    c, s = cs((2 * np.arange(256) + 1)[:, None] * np.arange(256)[None], 2 * Q)
    return np_split(np.concatenate([c, s], axis=0) / Q)


def pack_kernel(raw_ref, out_ref, raw_buf, buf_ref, out_buf, in_sems, out_sems):
    wide = C // 2
    takes = [
        pltpu.make_async_copy(
            raw_ref.at[:, pl.ds(k * wide, wide)], raw_buf.at[:, pl.ds(k * wide, wide)], in_sems.at[k]
        )
        for k in range(2)
    ]
    for take in takes:
        take.start()
    gives = []
    for k in range(2):
        takes[k].wait()
        for i in range(8):
            at = (8 * k + i) * 256
            rows = jnp.concatenate([raw_buf[:, at : at + DEV], raw_buf[:, at + DEV : at + 256]], axis=0)
            buf_ref[pl.ds(1024 * k + i, DEV, stride=8), :] = rows.T
        out_buf[k] = buf_ref[1024 * k : 1024 * (k + 1), :].reshape(DEV, 8, DEV).astype(BF)
        give = pltpu.make_async_copy(
            out_buf.at[k], out_ref.at[:, pl.ds(8 * k, 8), :], out_sems.at[k]
        )
        give.start()
        gives.append(give)
    for give in gives:
        give.wait()


def dot(a, b):
    return jnp.dot(a, b, preferred_element_type=F32)


def spectra_kernel(
    in_ref, s1_ref, tw_ref, s2_ref, win_ref, taper_ref, mask_ref, out_ref, live_ref,
    buf_ref, z_ref, white_ref,
):
    mask = mask_ref[...].astype(F32)
    for i in range(BLK):
        live_ref[i * BLK : (i + 1) * BLK, :] = jnp.broadcast_to(mask[:, i : i + 1], (BLK, DEV))
    series = in_ref[...].astype(F32).reshape(DEV, 2, 8, DEV)
    for k in range(2):
        buf_ref[1024 * k : 1024 * (k + 1), :] = series[:, k].reshape(1024, DEV)
    top_row = lax.broadcasted_iota(jnp.int32, (8, DEV), 0) == 0
    lane = lax.broadcasted_iota(jnp.int32, (1, DEV), 1) % J2

    def turn(g, w=0):
        rows = [
            buf_ref[pl.ds(1024 * (g // 2) + (4 * g + s) % 8, DEV, stride=8), :]
            for s in range(4)
        ]
        y = dot(s1_ref[...], jnp.concatenate(rows, axis=1).astype(BF))
        for s in range(4):
            re, im = y[:64, s * DEV : (s + 1) * DEV], y[64:, s * DEV : (s + 1) * DEV]
            no_im = jnp.concatenate([jnp.where(top_row, 0.0, im[:8]), im[8:]], axis=0)
            re_64 = jnp.concatenate([jnp.where(top_row, im[:8], re[:8]), re[8:]], axis=0)
            for half, real in enumerate((re, re_64)):
                at = slice(half * 64, half * 64 + 64)
                to = slice(g * DEV + half * 64, g * DEV + half * 64 + 64)
                col = s
                z_ref[to, col * DEV : (col + 1) * DEV] = (
                    real * tw_ref[0, at] + no_im * tw_ref[1, at]
                ).astype(BF)
                z_ref[to, (4 + col) * DEV : (5 + col) * DEV] = (
                    no_im * tw_ref[2, at] - real * tw_ref[3, at]
                ).astype(BF)

    def shifted(x, by, edge):
        tiles = [pltpu.roll(x[:, s * DEV : (s + 1) * DEV], by, 1) for s in range(2)]
        return jnp.concatenate([jnp.where(lane == edge, 0.0, t) for t in tiles], axis=1)

    def whiten(h, spec):
        re, im = (
            jnp.concatenate([spec[:DEV, at : at + DEV], spec[DEV:, at : at + DEV]], axis=1)
            for at in (0, DEV)
        )
        power = re * re + im * im
        amp = power * lax.rsqrt(jnp.maximum(power, 1e-30))
        near = [amp, shifted(amp[AFTER], DEV - 1, J2 - 1)]
        near += [shifted(amp[rows], 1, 0) for rows in BEFORE]
        total = dot(win_ref[...], jnp.concatenate(near, axis=0).astype(BF))
        gain = taper_ref[...] / (total * (1.0 / (2 * SW + 1)) + EPS)
        for part, value in enumerate((re * gain, im * gain)):
            for s in range(2):
                white_ref[pl.ds(4 * part + 2 * h + s, DEV, stride=8), :] = value[
                    :, s * DEV : (s + 1) * DEV
                ]

    for g in range(4):
        turn(g)
    spec = dot(z_ref[...], s2_ref[...])
    for h in range(2):
        whiten(h, spec[2 * h * DEV : 2 * (h + 1) * DEV])
    out_ref[...] = white_ref[...].astype(BF)


def stack_kernel(
    in_ref, mask_ref, rot_ref, eh_ref, el_ref, dh_ref, dl_ref, out_ref,
    buf_ref, f_ref, acc_ref, v_ref,
):
    buf_ref[...] = in_ref[...].astype(F32)
    pieces = [buf_ref[pl.ds(t, DEV, stride=8), :].T.astype(BF) for t in range(8)]
    rows = []
    for part in range(2):
        for i in range(BLK):
            g, s = i // 4, i % 4
            tiles = [
                pieces[4 * part + g][(2 * s + h) * J2 : (2 * s + h + 1) * J2] for h in range(2)
            ]
            rows.append(jnp.concatenate(tiles, axis=1))
    white = jnp.concatenate(rows, axis=0)
    product = dot(white, eh_ref[...]) + dot(white, el_ref[...])
    half = BLK * J2
    for t in range(2):
        at = slice(t * DEV, (t + 1) * DEV)
        to = slice(256 + t * DEV, 256 + (t + 1) * DEV)
        rc, rs, ic, ims = product[:half, at], product[:half, to], product[half:, at], product[half:, to]
        for part, sign, value in (
            (0, 0, rc + ims), (0, 1, rc - ims), (1, 0, ic - rs), (1, 1, ic + rs)
        ):
            for k in range(2 * BLK):
                f_ref[pl.ds(part * 1024 + 32 * k + 2 * sign + t, 8, stride=4), :] = value[
                    8 * k : 8 * k + 8
                ]
    acc_ref[...] = jnp.zeros_like(acc_ref)

    def unit(u, carry):
        at = lambda i, part: pl.ds(pl.multiple_of(part * 1024 + i * 64 + u * 8, 8), 8)
        re = [f_ref[at(i, 0), :] for i in range(BLK)]
        im = [f_ref[at(i, 1), :] for i in range(BLK)]
        both = [re[i] + im[i] for i in range(BLK)]
        less = [re[i] - im[i] for i in range(BLK)]
        for delta in range(FAR):
            sums = [None, None, None]
            for i in range(BLK - delta):
                j = i + delta
                live = mask_ref[pl.ds(i * BLK + j, 8, stride=0), :]
                a_re, a_im = re[i] * live, im[i] * live
                if delta == 0:
                    terms = [a_re * re[j] + a_im * im[j]]
                else:
                    terms = [(a_re + a_im) * re[j], a_im * less[j], a_re * both[j]]
                sums = [t if s is None else s + t for s, t in zip(sums, terms)]
            if delta == 0:
                acc_ref[0] = sums[0] - acc_ref[0]
            else:
                acc_ref[2 * delta] = sums[0] - sums[1] - acc_ref[2 * delta]
                acc_ref[2 * delta + 1] = sums[0] - sums[2] - acc_ref[2 * delta + 1]
        return carry

    lax.fori_loop(0, J2 // 2, unit, 0, unroll=2)
    first = lax.broadcasted_iota(jnp.int32, (8, DEV), 0) < 4
    lane = lax.broadcasted_iota(jnp.int32, (8, DEV), 1)
    row = lax.broadcasted_iota(jnp.int32, (8, DEV), 0)
    beside = jnp.where((lane % 2 == 1) == (row % 4 < 2), -1.0, 1.0)
    turn = jnp.where(first, -1.0, 1.0)
    for delta in range(BLK):
        if delta < FAR:
            x_re, x_im = acc_ref[2 * delta], acc_ref[2 * delta + 1]
            if delta + 1 < FAR:
                x_re = x_re - beside * acc_ref[2 * delta + 3]
                x_im = x_im + beside * acc_ref[2 * delta + 2]
            s_re, s_im = pltpu.roll(x_re, 4, 0), pltpu.roll(x_im, 4, 0)
            g_re = jnp.where(first, x_re, s_re) + turn * jnp.where(first, s_im, x_im)
            g_im = jnp.where(first, x_im, s_im) - turn * jnp.where(first, s_re, x_re)
        for u in range(4):
            at = pl.ds((delta * 4 + u) * 8, 8)
            to = pl.ds(512 + (delta * 4 + u) * 8, 8)
            if delta < FAR:
                c, s = rot_ref[0, u], rot_ref[1, u]
                v_ref[at, :] = s * g_im - c * g_re
                v_ref[to, :] = -(c * g_im) - s * g_re
            else:
                v_ref[at, :] = jnp.zeros((8, DEV), F32)
                v_ref[to, :] = jnp.zeros((8, DEV), F32)
    load = lambda c, t: v_ref[pl.ds(512 * c + t, DEV, stride=4), :]
    folded = [load(0, 0) + load(0, 2), load(0, 1) + load(0, 3)]
    folded += [load(1, 0) - load(1, 2), load(1, 1) - load(1, 3)]
    v_hi, v_lo = split(jnp.concatenate(folded, axis=1))
    fine = dot(jnp.concatenate([v_hi, v_lo], axis=0), dh_ref[...])
    stacked = fine[:DEV] + fine[DEV:] + dot(v_hi, dl_ref[...])
    left, right = stacked[:, :DEV], stacked[:, DEV:]
    last = lax.broadcasted_iota(jnp.int32, (DEV, DEV), 1) == DEV - 1
    left1, right1 = pltpu.roll(left, DEV - 1, 1), pltpu.roll(right, DEV - 1, 1)
    beyond = jnp.concatenate([left1[8:], jnp.zeros((8, DEV), F32)], axis=0)
    behind = (jnp.where(last, right1, left1), jnp.where(last, beyond, right1))
    same = first == (lane < 64)
    for delta in range(BLK):
        for t in range(2):
            tile = (left, right)[t][8 * delta : 8 * delta + 8]
            pair = jnp.where(same, tile, pltpu.roll(pltpu.roll(tile, 4, 0), 64, 1))
            at = 4 * (64 + 4 * delta + 2 * t)
            out_ref[at : at + 8, :] = pair.astype(BF)
            tile = behind[t][8 * delta : 8 * delta + 8]
            pair = jnp.where(same, pltpu.roll(tile, 64, 1), pltpu.roll(tile, 4, 0))
            at = 4 * (4 * (BLK - 1 - delta) + 2 - 2 * t)
            out_ref[at : at + 8, :] = pair.astype(BF)


def total_kernel(in_ref, scale_ref, out_ref):
    total = jnp.sum(in_ref[...].astype(F32).reshape(DEV // 2, 8, DEV), axis=0)
    total = total + pltpu.roll(total, 4, 0)
    low = lax.broadcasted_iota(jnp.int32, (8, DEV), 0) < 4
    lags = jnp.where(low, total, pltpu.roll(total, 64, 1))
    lane = lax.broadcasted_iota(jnp.int32, (8, DEV), 1)
    flipped = jnp.concatenate([lags[7 - j : 8 - j] for j in range(LAGS)], axis=0)
    flipped = jnp.take_along_axis(flipped, (63 - lane) & 127, axis=1)
    ahead, mirrored = scale_ref[0:1, :], scale_ref[1:2, :]
    out_ref[...] = jnp.where(
        mirrored > 0.0, flipped[:, :64] * mirrored, lags[:, :64] * ahead
    )


def pair_counts(mask, columns):
    blocks = mask.shape[0]
    width = C // blocks
    labels = lax.iota(jnp.int32, blocks)
    apart = labels[None, :] - labels[:, None]
    deltas = lax.iota(jnp.int32, 2 * blocks - 1) - (blocks - 1)
    per_delta = jnp.sum(
        mask[None] * (apart[None] == deltas[:, None, None]).astype(jnp.int32), axis=(1, 2)
    )
    offsets = columns - C
    intersection = jnp.maximum(0, width - jnp.abs(offsets[:, None] - width * deltas[None, :]))
    return jnp.sum(intersection * per_delta[None, :], axis=1)


def stack_scale(counts):
    return 1.0 / jnp.sqrt(NB * jnp.maximum(counts, 1).astype(jnp.float32))


VM = pl.BlockSpec(memory_space=pltpu.VMEM)
SM = pl.BlockSpec(memory_space=pltpu.SMEM)
LIMIT = pltpu.CompilerParams(vmem_limit_bytes=24 * 1024 * 1024)


def exchange(x, rows):
    x = x.reshape(DEV, rows, DEV)
    return lax.all_to_all(x, ("blk", "lag"), split_axis=0, concat_axis=0, tiled=True)


def on_device(raw, mask):
    device = lax.axis_index("blk") * lax.axis_size("lag") + lax.axis_index("lag")
    packed = pl.pallas_call(
        pack_kernel,
        out_shape=jax.ShapeDtypeStruct((DEV, BLK, DEV), BF),
        in_specs=[pl.BlockSpec(memory_space=pltpu.HBM)],
        out_specs=pl.BlockSpec(memory_space=pltpu.HBM),
        scratch_shapes=[
            pltpu.VMEM((ROWS, C), F32),
            pltpu.VMEM((BLK * DEV, DEV), F32),
            pltpu.VMEM((2, DEV, 8, DEV), BF),
            pltpu.SemaphoreType.DMA((2,)),
            pltpu.SemaphoreType.DMA((2,)),
        ],
    )(raw)
    series = exchange(packed, BLK).reshape(BLK * DEV, DEV)
    stage1, twiddle, stage2 = time_tables()
    white, live = pl.pallas_call(
        spectra_kernel,
        out_shape=(
            jax.ShapeDtypeStruct((8 * DEV, DEV), BF),
            jax.ShapeDtypeStruct((BLK * BLK, DEV), F32),
        ),
        in_specs=[VM] * 7,
        out_specs=(VM, VM),
        compiler_params=LIMIT,
        scratch_shapes=[
            pltpu.VMEM((BLK * DEV, DEV), F32),
            pltpu.VMEM((4 * DEV, 8 * DEV), BF),
            pltpu.VMEM((8 * DEV, DEV), F32),
        ],
    )(series, stage1, twiddle, stage2, window_table(), taper_table(), mask)
    banded = exchange(white, 8).reshape(8 * DEV, DEV)
    odd = 2 * lax.iota(jnp.int32, LAGS) - (LAGS - 1)
    angle = jnp.mod(odd * first_bin(device), Q).astype(F32) * (2 * math.pi / Q)
    spread = lambda x: jnp.broadcast_to(x.reshape(4, 2, 1, 1), (4, 2, 4, DEV)).reshape(4, 8, DEV)
    rotation = jnp.stack([spread(jnp.cos(angle)), spread(jnp.sin(angle))])
    parts = pl.pallas_call(
        stack_kernel,
        out_shape=jax.ShapeDtypeStruct((4 * DEV, DEV), BF),
        in_specs=[VM] * 7,
        out_specs=VM,
        compiler_params=LIMIT,
        scratch_shapes=[
            pltpu.VMEM((8 * DEV, DEV), F32),
            pltpu.VMEM((2048, DEV), F32),
            pltpu.VMEM((2 * FAR, 8, DEV), F32),
            pltpu.VMEM((8 * DEV, DEV), F32),
        ],
    )(banded, live, rotation, *channel_table(), *offset_table())
    shares = exchange(parts, 4).reshape(4 * DEV, DEV)
    columns = device * 64 + lax.iota(jnp.int32, 64)
    scale = stack_scale(pair_counts(mask, columns))
    scales = jnp.stack([scale, jnp.where(device < 64, scale, 0.0)])
    return pl.pallas_call(
        total_kernel,
        out_shape=jax.ShapeDtypeStruct((LAGS, 64), F32),
        in_specs=[VM, VM],
        out_specs=VM,
        compiler_params=LIMIT,
    )(shares, scales)


def solution(mesh):
    return jax.shard_map(
        on_device,
        mesh=mesh,
        in_specs=(P(("blk", "lag"), None), P()),
        out_specs=P(None, ("blk", "lag")),
        check_vma=False,
    )
```

```python
import math

import jax
import jax.numpy as jnp
import numpy as np
from jax import lax
from jax.experimental import pallas as pl
from jax.experimental.pallas import tpu as pltpu
from jax.sharding import PartitionSpec as P

NT = 8192
C = 4096
NB = 2048
K0 = 16
SW = 32
TAPER = 128
LAGS = 8
LAG_STEP = 32
EPS = 1e-06

DEV = 128
ROWS = NT // DEV
BLK = 16
J2 = NB // DEV
Q = 512
FAR = 15

BF = jnp.bfloat16
F32 = jnp.float32


def split(x):
    hi = x.astype(BF)
    return hi, (x - hi.astype(F32)).astype(BF)


def np_split(x):
    hi = np.asarray(x, np.float32).astype(jnp.bfloat16)
    lo = (np.asarray(x, np.float64) - hi.astype(np.float64)).astype(jnp.bfloat16)
    return hi, lo


def cs(numer, period):
    angle = 2 * np.pi * np.mod(numer, period) / period
    return np.cos(angle), np.sin(angle)


def first_bins():
    n = np.arange(64)
    residue = np.concatenate([n, (DEV - n) % DEV])
    residue[64] = 64
    return np.where(residue < K0, residue + DEV, residue)


def first_bin(row):
    residue = jnp.where(row <= 64, row, 192 - row)
    return jnp.where(residue < K0, residue + DEV, residue)


def time_tables():
    n, p = np.arange(64), np.arange(DEV)
    c, s = cs(n[:, None] * p[None], DEV)
    stage1 = np.concatenate([c, -s], axis=0)
    stage1[64] = np.cos(np.pi * p)
    r = np.tile(np.arange(ROWS), 2)
    c, s = cs(first_bins()[:, None] * r[None], NT)
    mirror = np.where(np.arange(DEV) < 64, 1.0, -1.0)[:, None]
    twiddle = np.stack([c, mirror * s, mirror * c, s]).astype(np.float32)
    r, j2 = np.arange(ROWS), np.arange(J2)
    c, s = cs(r[:, None] * j2[None], ROWS)
    eye = np.eye(8)
    place = lambda t: np.einsum("ab,rj->arbj", eye, t).reshape(8 * ROWS, 8 * J2)
    stage2 = np.block([[place(c), place(-s)], [place(s), place(c)]])
    return stage1.astype(jnp.bfloat16), twiddle, stage2.astype(jnp.bfloat16)


AFTER, BEFORE = slice(16, 48), (slice(0, 16), slice(64, 96))


def window_table():
    bins = first_bins()
    gap = bins[:, None] - bins[None]
    near = lambda d: (np.abs(d) <= SW).astype(np.float32)
    after, before = near(gap - DEV), near(gap + DEV)
    return np.concatenate(
        [near(gap), after[:, AFTER]] + [before[:, rows] for rows in BEFORE], axis=1
    ).astype(jnp.bfloat16)


def taper_table():
    position = (first_bins() - K0)[:, None] + DEV * np.arange(J2)[None]
    edge = np.minimum(position, NB - 1 - position)
    curve = 0.5 - 0.5 * np.cos(math.pi * (edge + 0.5) / TAPER)
    return np.tile(np.where(edge < TAPER, curve, 1.0), (1, 2 * DEV // J2)).astype(np.float32)


def channel_table():
    c, s = cs(np.arange(256)[:, None] * (2 * np.arange(256) + 1)[None], 2 * Q)
    return np_split(np.concatenate([c, s], axis=1))


def offset_table():
    c, s = cs((2 * np.arange(256) + 1)[:, None] * np.arange(256)[None], 2 * Q)
    return np_split(np.concatenate([c, s], axis=0) / Q)


def pack_kernel(raw_ref, out_ref, raw_buf, buf_ref, out_buf, in_sems, out_sems):
    wide = C // 2
    takes = [
        pltpu.make_async_copy(
            raw_ref.at[:, pl.ds(k * wide, wide)], raw_buf.at[:, pl.ds(k * wide, wide)], in_sems.at[k]
        )
        for k in range(2)
    ]
    for take in takes:
        take.start()
    gives = []
    for k in range(2):
        takes[k].wait()
        for i in range(8):
            at = (8 * k + i) * 256
            rows = jnp.concatenate([raw_buf[:, at : at + DEV], raw_buf[:, at + DEV : at + 256]], axis=0)
            buf_ref[pl.ds(1024 * k + i, DEV, stride=8), :] = rows.T
        out_buf[k] = buf_ref[1024 * k : 1024 * (k + 1), :].reshape(DEV, 8, DEV).astype(BF)
        give = pltpu.make_async_copy(
            out_buf.at[k], out_ref.at[:, pl.ds(8 * k, 8), :], out_sems.at[k]
        )
        give.start()
        gives.append(give)
    for give in gives:
        give.wait()


def dot(a, b):
    return jnp.dot(a, b, preferred_element_type=F32)


def spectra_kernel(
    in_ref, s1_ref, tw_ref, s2_ref, win_ref, taper_ref, mask_ref, out_ref, live_ref,
    buf_ref, z_ref, white_ref,
):
    mask = mask_ref[...].astype(F32)
    for i in range(BLK):
        live_ref[i * BLK : (i + 1) * BLK, :] = jnp.broadcast_to(mask[:, i : i + 1], (BLK, DEV))
    series = in_ref[...].astype(F32).reshape(DEV, 2, 8, DEV)
    for k in range(2):
        buf_ref[1024 * k : 1024 * (k + 1), :] = series[:, k].reshape(1024, DEV)
    top_row = lax.broadcasted_iota(jnp.int32, (8, DEV), 0) == 0
    lane = lax.broadcasted_iota(jnp.int32, (1, DEV), 1) % J2

    def turn(g, w=0):
        rows = [
            buf_ref[pl.ds(1024 * (g // 2) + (4 * g + s) % 8, DEV, stride=8), :]
            for s in range(4)
        ]
        y = dot(s1_ref[...], jnp.concatenate(rows, axis=1).astype(BF))
        for s in range(4):
            re, im = y[:64, s * DEV : (s + 1) * DEV], y[64:, s * DEV : (s + 1) * DEV]
            no_im = jnp.concatenate([jnp.where(top_row, 0.0, im[:8]), im[8:]], axis=0)
            re_64 = jnp.concatenate([jnp.where(top_row, im[:8], re[:8]), re[8:]], axis=0)
            for half, real in enumerate((re, re_64)):
                at = slice(half * 64, half * 64 + 64)
                to = slice(g * DEV + half * 64, g * DEV + half * 64 + 64)
                col = s
                z_ref[to, col * DEV : (col + 1) * DEV] = (
                    real * tw_ref[0, at] + no_im * tw_ref[1, at]
                ).astype(BF)
                z_ref[to, (4 + col) * DEV : (5 + col) * DEV] = (
                    no_im * tw_ref[2, at] - real * tw_ref[3, at]
                ).astype(BF)

    def shifted(x, by, edge):
        tiles = [pltpu.roll(x[:, s * DEV : (s + 1) * DEV], by, 1) for s in range(2)]
        return jnp.concatenate([jnp.where(lane == edge, 0.0, t) for t in tiles], axis=1)

    def whiten(h, spec):
        re, im = (
            jnp.concatenate([spec[:DEV, at : at + DEV], spec[DEV:, at : at + DEV]], axis=1)
            for at in (0, DEV)
        )
        power = re * re + im * im
        amp = power * lax.rsqrt(jnp.maximum(power, 1e-30))
        near = [amp, shifted(amp[AFTER], DEV - 1, J2 - 1)]
        near += [shifted(amp[rows], 1, 0) for rows in BEFORE]
        total = dot(win_ref[...], jnp.concatenate(near, axis=0).astype(BF))
        gain = taper_ref[...] / (total * (1.0 / (2 * SW + 1)) + EPS)
        for part, value in enumerate((re * gain, im * gain)):
            for s in range(2):
                white_ref[pl.ds(4 * part + 2 * h + s, DEV, stride=8), :] = value[
                    :, s * DEV : (s + 1) * DEV
                ]

    for g in range(4):
        turn(g)
    spec = dot(z_ref[...], s2_ref[...])
    for h in range(2):
        whiten(h, spec[2 * h * DEV : 2 * (h + 1) * DEV])
    out_ref[...] = white_ref[...].astype(BF)


def stack_kernel(
    in_ref, mask_ref, rot_ref, eh_ref, el_ref, dh_ref, dl_ref, out_ref,
    buf_ref, f_ref, acc_ref, v_ref,
):
    buf_ref[...] = in_ref[...].astype(F32)
    pieces = [buf_ref[pl.ds(t, DEV, stride=8), :].T.astype(BF) for t in range(8)]
    rows = []
    for part in range(2):
        for i in range(BLK):
            g, s = i // 4, i % 4
            tiles = [
                pieces[4 * part + g][(2 * s + h) * J2 : (2 * s + h + 1) * J2] for h in range(2)
            ]
            rows.append(jnp.concatenate(tiles, axis=1))
    white = jnp.concatenate(rows, axis=0)
    product = dot(white, eh_ref[...]) + dot(white, el_ref[...])
    half = BLK * J2
    for t in range(2):
        at = slice(t * DEV, (t + 1) * DEV)
        to = slice(256 + t * DEV, 256 + (t + 1) * DEV)
        rc, rs, ic, ims = product[:half, at], product[:half, to], product[half:, at], product[half:, to]
        for part, sign, value in (
            (0, 0, rc + ims), (0, 1, rc - ims), (1, 0, ic - rs), (1, 1, ic + rs)
        ):
            for k in range(2 * BLK):
                f_ref[pl.ds(part * 1024 + 32 * k + 2 * sign + t, 8, stride=4), :] = value[
                    8 * k : 8 * k + 8
                ]
    acc_ref[...] = jnp.zeros_like(acc_ref)

    def unit(u, carry):
        at = lambda i, part: pl.ds(pl.multiple_of(part * 1024 + i * 64 + u * 8, 8), 8)
        re = [f_ref[at(i, 0), :] for i in range(BLK)]
        im = [f_ref[at(i, 1), :] for i in range(BLK)]
        both = [re[i] + im[i] for i in range(BLK)]
        less = [re[i] - im[i] for i in range(BLK)]
        for delta in range(FAR):
            sums = [None, None, None]
            for i in range(BLK - delta):
                j = i + delta
                live = mask_ref[pl.ds(i * BLK + j, 8, stride=0), :]
                if delta == 0:
                    terms = [live * (re[i] * re[i] + im[i] * im[i])]
                else:
                    a_re, a_im = re[i] * live, im[i] * live
                    terms = [(a_re + a_im) * re[j], a_im * less[j], a_re * both[j]]
                sums = [t if s is None else s + t for s, t in zip(sums, terms)]
            if delta == 0:
                acc_ref[0] = sums[0] - acc_ref[0]
            else:
                acc_ref[2 * delta] = sums[0] - sums[1] - acc_ref[2 * delta]
                acc_ref[2 * delta + 1] = sums[0] - sums[2] - acc_ref[2 * delta + 1]
        return carry

    lax.fori_loop(0, J2 // 2, unit, 0, unroll=4)
    first = lax.broadcasted_iota(jnp.int32, (8, DEV), 0) < 4
    lane = lax.broadcasted_iota(jnp.int32, (8, DEV), 1)
    row = lax.broadcasted_iota(jnp.int32, (8, DEV), 0)
    beside = jnp.where((lane % 2 == 1) == (row % 4 < 2), -1.0, 1.0)
    turn = jnp.where(first, -1.0, 1.0)
    for delta in range(BLK):
        if delta < FAR:
            x_re, x_im = acc_ref[2 * delta], acc_ref[2 * delta + 1]
            if delta + 1 < FAR:
                x_re = x_re - beside * acc_ref[2 * delta + 3]
                x_im = x_im + beside * acc_ref[2 * delta + 2]
            s_re, s_im = pltpu.roll(x_re, 4, 0), pltpu.roll(x_im, 4, 0)
            g_re = jnp.where(first, x_re, s_re) + turn * jnp.where(first, s_im, x_im)
            g_im = jnp.where(first, x_im, s_im) - turn * jnp.where(first, s_re, x_re)
        for u in range(4):
            at = pl.ds((delta * 4 + u) * 8, 8)
            to = pl.ds(512 + (delta * 4 + u) * 8, 8)
            if delta < FAR:
                c, s = rot_ref[0, u], rot_ref[1, u]
                v_ref[at, :] = s * g_im - c * g_re
                v_ref[to, :] = -(c * g_im) - s * g_re
            else:
                v_ref[at, :] = jnp.zeros((8, DEV), F32)
                v_ref[to, :] = jnp.zeros((8, DEV), F32)
    load = lambda c, t: v_ref[pl.ds(512 * c + t, DEV, stride=4), :]
    folded = [load(0, 0) + load(0, 2), load(0, 1) + load(0, 3)]
    folded += [load(1, 0) - load(1, 2), load(1, 1) - load(1, 3)]
    v_hi, v_lo = split(jnp.concatenate(folded, axis=1))
    fine = dot(jnp.concatenate([v_hi, v_lo], axis=0), dh_ref[...])
    stacked = fine[:DEV] + fine[DEV:] + dot(v_hi, dl_ref[...])
    left, right = stacked[:, :DEV], stacked[:, DEV:]
    last = lax.broadcasted_iota(jnp.int32, (DEV, DEV), 1) == DEV - 1
    left1, right1 = pltpu.roll(left, DEV - 1, 1), pltpu.roll(right, DEV - 1, 1)
    beyond = jnp.concatenate([left1[8:], jnp.zeros((8, DEV), F32)], axis=0)
    behind = (jnp.where(last, right1, left1), jnp.where(last, beyond, right1))
    same = first == (lane < 64)
    for delta in range(BLK):
        for t in range(2):
            tile = (left, right)[t][8 * delta : 8 * delta + 8]
            pair = jnp.where(same, tile, pltpu.roll(pltpu.roll(tile, 4, 0), 64, 1))
            at = 4 * (64 + 4 * delta + 2 * t)
            out_ref[at : at + 8, :] = pair.astype(BF)
            tile = behind[t][8 * delta : 8 * delta + 8]
            pair = jnp.where(same, pltpu.roll(tile, 64, 1), pltpu.roll(tile, 4, 0))
            at = 4 * (4 * (BLK - 1 - delta) + 2 - 2 * t)
            out_ref[at : at + 8, :] = pair.astype(BF)


def total_kernel(in_ref, place_ref, scale_ref, out_ref):
    total = jnp.sum(in_ref[...].astype(F32).reshape(DEV // 2, 8, DEV), axis=0)
    total = total + pltpu.roll(total, 4, 0)
    low = lax.broadcasted_iota(jnp.int32, (8, DEV), 0) < 4
    lags = jnp.where(low, total, pltpu.roll(total, 64, 1))
    lane = lax.broadcasted_iota(jnp.int32, (8, DEV), 1)
    flipped = jnp.concatenate([lags[7 - j : 8 - j] for j in range(LAGS)], axis=0)
    flipped = jnp.take_along_axis(flipped, (63 - lane) & 127, axis=1)
    out = jnp.where(place_ref[0] == 1, flipped, lags)
    out_ref[...] = out[:, :64] * scale_ref[...]


def pair_counts(mask, columns):
    blocks = mask.shape[0]
    width = C // blocks
    labels = lax.iota(jnp.int32, blocks)
    apart = labels[None, :] - labels[:, None]
    deltas = lax.iota(jnp.int32, 2 * blocks - 1) - (blocks - 1)
    per_delta = jnp.sum(
        mask[None] * (apart[None] == deltas[:, None, None]).astype(jnp.int32), axis=(1, 2)
    )
    offsets = columns - C
    intersection = jnp.maximum(0, width - jnp.abs(offsets[:, None] - width * deltas[None, :]))
    return jnp.sum(intersection * per_delta[None, :], axis=1)


def stack_scale(counts):
    return 1.0 / jnp.sqrt(NB * jnp.maximum(counts, 1).astype(jnp.float32))


VM = pl.BlockSpec(memory_space=pltpu.VMEM)
SM = pl.BlockSpec(memory_space=pltpu.SMEM)
LIMIT = pltpu.CompilerParams(vmem_limit_bytes=24 * 1024 * 1024)


def exchange(x, rows):
    x = x.reshape(DEV, rows, DEV)
    return lax.all_to_all(x, ("blk", "lag"), split_axis=0, concat_axis=0, tiled=True)


def on_device(raw, mask):
    device = lax.axis_index("blk") * lax.axis_size("lag") + lax.axis_index("lag")
    packed = pl.pallas_call(
        pack_kernel,
        out_shape=jax.ShapeDtypeStruct((DEV, BLK, DEV), BF),
        in_specs=[pl.BlockSpec(memory_space=pltpu.HBM)],
        out_specs=pl.BlockSpec(memory_space=pltpu.HBM),
        scratch_shapes=[
            pltpu.VMEM((ROWS, C), F32),
            pltpu.VMEM((BLK * DEV, DEV), F32),
            pltpu.VMEM((2, DEV, 8, DEV), BF),
            pltpu.SemaphoreType.DMA((2,)),
            pltpu.SemaphoreType.DMA((2,)),
        ],
    )(raw)
    series = exchange(packed, BLK).reshape(BLK * DEV, DEV)
    stage1, twiddle, stage2 = time_tables()
    white, live = pl.pallas_call(
        spectra_kernel,
        out_shape=(
            jax.ShapeDtypeStruct((8 * DEV, DEV), BF),
            jax.ShapeDtypeStruct((BLK * BLK, DEV), F32),
        ),
        in_specs=[VM] * 7,
        out_specs=(VM, VM),
        compiler_params=LIMIT,
        scratch_shapes=[
            pltpu.VMEM((BLK * DEV, DEV), F32),
            pltpu.VMEM((4 * DEV, 8 * DEV), BF),
            pltpu.VMEM((8 * DEV, DEV), F32),
        ],
    )(series, stage1, twiddle, stage2, window_table(), taper_table(), mask)
    banded = exchange(white, 8).reshape(8 * DEV, DEV)
    odd = 2 * lax.iota(jnp.int32, LAGS) - (LAGS - 1)
    angle = jnp.mod(odd * first_bin(device), Q).astype(F32) * (2 * math.pi / Q)
    spread = lambda x: jnp.broadcast_to(x.reshape(4, 2, 1, 1), (4, 2, 4, DEV)).reshape(4, 8, DEV)
    rotation = jnp.stack([spread(jnp.cos(angle)), spread(jnp.sin(angle))])
    parts = pl.pallas_call(
        stack_kernel,
        out_shape=jax.ShapeDtypeStruct((4 * DEV, DEV), BF),
        in_specs=[VM] * 7,
        out_specs=VM,
        compiler_params=LIMIT,
        scratch_shapes=[
            pltpu.VMEM((8 * DEV, DEV), F32),
            pltpu.VMEM((2048, DEV), F32),
            pltpu.VMEM((2 * FAR, 8, DEV), F32),
            pltpu.VMEM((8 * DEV, DEV), F32),
        ],
    )(banded, live, rotation, *channel_table(), *offset_table())
    shares = exchange(parts, 4).reshape(4 * DEV, DEV)
    columns = device * 64 + lax.iota(jnp.int32, 64)
    scale = stack_scale(pair_counts(mask, columns))[None, :]
    place = (device < 64).astype(jnp.int32)[None]
    return pl.pallas_call(
        total_kernel,
        out_shape=jax.ShapeDtypeStruct((LAGS, 64), F32),
        in_specs=[VM, SM, VM],
        out_specs=VM,
        compiler_params=LIMIT,
    )(shares, place, scale)


def solution(mesh):
    return jax.shard_map(
        on_device,
        mesh=mesh,
        in_specs=(P(("blk", "lag"), None), P()),
        out_specs=P(None, ("blk", "lag")),
        check_vma=False,
    )
```

```python
import math

import jax
import jax.numpy as jnp
import numpy as np
from jax import lax
from jax.experimental import pallas as pl
from jax.experimental.pallas import tpu as pltpu
from jax.sharding import PartitionSpec as P

NT = 8192
C = 4096
NB = 2048
K0 = 16
SW = 32
TAPER = 128
LAGS = 8
LAG_STEP = 32
EPS = 1e-06

DEV = 128
ROWS = NT // DEV
BLK = 16
J2 = NB // DEV
Q = 512
FAR = 15

BF = jnp.bfloat16
F32 = jnp.float32


def split(x):
    hi = x.astype(BF)
    return hi, (x - hi.astype(F32)).astype(BF)


def np_split(x):
    hi = np.asarray(x, np.float32).astype(jnp.bfloat16)
    lo = (np.asarray(x, np.float64) - hi.astype(np.float64)).astype(jnp.bfloat16)
    return hi, lo


def cs(numer, period):
    angle = 2 * np.pi * np.mod(numer, period) / period
    return np.cos(angle), np.sin(angle)


def first_bins():
    n = np.arange(64)
    residue = np.concatenate([n, (DEV - n) % DEV])
    residue[64] = 64
    return np.where(residue < K0, residue + DEV, residue)


def first_bin(row):
    residue = jnp.where(row <= 64, row, 192 - row)
    return jnp.where(residue < K0, residue + DEV, residue)


def time_tables():
    n, p = np.arange(64), np.arange(DEV)
    c, s = cs(n[:, None] * p[None], DEV)
    stage1 = np.concatenate([c, -s], axis=0)
    stage1[64] = np.cos(np.pi * p)
    r = np.tile(np.arange(ROWS), 2)
    c, s = cs(first_bins()[:, None] * r[None], NT)
    mirror = np.where(np.arange(DEV) < 64, 1.0, -1.0)[:, None]
    twiddle = np.stack([c, mirror * s, mirror * c, s]).astype(np.float32)
    r, j2 = np.arange(ROWS), np.arange(J2)
    c, s = cs(r[:, None] * j2[None], ROWS)
    eye = np.eye(8)
    place = lambda t: np.einsum("ab,rj->arbj", eye, t).reshape(8 * ROWS, 8 * J2)
    stage2 = np.block([[place(c), place(-s)], [place(s), place(c)]])
    return stage1.astype(jnp.bfloat16), twiddle, stage2.astype(jnp.bfloat16)


AFTER, BEFORE = slice(16, 48), (slice(0, 16), slice(64, 96))


def window_table():
    bins = first_bins()
    gap = bins[:, None] - bins[None]
    near = lambda d: (np.abs(d) <= SW).astype(np.float32)
    after, before = near(gap - DEV), near(gap + DEV)
    return np.concatenate(
        [near(gap), after[:, AFTER]] + [before[:, rows] for rows in BEFORE], axis=1
    ).astype(jnp.bfloat16)


def taper_table():
    position = (first_bins() - K0)[:, None] + DEV * np.arange(J2)[None]
    edge = np.minimum(position, NB - 1 - position)
    curve = 0.5 - 0.5 * np.cos(math.pi * (edge + 0.5) / TAPER)
    return np.tile(np.where(edge < TAPER, curve, 1.0), (1, 2 * DEV // J2)).astype(np.float32)


def channel_table():
    c, s = cs(np.arange(256)[:, None] * (2 * np.arange(256) + 1)[None], 2 * Q)
    return np_split(np.concatenate([c, s], axis=1))


def offset_table():
    c, s = cs((2 * np.arange(256) + 1)[:, None] * np.arange(256)[None], 2 * Q)
    return np_split(np.concatenate([c, s], axis=0) / Q)


def pack_kernel(raw_ref, out_ref, raw_buf, buf_ref, out_buf, in_sems, out_sems):
    wide = C // 2
    takes = [
        pltpu.make_async_copy(
            raw_ref.at[:, pl.ds(k * wide, wide)], raw_buf.at[:, pl.ds(k * wide, wide)], in_sems.at[k]
        )
        for k in range(2)
    ]
    for take in takes:
        take.start()
    gives = []
    for k in range(2):
        takes[k].wait()
        for i in range(8):
            at = (8 * k + i) * 256
            rows = jnp.concatenate([raw_buf[:, at : at + DEV], raw_buf[:, at + DEV : at + 256]], axis=0)
            buf_ref[pl.ds(1024 * k + i, DEV, stride=8), :] = rows.T
        out_buf[k] = buf_ref[1024 * k : 1024 * (k + 1), :].reshape(DEV, 8, DEV).astype(BF)
        give = pltpu.make_async_copy(
            out_buf.at[k], out_ref.at[:, pl.ds(8 * k, 8), :], out_sems.at[k]
        )
        give.start()
        gives.append(give)
    for give in gives:
        give.wait()


def dot(a, b):
    return jnp.dot(a, b, preferred_element_type=F32)


def spectra_kernel(
    in_ref, s1_ref, tw_ref, s2_ref, win_ref, taper_ref, mask_ref, out_ref, live_ref,
    buf_ref, z_ref, white_ref,
):
    mask = mask_ref[...].astype(F32)
    for i in range(BLK):
        live_ref[i * BLK : (i + 1) * BLK, :] = jnp.broadcast_to(mask[:, i : i + 1], (BLK, DEV))
    series = in_ref[...].astype(F32).reshape(DEV, 2, 8, DEV)
    for k in range(2):
        buf_ref[1024 * k : 1024 * (k + 1), :] = series[:, k].reshape(1024, DEV)
    top_row = lax.broadcasted_iota(jnp.int32, (8, DEV), 0) == 0
    lane = lax.broadcasted_iota(jnp.int32, (1, DEV), 1) % J2

    def turn(g, w):
        rows = [
            buf_ref[pl.ds(1024 * (g // 2) + (4 * g + 2 * w + s) % 8, DEV, stride=8), :]
            for s in range(2)
        ]
        y = dot(s1_ref[...], jnp.concatenate(rows, axis=1).astype(BF))
        for s in range(2):
            re, im = y[:64, s * DEV : (s + 1) * DEV], y[64:, s * DEV : (s + 1) * DEV]
            no_im = jnp.concatenate([jnp.where(top_row, 0.0, im[:8]), im[8:]], axis=0)
            re_64 = jnp.concatenate([jnp.where(top_row, im[:8], re[:8]), re[8:]], axis=0)
            for half, real in enumerate((re, re_64)):
                at = slice(half * 64, half * 64 + 64)
                to = slice(g * DEV + half * 64, g * DEV + half * 64 + 64)
                col = 2 * w + s
                z_ref[to, col * DEV : (col + 1) * DEV] = (
                    real * tw_ref[0, at] + no_im * tw_ref[1, at]
                ).astype(BF)
                z_ref[to, (4 + col) * DEV : (5 + col) * DEV] = (
                    no_im * tw_ref[2, at] - real * tw_ref[3, at]
                ).astype(BF)

    def shifted(x, by, edge):
        tiles = [pltpu.roll(x[:, s * DEV : (s + 1) * DEV], by, 1) for s in range(2)]
        return jnp.concatenate([jnp.where(lane == edge, 0.0, t) for t in tiles], axis=1)

    def whiten(h, spec):
        re, im = (
            jnp.concatenate([spec[:DEV, at : at + DEV], spec[DEV:, at : at + DEV]], axis=1)
            for at in (0, DEV)
        )
        power = re * re + im * im
        amp = power * lax.rsqrt(jnp.maximum(power, 1e-30))
        near = [amp, shifted(amp[AFTER], DEV - 1, J2 - 1)]
        near += [shifted(amp[rows], 1, 0) for rows in BEFORE]
        total = dot(win_ref[...], jnp.concatenate(near, axis=0).astype(BF))
        gain = taper_ref[...] / (total * (1.0 / (2 * SW + 1)) + EPS)
        for part, value in enumerate((re * gain, im * gain)):
            for s in range(2):
                white_ref[pl.ds(4 * part + 2 * h + s, DEV, stride=8), :] = value[
                    :, s * DEV : (s + 1) * DEV
                ]

    for g in range(4):
        for w in range(2):
            turn(g, w)
    spec = dot(z_ref[...], s2_ref[...])
    for h in range(2):
        whiten(h, spec[2 * h * DEV : 2 * (h + 1) * DEV])
    out_ref[...] = white_ref[...].astype(BF)


def stack_kernel(
    in_ref, mask_ref, rot_ref, eh_ref, el_ref, dh_ref, dl_ref, out_ref,
    buf_ref, f_ref, acc_ref, v_ref,
):
    buf_ref[...] = in_ref[...].astype(F32)
    pieces = [buf_ref[pl.ds(t, DEV, stride=8), :].T.astype(BF) for t in range(8)]
    rows = []
    for part in range(2):
        for i in range(BLK):
            g, s = i // 4, i % 4
            tiles = [
                pieces[4 * part + g][(2 * s + h) * J2 : (2 * s + h + 1) * J2] for h in range(2)
            ]
            rows.append(jnp.concatenate(tiles, axis=1))
    white = jnp.concatenate(rows, axis=0)
    product = dot(white, eh_ref[...]) + dot(white, el_ref[...])
    half = BLK * J2
    for t in range(2):
        at = slice(t * DEV, (t + 1) * DEV)
        to = slice(256 + t * DEV, 256 + (t + 1) * DEV)
        rc, rs, ic, ims = product[:half, at], product[:half, to], product[half:, at], product[half:, to]
        for part, sign, value in (
            (0, 0, rc + ims), (0, 1, rc - ims), (1, 0, ic - rs), (1, 1, ic + rs)
        ):
            for k in range(2 * BLK):
                f_ref[pl.ds(part * 1024 + 32 * k + 2 * sign + t, 8, stride=4), :] = value[
                    8 * k : 8 * k + 8
                ]
    acc_ref[...] = jnp.zeros_like(acc_ref)

    def unit(u, carry):
        at = lambda i, part: pl.ds(pl.multiple_of(part * 1024 + i * 64 + u * 8, 8), 8)
        re = [f_ref[at(i, 0), :] for i in range(BLK)]
        im = [f_ref[at(i, 1), :] for i in range(BLK)]
        both = [re[i] + im[i] for i in range(BLK)]
        less = [re[i] - im[i] for i in range(BLK)]
        for delta in range(FAR):
            sums = [None, None, None]
            for i in range(BLK - delta):
                j = i + delta
                live = mask_ref[pl.ds(i * BLK + j, 8, stride=0), :]
                if delta == 0:
                    terms = [live * (re[i] * re[i] + im[i] * im[i])]
                else:
                    a_re, a_im = re[i] * live, im[i] * live
                    terms = [(a_re + a_im) * re[j], a_im * less[j], a_re * both[j]]
                sums = [t if s is None else s + t for s, t in zip(sums, terms)]
            if delta == 0:
                acc_ref[0] = sums[0] - acc_ref[0]
            else:
                acc_ref[2 * delta] = sums[0] - sums[1] - acc_ref[2 * delta]
                acc_ref[2 * delta + 1] = sums[0] - sums[2] - acc_ref[2 * delta + 1]
        return carry

    lax.fori_loop(0, J2 // 2, unit, 0, unroll=4)
    first = lax.broadcasted_iota(jnp.int32, (8, DEV), 0) < 4
    lane = lax.broadcasted_iota(jnp.int32, (8, DEV), 1)
    row = lax.broadcasted_iota(jnp.int32, (8, DEV), 0)
    beside = jnp.where((lane % 2 == 1) == (row % 4 < 2), -1.0, 1.0)
    turn = jnp.where(first, -1.0, 1.0)
    for delta in range(BLK):
        if delta < FAR:
            x_re, x_im = acc_ref[2 * delta], acc_ref[2 * delta + 1]
            if delta + 1 < FAR:
                x_re = x_re - beside * acc_ref[2 * delta + 3]
                x_im = x_im + beside * acc_ref[2 * delta + 2]
            s_re, s_im = pltpu.roll(x_re, 4, 0), pltpu.roll(x_im, 4, 0)
            g_re = jnp.where(first, x_re, s_re) + turn * jnp.where(first, s_im, x_im)
            g_im = jnp.where(first, x_im, s_im) - turn * jnp.where(first, s_re, x_re)
        for u in range(4):
            at = pl.ds((delta * 4 + u) * 8, 8)
            to = pl.ds(512 + (delta * 4 + u) * 8, 8)
            if delta < FAR:
                c, s = rot_ref[0, u], rot_ref[1, u]
                v_ref[at, :] = s * g_im - c * g_re
                v_ref[to, :] = -(c * g_im) - s * g_re
            else:
                v_ref[at, :] = jnp.zeros((8, DEV), F32)
                v_ref[to, :] = jnp.zeros((8, DEV), F32)
    load = lambda c, t: v_ref[pl.ds(512 * c + t, DEV, stride=4), :]
    folded = [load(0, 0) + load(0, 2), load(0, 1) + load(0, 3)]
    folded += [load(1, 0) - load(1, 2), load(1, 1) - load(1, 3)]
    v_hi, v_lo = split(jnp.concatenate(folded, axis=1))
    fine = dot(jnp.concatenate([v_hi, v_lo], axis=0), dh_ref[...])
    stacked = fine[:DEV] + fine[DEV:] + dot(v_hi, dl_ref[...])
    left, right = stacked[:, :DEV], stacked[:, DEV:]
    last = lax.broadcasted_iota(jnp.int32, (DEV, DEV), 1) == DEV - 1
    left1, right1 = pltpu.roll(left, DEV - 1, 1), pltpu.roll(right, DEV - 1, 1)
    beyond = jnp.concatenate([left1[8:], jnp.zeros((8, DEV), F32)], axis=0)
    behind = (jnp.where(last, right1, left1), jnp.where(last, beyond, right1))
    same = first == (lane < 64)
    for delta in range(BLK):
        for t in range(2):
            tile = (left, right)[t][8 * delta : 8 * delta + 8]
            pair = jnp.where(same, tile, pltpu.roll(pltpu.roll(tile, 4, 0), 64, 1))
            at = 4 * (64 + 4 * delta + 2 * t)
            out_ref[at : at + 8, :] = pair.astype(BF)
            tile = behind[t][8 * delta : 8 * delta + 8]
            pair = jnp.where(same, pltpu.roll(tile, 64, 1), pltpu.roll(tile, 4, 0))
            at = 4 * (4 * (BLK - 1 - delta) + 2 - 2 * t)
            out_ref[at : at + 8, :] = pair.astype(BF)


def total_kernel(in_ref, place_ref, scale_ref, out_ref):
    total = jnp.sum(in_ref[...].astype(F32).reshape(DEV // 2, 8, DEV), axis=0)
    total = total + pltpu.roll(total, 4, 0)
    low = lax.broadcasted_iota(jnp.int32, (8, DEV), 0) < 4
    lags = jnp.where(low, total, pltpu.roll(total, 64, 1))
    lane = lax.broadcasted_iota(jnp.int32, (8, DEV), 1)
    flipped = jnp.concatenate([lags[7 - j : 8 - j] for j in range(LAGS)], axis=0)
    flipped = jnp.take_along_axis(flipped, (63 - lane) & 127, axis=1)
    out = jnp.where(place_ref[0] == 1, flipped, lags)
    out_ref[...] = out[:, :64] * scale_ref[...]


def pair_counts(mask, columns):
    blocks = mask.shape[0]
    width = C // blocks
    labels = lax.iota(jnp.int32, blocks)
    apart = labels[None, :] - labels[:, None]
    deltas = lax.iota(jnp.int32, 2 * blocks - 1) - (blocks - 1)
    per_delta = jnp.sum(
        mask[None] * (apart[None] == deltas[:, None, None]).astype(jnp.int32), axis=(1, 2)
    )
    offsets = columns - C
    intersection = jnp.maximum(0, width - jnp.abs(offsets[:, None] - width * deltas[None, :]))
    return jnp.sum(intersection * per_delta[None, :], axis=1)


def stack_scale(counts):
    return 1.0 / jnp.sqrt(NB * jnp.maximum(counts, 1).astype(jnp.float32))


VM = pl.BlockSpec(memory_space=pltpu.VMEM)
SM = pl.BlockSpec(memory_space=pltpu.SMEM)
LIMIT = pltpu.CompilerParams(vmem_limit_bytes=24 * 1024 * 1024)


def exchange(x, rows):
    x = x.reshape(DEV, rows, DEV)
    return lax.all_to_all(x, ("blk", "lag"), split_axis=0, concat_axis=0, tiled=True)


def on_device(raw, mask):
    device = lax.axis_index("blk") * lax.axis_size("lag") + lax.axis_index("lag")
    packed = pl.pallas_call(
        pack_kernel,
        out_shape=jax.ShapeDtypeStruct((DEV, BLK, DEV), BF),
        in_specs=[pl.BlockSpec(memory_space=pltpu.HBM)],
        out_specs=pl.BlockSpec(memory_space=pltpu.HBM),
        scratch_shapes=[
            pltpu.VMEM((ROWS, C), F32),
            pltpu.VMEM((BLK * DEV, DEV), F32),
            pltpu.VMEM((2, DEV, 8, DEV), BF),
            pltpu.SemaphoreType.DMA((2,)),
            pltpu.SemaphoreType.DMA((2,)),
        ],
    )(raw)
    series = exchange(packed, BLK).reshape(BLK * DEV, DEV)
    stage1, twiddle, stage2 = time_tables()
    white, live = pl.pallas_call(
        spectra_kernel,
        out_shape=(
            jax.ShapeDtypeStruct((8 * DEV, DEV), BF),
            jax.ShapeDtypeStruct((BLK * BLK, DEV), F32),
        ),
        in_specs=[VM] * 7,
        out_specs=(VM, VM),
        compiler_params=LIMIT,
        scratch_shapes=[
            pltpu.VMEM((BLK * DEV, DEV), F32),
            pltpu.VMEM((4 * DEV, 8 * DEV), BF),
            pltpu.VMEM((8 * DEV, DEV), F32),
        ],
    )(series, stage1, twiddle, stage2, window_table(), taper_table(), mask)
    banded = exchange(white, 8).reshape(8 * DEV, DEV)
    odd = 2 * lax.iota(jnp.int32, LAGS) - (LAGS - 1)
    angle = jnp.mod(odd * first_bin(device), Q).astype(F32) * (2 * math.pi / Q)
    spread = lambda x: jnp.broadcast_to(x.reshape(4, 2, 1, 1), (4, 2, 4, DEV)).reshape(4, 8, DEV)
    rotation = jnp.stack([spread(jnp.cos(angle)), spread(jnp.sin(angle))])
    parts = pl.pallas_call(
        stack_kernel,
        out_shape=jax.ShapeDtypeStruct((4 * DEV, DEV), BF),
        in_specs=[VM] * 7,
        out_specs=VM,
        compiler_params=LIMIT,
        scratch_shapes=[
            pltpu.VMEM((8 * DEV, DEV), F32),
            pltpu.VMEM((2048, DEV), F32),
            pltpu.VMEM((2 * FAR, 8, DEV), F32),
            pltpu.VMEM((8 * DEV, DEV), F32),
        ],
    )(banded, live, rotation, *channel_table(), *offset_table())
    shares = exchange(parts, 4).reshape(4 * DEV, DEV)
    columns = device * 64 + lax.iota(jnp.int32, 64)
    scale = stack_scale(pair_counts(mask, columns))[None, :]
    place = (device < 64).astype(jnp.int32)[None]
    return pl.pallas_call(
        total_kernel,
        out_shape=jax.ShapeDtypeStruct((LAGS, 64), F32),
        in_specs=[VM, SM, VM],
        out_specs=VM,
        compiler_params=LIMIT,
    )(shares, place, scale)


def solution(mesh):
    return jax.shard_map(
        on_device,
        mesh=mesh,
        in_specs=(P(("blk", "lag"), None), P()),
        out_specs=P(None, ("blk", "lag")),
        check_vma=False,
    )
```

```python
import math

import jax
import jax.numpy as jnp
import numpy as np
from jax import lax
from jax.experimental import pallas as pl
from jax.experimental.pallas import tpu as pltpu
from jax.sharding import PartitionSpec as P

NT = 8192
C = 4096
NB = 2048
K0 = 16
SW = 32
TAPER = 128
LAGS = 8
LAG_STEP = 32
EPS = 1e-06

DEV = 128
ROWS = NT // DEV
BLK = 16
J2 = NB // DEV
Q = 512
FAR = 15

BF = jnp.bfloat16
F32 = jnp.float32


def split(x):
    hi = x.astype(BF)
    return hi, (x - hi.astype(F32)).astype(BF)


def np_split(x):
    hi = np.asarray(x, np.float32).astype(jnp.bfloat16)
    lo = (np.asarray(x, np.float64) - hi.astype(np.float64)).astype(jnp.bfloat16)
    return hi, lo


def cs(numer, period):
    angle = 2 * np.pi * np.mod(numer, period) / period
    return np.cos(angle), np.sin(angle)


def first_bins():
    n = np.arange(64)
    residue = np.concatenate([n, (DEV - n) % DEV])
    residue[64] = 64
    return np.where(residue < K0, residue + DEV, residue)


def first_bin(row):
    residue = jnp.where(row <= 64, row, 192 - row)
    return jnp.where(residue < K0, residue + DEV, residue)


def time_tables():
    n, p = np.arange(64), np.arange(DEV)
    c, s = cs(n[:, None] * p[None], DEV)
    stage1 = np.concatenate([c, -s], axis=0)
    stage1[64] = np.cos(np.pi * p)
    r = np.tile(np.arange(ROWS), 2)
    c, s = cs(first_bins()[:, None] * r[None], NT)
    mirror = np.where(np.arange(DEV) < 64, 1.0, -1.0)[:, None]
    twiddle = np.stack([c, mirror * s, mirror * c, s]).astype(np.float32)
    r, j2 = np.arange(ROWS), np.arange(J2)
    c, s = cs(r[:, None] * j2[None], ROWS)
    eye = np.eye(8)
    place = lambda t: np.einsum("ab,rj->arbj", eye, t).reshape(8 * ROWS, 8 * J2)
    stage2 = np.block([[place(c), place(-s)], [place(s), place(c)]])
    return stage1.astype(jnp.bfloat16), twiddle, stage2.astype(jnp.bfloat16)


AFTER, BEFORE = slice(16, 48), (slice(0, 16), slice(64, 96))


def window_table():
    bins = first_bins()
    gap = bins[:, None] - bins[None]
    near = lambda d: (np.abs(d) <= SW).astype(np.float32)
    after, before = near(gap - DEV), near(gap + DEV)
    return np.concatenate(
        [near(gap), after[:, AFTER]] + [before[:, rows] for rows in BEFORE], axis=1
    ).astype(jnp.bfloat16)


def taper_table():
    position = (first_bins() - K0)[:, None] + DEV * np.arange(J2)[None]
    edge = np.minimum(position, NB - 1 - position)
    curve = 0.5 - 0.5 * np.cos(math.pi * (edge + 0.5) / TAPER)
    return np.tile(np.where(edge < TAPER, curve, 1.0), (1, 2 * DEV // J2)).astype(np.float32)


def channel_table():
    c, s = cs(np.arange(256)[:, None] * (2 * np.arange(256) + 1)[None], 2 * Q)
    return np_split(np.concatenate([c, s], axis=1))


def offset_table():
    c, s = cs((2 * np.arange(256) + 1)[:, None] * np.arange(256)[None], 2 * Q)
    return np_split(np.concatenate([c, s], axis=0) / Q)


def pack_kernel(raw_ref, out_ref, raw_buf, buf_ref, out_buf, in_sems, out_sems):
    wide = C // 2
    takes = [
        pltpu.make_async_copy(
            raw_ref.at[:, pl.ds(k * wide, wide)], raw_buf.at[:, pl.ds(k * wide, wide)], in_sems.at[k]
        )
        for k in range(2)
    ]
    for take in takes:
        take.start()
    gives = []
    for k in range(2):
        takes[k].wait()
        for i in range(8):
            at = (8 * k + i) * 256
            rows = jnp.concatenate([raw_buf[:, at : at + DEV], raw_buf[:, at + DEV : at + 256]], axis=0)
            buf_ref[pl.ds(1024 * k + i, DEV, stride=8), :] = rows.T
        out_buf[k] = buf_ref[1024 * k : 1024 * (k + 1), :].reshape(DEV, 8, DEV).astype(BF)
        give = pltpu.make_async_copy(
            out_buf.at[k], out_ref.at[:, pl.ds(8 * k, 8), :], out_sems.at[k]
        )
        give.start()
        gives.append(give)
    for give in gives:
        give.wait()


def dot(a, b):
    return jnp.dot(a, b, preferred_element_type=F32)


def spectra_kernel(
    in_ref, s1_ref, tw_ref, s2_ref, win_ref, taper_ref, mask_ref, out_ref, live_ref,
    buf_ref, z_ref, white_ref,
):
    mask = mask_ref[...].astype(F32)
    for i in range(BLK):
        live_ref[i * BLK : (i + 1) * BLK, :] = jnp.broadcast_to(mask[:, i : i + 1], (BLK, DEV))
    series = in_ref[...].astype(F32).reshape(DEV, 2, 8, DEV)
    for k in range(2):
        buf_ref[1024 * k : 1024 * (k + 1), :] = series[:, k].reshape(1024, DEV)
    top_row = lax.broadcasted_iota(jnp.int32, (8, DEV), 0) == 0
    lane = lax.broadcasted_iota(jnp.int32, (1, DEV), 1) % J2

    def turn(g, w):
        rows = [
            buf_ref[pl.ds(1024 * (g // 2) + (4 * g + 2 * w + s) % 8, DEV, stride=8), :]
            for s in range(2)
        ]
        y = dot(s1_ref[...], jnp.concatenate(rows, axis=1).astype(BF))
        for s in range(2):
            re, im = y[:64, s * DEV : (s + 1) * DEV], y[64:, s * DEV : (s + 1) * DEV]
            no_im = jnp.concatenate([jnp.where(top_row, 0.0, im[:8]), im[8:]], axis=0)
            re_64 = jnp.concatenate([jnp.where(top_row, im[:8], re[:8]), re[8:]], axis=0)
            for half, real in enumerate((re, re_64)):
                at = slice(half * 64, half * 64 + 64)
                to = slice(g * DEV + half * 64, g * DEV + half * 64 + 64)
                col = 2 * w + s
                z_ref[to, col * DEV : (col + 1) * DEV] = (
                    real * tw_ref[0, at] + no_im * tw_ref[1, at]
                ).astype(BF)
                z_ref[to, (4 + col) * DEV : (5 + col) * DEV] = (
                    no_im * tw_ref[2, at] - real * tw_ref[3, at]
                ).astype(BF)

    def shifted(x, by, edge):
        tiles = [pltpu.roll(x[:, s * DEV : (s + 1) * DEV], by, 1) for s in range(2)]
        return jnp.concatenate([jnp.where(lane == edge, 0.0, t) for t in tiles], axis=1)

    def whiten(h, spec):
        re, im = (
            jnp.concatenate([spec[:DEV, at : at + DEV], spec[DEV:, at : at + DEV]], axis=1)
            for at in (0, DEV)
        )
        power = re * re + im * im
        amp = power * lax.rsqrt(jnp.maximum(power, 1e-30))
        near = [amp, shifted(amp[AFTER], DEV - 1, J2 - 1)]
        near += [shifted(amp[rows], 1, 0) for rows in BEFORE]
        total = dot(win_ref[...], jnp.concatenate(near, axis=0).astype(BF))
        gain = taper_ref[...] / (total * (1.0 / (2 * SW + 1)) + EPS)
        for part, value in enumerate((re * gain, im * gain)):
            for s in range(2):
                white_ref[pl.ds(4 * part + 2 * h + s, DEV, stride=8), :] = value[
                    :, s * DEV : (s + 1) * DEV
                ]

    for g in range(4):
        for w in range(2):
            turn(g, w)
    spec = dot(z_ref[...], s2_ref[...])
    for h in range(2):
        whiten(h, spec[2 * h * DEV : 2 * (h + 1) * DEV])
    out_ref[...] = white_ref[...].astype(BF)


def stack_kernel(
    in_ref, mask_ref, rot_ref, eh_ref, el_ref, dh_ref, dl_ref, out_ref,
    buf_ref, f_ref, acc_ref, v_ref,
):
    buf_ref[...] = in_ref[...].astype(F32)
    pieces = [buf_ref[pl.ds(t, DEV, stride=8), :].T.astype(BF) for t in range(8)]
    rows = []
    for part in range(2):
        for i in range(BLK):
            g, s = i // 4, i % 4
            tiles = [
                pieces[4 * part + g][(2 * s + h) * J2 : (2 * s + h + 1) * J2] for h in range(2)
            ]
            rows.append(jnp.concatenate(tiles, axis=1))
    white = jnp.concatenate(rows, axis=0)
    product = dot(white, eh_ref[...]) + dot(white, el_ref[...])
    half = BLK * J2
    for t in range(2):
        at = slice(t * DEV, (t + 1) * DEV)
        to = slice(256 + t * DEV, 256 + (t + 1) * DEV)
        rc, rs, ic, ims = product[:half, at], product[:half, to], product[half:, at], product[half:, to]
        for part, sign, value in (
            (0, 0, rc + ims), (0, 1, rc - ims), (1, 0, ic - rs), (1, 1, ic + rs)
        ):
            for k in range(2 * BLK):
                f_ref[pl.ds(part * 1024 + 32 * k + 2 * sign + t, 8, stride=4), :] = value[
                    8 * k : 8 * k + 8
                ]
    acc_ref[...] = jnp.zeros_like(acc_ref)

    def unit(u, carry):
        at = lambda i, part: pl.ds(pl.multiple_of(part * 1024 + i * 64 + u * 8, 8), 8)
        re = [f_ref[at(i, 0), :] for i in range(BLK)]
        im = [f_ref[at(i, 1), :] for i in range(BLK)]
        both = [re[i] + im[i] for i in range(BLK)]
        less = [re[i] - im[i] for i in range(BLK)]
        for delta in range(FAR):
            sums = [None, None, None]
            for i in range(BLK - delta):
                j = i + delta
                live = mask_ref[pl.ds(i * BLK + j, 8, stride=0), :]
                if delta == 0:
                    terms = [live * (re[i] * re[i] + im[i] * im[i])]
                else:
                    a_re, a_im = re[i] * live, im[i] * live
                    terms = [(a_re + a_im) * re[j], a_im * less[j], a_re * both[j]]
                sums = [t if s is None else s + t for s, t in zip(sums, terms)]
            if delta == 0:
                acc_ref[0] = sums[0] - acc_ref[0]
            else:
                acc_ref[2 * delta] = sums[0] - sums[1] - acc_ref[2 * delta]
                acc_ref[2 * delta + 1] = sums[0] - sums[2] - acc_ref[2 * delta + 1]
        return carry

    lax.fori_loop(0, J2 // 2, unit, 0, unroll=4)
    first = lax.broadcasted_iota(jnp.int32, (8, DEV), 0) < 4
    lane = lax.broadcasted_iota(jnp.int32, (8, DEV), 1)
    row = lax.broadcasted_iota(jnp.int32, (8, DEV), 0)
    beside = jnp.where((lane % 2 == 1) == (row % 4 < 2), -1.0, 1.0)
    turn = jnp.where(first, -1.0, 1.0)
    for delta in range(BLK):
        if delta < FAR:
            x_re, x_im = acc_ref[2 * delta], acc_ref[2 * delta + 1]
            if delta + 1 < FAR:
                x_re = x_re - beside * acc_ref[2 * delta + 3]
                x_im = x_im + beside * acc_ref[2 * delta + 2]
            s_re, s_im = pltpu.roll(x_re, 4, 0), pltpu.roll(x_im, 4, 0)
            g_re = jnp.where(first, x_re, s_re) + turn * jnp.where(first, s_im, x_im)
            g_im = jnp.where(first, x_im, s_im) - turn * jnp.where(first, s_re, x_re)
        for u in range(4):
            at = pl.ds((delta * 4 + u) * 8, 8)
            to = pl.ds(512 + (delta * 4 + u) * 8, 8)
            if delta < FAR:
                c, s = rot_ref[0, u], rot_ref[1, u]
                v_ref[at, :] = s * g_im - c * g_re
                v_ref[to, :] = -(c * g_im) - s * g_re
            else:
                v_ref[at, :] = jnp.zeros((8, DEV), F32)
                v_ref[to, :] = jnp.zeros((8, DEV), F32)
    load = lambda c, t: v_ref[pl.ds(512 * c + t, DEV, stride=4), :]
    folded = [load(0, 0) + load(0, 2), load(0, 1) + load(0, 3)]
    folded += [load(1, 0) - load(1, 2), load(1, 1) - load(1, 3)]
    v_hi, v_lo = split(jnp.concatenate(folded, axis=1))
    fine = dot(jnp.concatenate([v_hi, v_lo], axis=0), dh_ref[...])
    stacked = fine[:DEV] + fine[DEV:] + dot(v_hi, dl_ref[...])
    left, right = stacked[:, :DEV], stacked[:, DEV:]
    last = lax.broadcasted_iota(jnp.int32, (DEV, DEV), 1) == DEV - 1
    left1, right1 = pltpu.roll(left, DEV - 1, 1), pltpu.roll(right, DEV - 1, 1)
    beyond = jnp.concatenate([left1[8:], jnp.zeros((8, DEV), F32)], axis=0)
    behind = (jnp.where(last, right1, left1), jnp.where(last, beyond, right1))
    same = first == (lane < 64)
    for delta in range(BLK):
        for t in range(2):
            tile = (left, right)[t][8 * delta : 8 * delta + 8]
            pair = jnp.where(same, tile, pltpu.roll(pltpu.roll(tile, 4, 0), 64, 1))
            at = 4 * (64 + 4 * delta + 2 * t)
            out_ref[at : at + 8, :] = pair.astype(BF)
            tile = behind[t][8 * delta : 8 * delta + 8]
            pair = jnp.where(same, pltpu.roll(tile, 64, 1), pltpu.roll(tile, 4, 0))
            at = 4 * (4 * (BLK - 1 - delta) + 2 - 2 * t)
            out_ref[at : at + 8, :] = pair.astype(BF)


def total_kernel(in_ref, scale_ref, out_ref):
    total = jnp.sum(in_ref[...].astype(F32).reshape(DEV // 2, 8, DEV), axis=0)
    total = total + pltpu.roll(total, 4, 0)
    low = lax.broadcasted_iota(jnp.int32, (8, DEV), 0) < 4
    lags = jnp.where(low, total, pltpu.roll(total, 64, 1))
    lane = lax.broadcasted_iota(jnp.int32, (8, DEV), 1)
    flipped = jnp.concatenate([lags[7 - j : 8 - j] for j in range(LAGS)], axis=0)
    flipped = jnp.take_along_axis(flipped, (63 - lane) & 127, axis=1)
    ahead, mirrored = scale_ref[0:1, :], scale_ref[1:2, :]
    out_ref[...] = jnp.where(
        mirrored > 0.0, flipped[:, :64] * mirrored, lags[:, :64] * ahead
    )


def pair_counts(mask, columns):
    blocks = mask.shape[0]
    width = C // blocks
    labels = lax.iota(jnp.int32, blocks)
    apart = labels[None, :] - labels[:, None]
    deltas = lax.iota(jnp.int32, 2 * blocks - 1) - (blocks - 1)
    per_delta = jnp.sum(
        mask[None] * (apart[None] == deltas[:, None, None]).astype(jnp.int32), axis=(1, 2)
    )
    offsets = columns - C
    intersection = jnp.maximum(0, width - jnp.abs(offsets[:, None] - width * deltas[None, :]))
    return jnp.sum(intersection * per_delta[None, :], axis=1)


def stack_scale(counts):
    return 1.0 / jnp.sqrt(NB * jnp.maximum(counts, 1).astype(jnp.float32))


VM = pl.BlockSpec(memory_space=pltpu.VMEM)
SM = pl.BlockSpec(memory_space=pltpu.SMEM)
LIMIT = pltpu.CompilerParams(vmem_limit_bytes=24 * 1024 * 1024)


def exchange(x, rows):
    x = x.reshape(DEV, rows, DEV)
    return lax.all_to_all(x, ("blk", "lag"), split_axis=0, concat_axis=0, tiled=True)


def on_device(raw, mask):
    device = lax.axis_index("blk") * lax.axis_size("lag") + lax.axis_index("lag")
    packed = pl.pallas_call(
        pack_kernel,
        out_shape=jax.ShapeDtypeStruct((DEV, BLK, DEV), BF),
        in_specs=[pl.BlockSpec(memory_space=pltpu.HBM)],
        out_specs=pl.BlockSpec(memory_space=pltpu.HBM),
        scratch_shapes=[
            pltpu.VMEM((ROWS, C), F32),
            pltpu.VMEM((BLK * DEV, DEV), F32),
            pltpu.VMEM((2, DEV, 8, DEV), BF),
            pltpu.SemaphoreType.DMA((2,)),
            pltpu.SemaphoreType.DMA((2,)),
        ],
    )(raw)
    series = exchange(packed, BLK).reshape(BLK * DEV, DEV)
    stage1, twiddle, stage2 = time_tables()
    white, live = pl.pallas_call(
        spectra_kernel,
        out_shape=(
            jax.ShapeDtypeStruct((8 * DEV, DEV), BF),
            jax.ShapeDtypeStruct((BLK * BLK, DEV), F32),
        ),
        in_specs=[VM] * 7,
        out_specs=(VM, VM),
        compiler_params=LIMIT,
        scratch_shapes=[
            pltpu.VMEM((BLK * DEV, DEV), F32),
            pltpu.VMEM((4 * DEV, 8 * DEV), BF),
            pltpu.VMEM((8 * DEV, DEV), F32),
        ],
    )(series, stage1, twiddle, stage2, window_table(), taper_table(), mask)
    banded = exchange(white, 8).reshape(8 * DEV, DEV)
    odd = 2 * lax.iota(jnp.int32, LAGS) - (LAGS - 1)
    angle = jnp.mod(odd * first_bin(device), Q).astype(F32) * (2 * math.pi / Q)
    spread = lambda x: jnp.broadcast_to(x.reshape(4, 2, 1, 1), (4, 2, 4, DEV)).reshape(4, 8, DEV)
    rotation = jnp.stack([spread(jnp.cos(angle)), spread(jnp.sin(angle))])
    parts = pl.pallas_call(
        stack_kernel,
        out_shape=jax.ShapeDtypeStruct((4 * DEV, DEV), BF),
        in_specs=[VM] * 7,
        out_specs=VM,
        compiler_params=LIMIT,
        scratch_shapes=[
            pltpu.VMEM((8 * DEV, DEV), F32),
            pltpu.VMEM((2048, DEV), F32),
            pltpu.VMEM((2 * FAR, 8, DEV), F32),
            pltpu.VMEM((8 * DEV, DEV), F32),
        ],
    )(banded, live, rotation, *channel_table(), *offset_table())
    shares = exchange(parts, 4).reshape(4 * DEV, DEV)
    columns = device * 64 + lax.iota(jnp.int32, 64)
    scale = stack_scale(pair_counts(mask, columns))
    scales = jnp.stack([scale, jnp.where(device < 64, scale, 0.0)])
    return pl.pallas_call(
        total_kernel,
        out_shape=jax.ShapeDtypeStruct((LAGS, 64), F32),
        in_specs=[VM, VM],
        out_specs=VM,
        compiler_params=LIMIT,
    )(shares, scales)


def solution(mesh):
    return jax.shard_map(
        on_device,
        mesh=mesh,
        in_specs=(P(("blk", "lag"), None), P()),
        out_specs=P(None, ("blk", "lag")),
        check_vma=False,
    )
```
